32 devices in a mesh: shard: 4 (over y, x), rep: 8 (over z, core).
Axes of the slice: x: 2, y: 2, z: 4, core: 2. Of those that a mesh axis runs over, the one named last changes fastest.
Arguments:
- tokens: bfloat16 [32768, 1024], P(('shard', 'rep')), may hold values from -6 to 6
- cotangent: bfloat16 [32768, 1024], P(('shard', 'rep')), may hold values from -6 to 6
- segment: int32 [32768], P(('shard', 'rep')), may hold values from -1 to 15, as said below
- attn_gain: bfloat16 [1024], P('shard'), may hold values from 0.5 to 1.5
- w_query: bfloat16 [1024, 1024], P('shard'), may hold values from -0.1875 to 0.1875
- w_key: bfloat16 [1024, 512], P('shard'), may hold values from -0.1875 to 0.1875
- w_value: bfloat16 [1024, 512], P('shard'), may hold values from -0.1875 to 0.1875
- qk_gain: bfloat16 [128], P('shard'), may hold values from 0.099609375 to 1.8984375
- w_out: bfloat16 [1024, 1024], P('shard'), may hold values from -1.5 to 1.5
- ffn_gain: bfloat16 [1024], P('shard'), may hold values from 0.5 to 1.5
- w_gate: bfloat16 [1024, 4608], P('shard'), may hold values from -0.1875 to 0.1875
- w_up: bfloat16 [1024, 4608], P('shard'), may hold values from -0.1875 to 0.1875
- w_down: bfloat16 [4608, 1024], P('shard'), may hold values from -0.09375 to 0.09375
Outputs:
- out: bfloat16 [32768, 1024], P(('shard', 'rep'))
- grad_tokens: bfloat16 [32768, 1024], P(('shard', 'rep'))
- grad_attn_gain: float32 [1024], P('shard')
- grad_w_query: float32 [1024, 1024], P('shard')
- grad_w_key: float32 [1024, 512], P('shard')
- grad_w_value: float32 [1024, 512], P('shard')
- grad_qk_gain: float32 [128], P('shard')
- grad_w_out: float32 [1024, 1024], P('shard')
- grad_ffn_gain: float32 [1024], P('shard')
- grad_w_gate: float32 [1024, 4608], P('shard')
- grad_w_up: float32 [1024, 4608], P('shard')
- grad_w_down: float32 [4608, 1024], P('shard')
The draws below stay inside these ranges and needn't reach their ends.
Inputs may be any that keep to these rules, and one draw needn't show every extreme that they name: `segment`: within each device's 1024 slots the live tokens come first, 512 to 1024 of them, followed by padding marked -1; live tokens form runs of equal ids 0, 1, 2, ... in rising order, each run one sequence of 1 to 512 tokens, at most 16 of them on a device. Some device has no padding and holds 16 sequences, some has 512 live tokens, and some sequence has exactly 512 tokens.
All inputs are finite; a program needn't handle non-finite values.
Results may differ from the reference program's by a relative error of at most 0.02.
Values may be sent and summed in bfloat16 or wider, within the bound.
No kernel may reach another device: no remote copies, remote signals or barrier semaphores. Data moves between devices by JAX's collectives and lax.ppermute only.
A program may use at most 384 MiB of HBM per device.

```python
import math
import jax
import jax.numpy as jnp
from jax import lax

D = 1024
HQ = 16
HK = 8
HD = 64
FF = 4608
TOK_DEV = 1024
LMAX = 512
MAXSEQ = 16
TOKENS = 32768


def draw_segment(key, part):
    block_count = TOKENS // TOK_DEV
    first_key, second_key = jax.random.split(jax.random.fold_in(key, 11))
    lengths = jax.random.randint(first_key, (block_count, MAXSEQ), LMAX // 8, LMAX + 1)
    lengths = lengths.at[0].set(LMAX // 8)
    lengths = lengths.at[2, 0].set(LMAX)
    live_count = jax.random.randint(second_key, (block_count,), TOK_DEV // 2, TOK_DEV + 1)
    live_count = live_count.at[0].set(TOK_DEV).at[1].set(TOK_DEV // 2).at[2].set(TOK_DEV)
    ends = jnp.cumsum(lengths, axis=1)
    slot_index = jnp.arange(TOK_DEV)
    which_seq = jnp.sum((ends[:, None, :] <= slot_index[None, :, None]).astype(jnp.int32), axis=2)
    which_seq = jnp.minimum(which_seq, MAXSEQ - 1)
    seg_ids = jnp.where(slot_index[None, :] < live_count[:, None], which_seq, -1)
    return seg_ids.reshape(TOKENS).astype(jnp.int32)


def level_of(own_key, extent, shards, low, high):
    def one(position, blocks):
        draws = jax.random.uniform(jax.random.fold_in(jax.random.fold_in(own_key, 6), position), (blocks,), jnp.float32, low / len(shards), high / len(shards))
        return jnp.repeat(jnp.exp(draws), extent[position] // blocks).reshape((-1,) + (1,) * (len(extent) - position - 1))

    gain = one(*shards[0])
    for cut in shards[1:]:
        gain = gain * one(*cut)
    return gain


def centred(own_key, dims, spread, bound, shards=(), kind=jnp.bfloat16):
    array = jax.random.normal(own_key, dims, jnp.float32) * spread
    if len(shards) > 0:
        array = level_of(own_key, dims, shards, -0.22, 0.18) * array
    return jnp.clip(array, min=-bound, max=bound).astype(kind)


def setup_inputs(seed: int = 0) -> dict:
    key_of = jax.random.split(jax.random.key(seed), 14)
    return {
        "tokens": centred(key_of[0], (TOKENS, D), 1.0, 6.0, ((0, 32),)),
        "cotangent": centred(key_of[1], (TOKENS, D), 1.0, 6.0, ((0, 32),)),
        "segment": draw_segment(jax.random.fold_in(key_of[13], 71), 0),
        "attn_gain": jnp.clip(1.0 + 0.1 * jax.random.normal(key_of[3], (D,), jnp.float32), 0.5, 1.5).astype(jnp.bfloat16),
        "w_query": centred(key_of[4], (D, HQ * HD), D ** -0.5, 0.1875, ((0, 4),)),
        "w_key": centred(key_of[5], (D, HK * HD), D ** -0.5, 0.1875, ((0, 4),)),
        "w_value": centred(key_of[6], (D, HK * HD), D ** -0.5, 0.1875, ((0, 4),)),
        "qk_gain": jnp.clip(1.0 + 0.18 * jax.random.normal(key_of[7], (2 * HD,), jnp.float32), 0.099609375, 1.8984375).astype(jnp.bfloat16),
        "w_out": centred(key_of[8], (HQ * HD, D), (max(HQ * HD // 64, 4)) ** -0.5, 1.5, ((0, 4),)),
        "ffn_gain": jnp.clip(1.0 + 0.1 * jax.random.normal(key_of[9], (D,), jnp.float32), 0.5, 1.5).astype(jnp.bfloat16),
        "w_gate": centred(key_of[10], (D, FF), D ** -0.5, 0.1875, ((0, 4),)),
        "w_up": centred(key_of[11], (D, FF), D ** -0.5, 0.1875, ((0, 4),)),
        "w_down": centred(key_of[12], (FF, D), FF ** -0.5, 0.09375, ((0, 4),)),
    }


norm_eps = 1e-05
rope_base = 1000000.0

@jax.custom_vjp
def low(v):
    return lax.optimization_barrier(v.astype(jnp.bfloat16)).astype(jnp.float32)

@jax.custom_vjp
def low_back(v):
    return v

def low_keep(v):
    return (low(v), None)

def low_pass(kept, grad):
    return (grad,)

def back_keep(v):
    return (v, None)

def back_low(kept, grad):
    return (low(grad),)
low.defvjp(low_keep, low_pass)
low_back.defvjp(back_keep, back_low)

def inv_rms(values):
    return lax.rsqrt(lax.optimization_barrier(jnp.mean(values * values, axis=-1, keepdims=True)) + norm_eps)

def rope_tables(positions):
    half_dim = HD // 2
    freq_index = jnp.arange(half_dim).astype(positions.dtype)
    freq_vals = jnp.power(rope_base, -(2.0 * freq_index) / HD).astype(positions.dtype)
    angles = positions[:, None] * freq_vals[None, :]
    return (jnp.cos(angles)[:, None, :], jnp.sin(angles)[:, None, :])

def rotate(values, cosine, sine_table):
    half_dim = HD // 2
    first_half = values[..., :half_dim]
    second_half = values[..., half_dim:]
    return jnp.concatenate([first_half * cosine - second_half * sine_table, second_half * cosine + first_half * sine_table], axis=-1)

def block_forward(params, inputs, segment_ids):
    attn_gain, w_query, w_key, w_value, qk_gain, w_out, ffn_gain, w_gate, w_up, w_down = params
    highest = lax.Precision.HIGHEST
    row_count = inputs.shape[0]
    float_type = inputs.dtype
    group_size = HQ // HK
    score_scale = 1.0 / math.sqrt(HD)
    token_index = jnp.arange(row_count)
    same_seq = segment_ids[:, None] == segment_ids[None, :]
    allowed = same_seq & (token_index[None, :] <= token_index[:, None])
    positions = lax.optimization_barrier(jnp.sum((same_seq & (token_index[None, :] < token_index[:, None])).astype(float_type), axis=1))
    live_rows = (segment_ids >= 0).astype(float_type)[:, None]
    cosine, sine_table = rope_tables(positions)
    normed = low(inputs * inv_rms(inputs) * attn_gain)
    query_lin = low_back(jnp.dot(normed, w_query, precision=highest)).reshape(row_count, HQ, HD)
    key_lin = low_back(jnp.dot(normed, w_key, precision=highest)).reshape(row_count, HK, HD)
    value_low = low(low_back(jnp.dot(normed, w_value, precision=highest))).reshape(row_count, HK, HD)
    query_rot = low(rotate(query_lin * inv_rms(query_lin) * qk_gain[:HD], cosine, sine_table))
    key_rot = low(rotate(key_lin * inv_rms(key_lin) * qk_gain[HD:], cosine, sine_table))
    key_full = jnp.repeat(key_rot, group_size, axis=1)
    value_full = jnp.repeat(value_low, group_size, axis=1)
    raw_scores = low_back(score_scale * jnp.einsum('qhd,khd->hqk', query_rot, key_full, precision=highest))
    masked = jnp.where(allowed[None, :, :], raw_scores, -1e+30)
    attn_probs = jax.nn.softmax(masked, axis=-1)
    attended = jnp.einsum('hqk,khd->qhd', low(attn_probs), value_full, precision=highest)
    attn_flat = low(low_back(attended)).reshape(row_count, HQ * HD)
    hidden = inputs + low_back(jnp.dot(attn_flat, w_out, precision=highest))
    normed_ffn = low(hidden * inv_rms(hidden) * ffn_gain)
    gate_proj = low_back(jnp.dot(normed_ffn, w_gate, precision=highest))
    up_proj = low_back(jnp.dot(normed_ffn, w_up, precision=highest))
    mixed_act = low(jax.nn.silu(gate_proj) * up_proj)
    return live_rows * (hidden + low_back(jnp.dot(mixed_act, w_down, precision=highest)))

def reference(tokens, cotangent, segment, attn_gain, w_query, w_key, w_value, qk_gain, w_out, ffn_gain, w_gate, w_up, w_down):
    params = tuple((weight.astype(jnp.float32) for weight in (attn_gain, w_query, w_key, w_value, qk_gain, w_out, ffn_gain, w_gate, w_up, w_down)))
    inputs_all = tokens.astype(jnp.float32).reshape(-1, TOK_DEV, D)
    cot_all = cotangent.astype(jnp.float32).reshape(-1, TOK_DEV, D)
    seg_all = segment.reshape(-1, TOK_DEV)

    def scan_step(totals, block_item):
        block_in, block_cot, block_seg = block_item
        result, pullback = jax.vjp(lambda weights, inputs: block_forward(weights, inputs, block_seg), params, block_in)
        grad_params, grad_in = pullback(block_cot)
        totals = jax.tree.map(lambda running, addend: running + addend, totals, grad_params)
        return (totals, (result.astype(jnp.bfloat16), grad_in.astype(jnp.bfloat16)))
    zero_grads = jax.tree.map(jnp.zeros_like, params)
    totals, (outputs, grads_in) = lax.scan(scan_step, zero_grads, (inputs_all, cot_all, seg_all))
    return (outputs.reshape(-1, D), grads_in.reshape(-1, D), totals[0], totals[1], totals[2], totals[3], totals[4], totals[5], totals[6], totals[7], totals[8], totals[9])
```

```python
import functools
import math

import jax
import jax.numpy as jnp
from jax import lax
from jax.sharding import PartitionSpec as P

HQ = 16
HK = 8
HD = 64


norm_eps = 1e-05
rope_base = 1000000.0


def inv_rms(values):
    return lax.rsqrt(jnp.mean(values * values, axis=-1, keepdims=True) + norm_eps)


def rope_tables(positions):
    half_dim = HD // 2
    freq_index = jnp.arange(half_dim).astype(jnp.float32)
    freq_vals = jnp.power(rope_base, -(2.0 * freq_index) / HD)
    angles = positions[:, None] * freq_vals[None, :]
    return (jnp.cos(angles)[:, None, :], jnp.sin(angles)[:, None, :])


def rotate(values, cosine, sine_table):
    half_dim = HD // 2
    first_half = values[..., :half_dim]
    second_half = values[..., half_dim:]
    return jnp.concatenate(
        [
            first_half * cosine - second_half * sine_table,
            second_half * cosine + first_half * sine_table,
        ],
        axis=-1,
    )


def rotate_back(grad_vals, cosine, sine_table):
    half_dim = HD // 2
    first_half = grad_vals[..., :half_dim]
    second_half = grad_vals[..., half_dim:]
    return jnp.concatenate(
        [
            first_half * cosine + second_half * sine_table,
            second_half * cosine - first_half * sine_table,
        ],
        axis=-1,
    )


def norm_back(grad_out, inputs, scale_inv, gain_vec):
    weighted = grad_out * gain_vec
    row_inner = jnp.mean(weighted * inputs, axis=-1, keepdims=True)
    return scale_inv * weighted - inputs * (scale_inv * scale_inv * scale_inv) * row_inner


def matmul_plain(left_mat, right_mat):
    return jnp.dot(left_mat, right_mat, preferred_element_type=jnp.float32)


def matmul_rows(left_mat, right_mat):
    return lax.dot_general(
        left_mat, right_mat, (((0,), (0,)), ((), ())), preferred_element_type=jnp.float32
    )


def matmul_cols(left_mat, right_mat):
    return lax.dot_general(
        left_mat, right_mat, (((1,), (1,)), ((), ())), preferred_element_type=jnp.float32
    )


def make_links(mesh):
    shard_size, rep_size = mesh.shape["shard"], mesh.shape["rep"]
    axes = ("shard", "rep")

    def shard_swap(value, bit):
        pairs = [
            (s * rep_size + r, (s ^ bit) * rep_size + r)
            for s in range(shard_size)
            for r in range(rep_size)
        ]
        return lax.ppermute(value, axes, pairs)

    def rep_swap(value, bit):
        pairs = [
            (s * rep_size + r, s * rep_size + (r ^ bit))
            for s in range(shard_size)
            for r in range(rep_size)
        ]
        return lax.ppermute(value, axes, pairs)

    return shard_size, rep_size, shard_swap, rep_swap


def add_low(left, right):
    return (left.astype(jnp.float32) + right.astype(jnp.float32)).astype(jnp.bfloat16)


def gather_rows(links, weight):
    shard_size, rep_size, shard_swap, rep_swap = links
    me = lax.axis_index("shard")
    core = lax.rem(lax.axis_index("rep"), 2)
    half = weight.shape[0] // 2
    quarter = half // 2
    mine = lax.dynamic_slice_in_dim(weight, core * half, half, 0)
    if shard_size == 4:
        from_x = shard_swap(mine, 1)
        from_y = shard_swap(mine, 2)
        corner_a = shard_swap(from_x[:quarter], 2)
        corner_b = shard_swap(from_y[quarter:], 1)
        pieces = {1: from_x, 2: from_y, 3: jnp.concatenate([corner_a, corner_b], axis=0)}
    else:
        pieces = {0: mine}
        bit = 1
        while bit < shard_size:
            order = sorted(pieces)
            got = shard_swap(jnp.stack([pieces[d] for d in order]), bit)
            for at, d in enumerate(order):
                pieces[d ^ bit] = got[at]
            bit *= 2
        del pieces[0]
    others = {d: rep_swap(piece, 1) for d, piece in pieces.items()}
    full = jnp.zeros((shard_size, 2, half, weight.shape[1]), weight.dtype)
    full = lax.dynamic_update_slice(
        full, weight.reshape((1, 2, half, weight.shape[1])), (me, 0, 0, 0)
    )
    for d in pieces:
        full = lax.dynamic_update_slice(full, pieces[d][None, None], (me ^ d, core, 0, 0))
        full = lax.dynamic_update_slice(full, others[d][None, None], (me ^ d, 1 - core, 0, 0))
    return full.reshape(shard_size * weight.shape[0], weight.shape[1])


def scatter_sum(links, own, other):
    shard_size, rep_size, shard_swap, rep_swap = links
    me = lax.axis_index("shard")
    rep = lax.axis_index("rep")
    received = rep_swap(other().astype(jnp.bfloat16), 1)
    part = (own() + received.astype(jnp.float32)).astype(jnp.bfloat16)
    rows = part.shape[1] // 2

    def piece(d, at):
        return lax.dynamic_slice(
            part, (me ^ d, at * rows, 0), (1, rows, part.shape[2])
        )[0]

    if shard_size == 4:
        got_a = shard_swap(jnp.stack([piece(1, 0), piece(3, 0)]), 1)
        got_b = shard_swap(jnp.stack([piece(2, 1), piece(3, 1)]), 2)
        pass_a = shard_swap(add_low(piece(2, 0), got_a[1]), 2)
        pass_b = shard_swap(add_low(piece(1, 1), got_b[1]), 1)
        sum_a = add_low(piece(0, 0).astype(jnp.float32) + got_a[0].astype(jnp.float32), pass_a)
        sum_b = add_low(piece(0, 1).astype(jnp.float32) + got_b[0].astype(jnp.float32), pass_b)
        halves = [sum_a, sum_b]
    else:
        held = {d: jnp.stack([piece(d, 0), piece(d, 1)]) for d in range(shard_size)}
        bit = shard_size // 2
        while bit:
            sent = [d for d in sorted(held) if d & bit]
            got = shard_swap(jnp.stack([held[d] for d in sent]), bit)
            held = {d ^ bit: add_low(held[d ^ bit], got[at]) for at, d in enumerate(sent)}
            bit //= 2
        halves = [held[0][0], held[0][1]]
    upper = lax.rem(rep // 2, 2) == 1
    if rep_size >= 8:
        keep = jnp.where(upper, halves[1], halves[0])
        send = jnp.where(upper, halves[0], halves[1])
        keep = add_low(keep, rep_swap(send, 2))
        bit = 4
        while bit < rep_size:
            keep = add_low(keep, rep_swap(keep, bit))
            bit *= 2
        back = rep_swap(keep, 2)
        halves = [jnp.where(upper, back, keep), jnp.where(upper, keep, back)]
        half = jnp.concatenate(halves, axis=0)
    else:
        half = jnp.concatenate(halves, axis=0)
        bit = 2
        while bit < rep_size:
            half = add_low(half, rep_swap(half, bit))
            bit *= 2
    return half, rep_swap(half, 1)


def join_rows(pair):
    core = lax.rem(lax.axis_index("rep"), 2)
    half, other = pair
    return jnp.where(
        core == 0,
        jnp.concatenate([half, other], axis=0),
        jnp.concatenate([other, half], axis=0),
    ).astype(jnp.float32)


def join_columns(pair):
    core = lax.rem(lax.axis_index("rep"), 2)
    half, other = pair
    return jnp.where(
        core == 0,
        jnp.concatenate([half, other], axis=1),
        jnp.concatenate([other, half], axis=1),
    ).astype(jnp.float32)


def row_halves(links, left_mat, right_mat):
    shard_size = links[0]
    core = lax.rem(lax.axis_index("rep"), 2)
    count, width = left_mat.shape
    cut = left_mat.reshape(count, shard_size, 2, width // shard_size // 2)

    def half(which):
        picked = lax.dynamic_slice_in_dim(cut, which, 1, 2)
        product = matmul_rows(picked.reshape(count, width // 2), right_mat)
        return product.reshape(shard_size, width // shard_size // 2, right_mat.shape[1])

    return (lambda: half(core)), (lambda: half(1 - core))


def column_halves(links, left_mat, right_mat):
    shard_size = links[0]
    core = lax.rem(lax.axis_index("rep"), 2)
    width = right_mat.shape[1] // 2

    def half(which):
        picked = lax.dynamic_slice_in_dim(right_mat, which * width, width, 1)
        return matmul_rows(left_mat, picked).reshape(shard_size, -1, width)

    return (lambda: half(core)), (lambda: half(1 - core))


def body(
    links,
    tokens,
    cotangent,
    segment,
    attn_gain,
    w_query,
    w_key,
    w_value,
    qk_gain,
    w_out,
    ffn_gain,
    w_gate,
    w_up,
    w_down,
):
    row_count = tokens.shape[0]
    group_size = HQ // HK
    score_scale = 1.0 / math.sqrt(HD)
    block_rows = min(512, row_count)
    block_count = row_count // block_rows
    packed = jnp.zeros((attn_gain.shape[0], 128), jnp.bfloat16)
    packed = packed.at[:, 0].set(attn_gain).at[:, 1].set(ffn_gain)
    packed = packed.at[: qk_gain.shape[0], 2].set(qk_gain)
    front = gather_rows(links, jnp.concatenate([w_query, w_key, w_value, packed], axis=1))
    full_out = gather_rows(links, w_out)
    full_gate = gather_rows(links, w_gate)
    full_up = gather_rows(links, w_up)
    full_down = gather_rows(links, w_down)
    full_query = front[:, : HQ * HD]
    full_key = front[:, HQ * HD : (HQ + HK) * HD]
    full_value = front[:, (HQ + HK) * HD : (HQ + 2 * HK) * HD]
    gains = front[:, (HQ + 2 * HK) * HD :]
    full_attn_gain = gains[:, 0]
    full_ffn_gain = gains[:, 1]
    full_qk_gain = gains.reshape(links[0], -1, 128)[:, : qk_gain.shape[0], 2].reshape(-1)
    inputs = tokens.astype(jnp.float32)
    token_index = jnp.arange(row_count)
    same_seq = segment[:, None] == segment[None, :]
    allowed = same_seq & (token_index[None, :] <= token_index[:, None])
    positions = jnp.sum(
        (same_seq & (token_index[None, :] < token_index[:, None])).astype(jnp.float32), axis=1
    )
    live_rows = (segment >= 0).astype(jnp.float32)[:, None]
    cosine, sine_table = rope_tables(positions)
    scale_one = inv_rms(inputs)
    normed = (inputs * scale_one * full_attn_gain.astype(jnp.float32)).astype(jnp.bfloat16)
    query_lin = matmul_plain(normed, full_query).reshape(row_count, HQ, HD)
    key_lin = matmul_plain(normed, full_key).reshape(row_count, HK, HD)
    value_low = matmul_plain(normed, full_value).astype(jnp.bfloat16).reshape(row_count, HK, HD)
    qk_gains = full_qk_gain.astype(jnp.float32)
    query_scale = inv_rms(query_lin)
    key_scale = inv_rms(key_lin)
    query_rot = (
        rotate(query_lin * query_scale * qk_gains[:HD], cosine, sine_table)
        .astype(jnp.bfloat16)
        .reshape(row_count, HK, group_size, HD)
    )
    key_rot = rotate(key_lin * key_scale * qk_gains[HD:], cosine, sine_table).astype(jnp.bfloat16)

    def block_scores(begin_row):
        query_block = query_rot[begin_row : begin_row + block_rows]
        raw_scores = score_scale * jnp.einsum(
            "qgrd,kgd->grqk", query_block, key_rot, preferred_element_type=jnp.float32
        )
        mask_block = allowed[begin_row : begin_row + block_rows]
        return jnp.where(mask_block[None, None, :, :], raw_scores, -1e30)

    lse_parts = []
    attended_parts = []
    for block_id in range(block_count):
        begin_row = block_id * block_rows
        masked = block_scores(begin_row)
        row_peak = jnp.max(masked, axis=-1, keepdims=True)
        exp_scores = jnp.exp(masked - row_peak)
        row_total = jnp.sum(exp_scores, axis=-1, keepdims=True)
        probs_low = (exp_scores / row_total).astype(jnp.bfloat16)
        lse_parts.append(row_peak + jnp.log(row_total))
        attended_parts.append(
            jnp.einsum("grqk,kgd->qgrd", probs_low, value_low, preferred_element_type=jnp.float32)
        )
    attn_low = (
        jnp.concatenate(attended_parts, axis=0).astype(jnp.bfloat16).reshape(row_count, HQ * HD)
    )
    hidden = inputs + matmul_plain(attn_low, full_out)
    scale_two = inv_rms(hidden)
    normed_ffn = (hidden * scale_two * full_ffn_gain.astype(jnp.float32)).astype(jnp.bfloat16)
    gate_proj = matmul_plain(normed_ffn, full_gate)
    up_proj = matmul_plain(normed_ffn, full_up)
    gate_sig = jax.nn.sigmoid(gate_proj)
    gate_act = gate_proj * gate_sig
    mixed_act = (gate_act * up_proj).astype(jnp.bfloat16)
    result = live_rows * (hidden + matmul_plain(mixed_act, full_down))
    out_grad = live_rows * cotangent.astype(jnp.float32)
    out_low = out_grad.astype(jnp.bfloat16)
    grad_mixed = matmul_cols(out_low, full_down)
    down_pair = scatter_sum(links, *column_halves(links, mixed_act, out_low))
    grad_up_low = (grad_mixed * gate_act).astype(jnp.bfloat16)
    grad_gate_low = (grad_mixed * up_proj * gate_sig * (1.0 + gate_proj * (1.0 - gate_sig))).astype(
        jnp.bfloat16
    )
    gate_pair = scatter_sum(links, *row_halves(links, normed_ffn, grad_gate_low))
    up_pair = scatter_sum(links, *row_halves(links, normed_ffn, grad_up_low))
    grad_normed_ffn = matmul_cols(grad_gate_low, full_gate) + matmul_cols(grad_up_low, full_up)
    grad_ffn_gain = jnp.sum(grad_normed_ffn * hidden * scale_two, axis=0)
    grad_hidden = out_grad + norm_back(
        grad_normed_ffn, hidden, scale_two, full_ffn_gain.astype(jnp.float32)
    )
    hidden_low = grad_hidden.astype(jnp.bfloat16)
    grad_attn_low = (
        matmul_cols(hidden_low, full_out)
        .astype(jnp.bfloat16)
        .reshape(row_count, HK, group_size, HD)
    )
    out_pair = scatter_sum(links, *row_halves(links, attn_low, hidden_low))
    grad_query_parts = []
    grad_key_rot = jnp.zeros((row_count, HK, HD), jnp.float32)
    grad_value = jnp.zeros((row_count, HK, HD), jnp.float32)
    for block_id in range(block_count):
        begin_row = block_id * block_rows
        masked = block_scores(begin_row)
        attn_probs = jnp.exp(masked - lse_parts[block_id])
        probs_low = attn_probs.astype(jnp.bfloat16)
        grad_block = grad_attn_low[begin_row : begin_row + block_rows]
        query_block = query_rot[begin_row : begin_row + block_rows]
        grad_probs = jnp.einsum(
            "qgrd,kgd->grqk", grad_block, value_low, preferred_element_type=jnp.float32
        )
        row_inner = jnp.sum(attn_probs * grad_probs, axis=-1, keepdims=True)
        grad_scores = (attn_probs * (grad_probs - row_inner)).astype(jnp.bfloat16)
        grad_query_parts.append(
            score_scale
            * jnp.einsum("grqk,kgd->qgrd", grad_scores, key_rot, preferred_element_type=jnp.float32)
        )
        grad_key_rot = grad_key_rot + score_scale * jnp.einsum(
            "grqk,qgrd->kgd", grad_scores, query_block, preferred_element_type=jnp.float32
        )
        grad_value = grad_value + jnp.einsum(
            "grqk,qgrd->kgd", probs_low, grad_block, preferred_element_type=jnp.float32
        )
    grad_query_rot = jnp.concatenate(grad_query_parts, axis=0).reshape(row_count, HQ, HD)
    grad_query_norm = rotate_back(grad_query_rot, cosine, sine_table)
    grad_key_norm = rotate_back(grad_key_rot, cosine, sine_table)
    back_gains = full_qk_gain.astype(jnp.float32)
    grad_qk_gain = jnp.concatenate(
        [
            jnp.sum(grad_query_norm * query_lin * query_scale, axis=(0, 1)),
            jnp.sum(grad_key_norm * key_lin * key_scale, axis=(0, 1)),
        ]
    )
    grad_query_low = (
        norm_back(grad_query_norm, query_lin, query_scale, back_gains[:HD])
        .astype(jnp.bfloat16)
        .reshape(row_count, HQ * HD)
    )
    grad_key_low = (
        norm_back(grad_key_norm, key_lin, key_scale, back_gains[HD:])
        .astype(jnp.bfloat16)
        .reshape(row_count, HK * HD)
    )
    grad_value_low = grad_value.astype(jnp.bfloat16).reshape(row_count, HK * HD)
    grad_normed = (
        matmul_cols(grad_query_low, full_query)
        + matmul_cols(grad_key_low, full_key)
        + matmul_cols(grad_value_low, full_value)
    )
    grad_attn_gain = jnp.sum(grad_normed * inputs * scale_one, axis=0)
    grad_inputs = grad_hidden + norm_back(
        grad_normed, inputs, scale_one, full_attn_gain.astype(jnp.float32)
    )
    small = jnp.zeros((links[0], attn_gain.shape[0], 128), jnp.float32)
    small = small.at[:, :, 0].set(grad_attn_gain.reshape(links[0], -1))
    small = small.at[:, :, 1].set(grad_ffn_gain.reshape(links[0], -1))
    small = small.at[:, : qk_gain.shape[0], 2].set(grad_qk_gain.reshape(links[0], -1))
    small = small.reshape(links[0], 2, -1, 128)
    core = lax.rem(lax.axis_index("rep"), 2)
    own_front, other_front = row_halves(
        links, normed, jnp.concatenate([grad_query_low, grad_key_low, grad_value_low], axis=1)
    )

    def with_small(product, which):
        extra = lax.dynamic_slice_in_dim(small, which, 1, 1)[:, 0]
        return jnp.concatenate([product(), extra], axis=2)

    front_share = join_rows(
        scatter_sum(
            links,
            lambda: with_small(own_front, core),
            lambda: with_small(other_front, 1 - core),
        )
    )
    share_query = front_share[:, : HQ * HD]
    share_key = front_share[:, HQ * HD : (HQ + HK) * HD]
    share_value = front_share[:, (HQ + HK) * HD : (HQ + 2 * HK) * HD]
    extras = front_share[:, (HQ + 2 * HK) * HD :]
    share_again = extras[:, 0]
    share_fgain = extras[:, 1]
    share_qk = extras[: qk_gain.shape[0], 2]
    share_out = join_rows(out_pair)
    share_gate = join_rows(gate_pair)
    share_up = join_rows(up_pair)
    share_down = join_columns(down_pair)
    return (
        result.astype(jnp.bfloat16),
        grad_inputs.astype(jnp.bfloat16),
        share_again,
        share_query,
        share_key,
        share_value,
        share_qk,
        share_out,
        share_fgain,
        share_gate,
        share_up,
        share_down,
    )


def solution(mesh):
    return jax.shard_map(
        functools.partial(body, make_links(mesh)),
        mesh=mesh,
        in_specs=(
            P(("shard", "rep"), None),
            P(("shard", "rep"), None),
            P(("shard", "rep")),
            P("shard"),
            P("shard", None),
            P("shard", None),
            P("shard", None),
            P("shard"),
            P("shard", None),
            P("shard"),
            P("shard", None),
            P("shard", None),
            P("shard", None),
        ),
        out_specs=(
            P(("shard", "rep"), None),
            P(("shard", "rep"), None),
            P("shard"),
            P("shard", None),
            P("shard", None),
            P("shard", None),
            P("shard"),
            P("shard", None),
            P("shard"),
            P("shard", None),
            P("shard", None),
            P("shard", None),
        ),
        check_vma=False,
    )
```

```python
import functools
import math

import jax
import jax.numpy as jnp
from jax import lax
from jax.experimental import pallas as pl
from jax.experimental.pallas import tpu as pltpu
from jax.sharding import PartitionSpec as P

HQ = 16
HK = 8
HD = 64


norm_eps = 1e-05
rope_base = 1000000.0


def inv_rms(values):
    return lax.rsqrt(jnp.mean(values * values, axis=-1, keepdims=True) + norm_eps)


def rope_tables(positions):
    half_dim = HD // 2
    freq_index = jnp.arange(half_dim).astype(jnp.float32)
    freq_vals = jnp.power(rope_base, -(2.0 * freq_index) / HD)
    angles = positions[:, None] * freq_vals[None, :]
    return (jnp.cos(angles)[:, None, :], jnp.sin(angles)[:, None, :])


def rotate(values, cosine, sine_table):
    half_dim = HD // 2
    first_half = values[..., :half_dim]
    second_half = values[..., half_dim:]
    return jnp.concatenate(
        [
            first_half * cosine - second_half * sine_table,
            second_half * cosine + first_half * sine_table,
        ],
        axis=-1,
    )


def rotate_back(grad_vals, cosine, sine_table):
    half_dim = HD // 2
    first_half = grad_vals[..., :half_dim]
    second_half = grad_vals[..., half_dim:]
    return jnp.concatenate(
        [
            first_half * cosine + second_half * sine_table,
            second_half * cosine - first_half * sine_table,
        ],
        axis=-1,
    )


def norm_back(grad_out, inputs, scale_inv, gain_vec):
    weighted = grad_out * gain_vec
    row_inner = jnp.mean(weighted * inputs, axis=-1, keepdims=True)
    return scale_inv * weighted - inputs * (scale_inv * scale_inv * scale_inv) * row_inner


def matmul_plain(left_mat, right_mat):
    return jnp.dot(left_mat, right_mat, preferred_element_type=jnp.float32)


def matmul_rows(left_mat, right_mat):
    return lax.dot_general(
        left_mat, right_mat, (((0,), (0,)), ((), ())), preferred_element_type=jnp.float32
    )


def matmul_cols(left_mat, right_mat):
    return lax.dot_general(
        left_mat, right_mat, (((1,), (1,)), ((), ())), preferred_element_type=jnp.float32
    )


def make_links(mesh):
    shard_size, rep_size = mesh.shape["shard"], mesh.shape["rep"]
    axes = ("shard", "rep")

    def shard_swap(value, bit):
        pairs = [
            (s * rep_size + r, (s ^ bit) * rep_size + r)
            for s in range(shard_size)
            for r in range(rep_size)
        ]
        return lax.ppermute(value, axes, pairs)

    def rep_swap(value, bit):
        pairs = [
            (s * rep_size + r, s * rep_size + (r ^ bit))
            for s in range(shard_size)
            for r in range(rep_size)
        ]
        return lax.ppermute(value, axes, pairs)

    return shard_size, rep_size, shard_swap, rep_swap


def add_low(left, right):
    return (left.astype(jnp.float32) + right.astype(jnp.float32)).astype(jnp.bfloat16)


def pin(values, *waits):
    return lax.optimization_barrier((values, waits))[0]


class Flow:
    def __init__(self, steps):
        self.steps = steps
        self.pending = ()
        self.result = None
        self.advance()

    def advance(self):
        try:
            self.pending = next(self.steps)
        except StopIteration as stop:
            self.pending = ()
            if stop.value is not None:
                self.result = stop.value

    def finish(self):
        while self.result is None:
            self.advance()
        return self.result


def gather_steps(links, mine, whole):
    shard_size, rep_size, shard_swap, rep_swap = links
    me = lax.axis_index("shard")
    core = lax.rem(lax.axis_index("rep"), 2)
    half, width = mine.shape
    quarter = half // 2
    pieces, others = {}, {}
    if shard_size == 4:
        pieces[1] = shard_swap(mine, 1)
        pieces[2] = shard_swap(mine, 2)
        yield (pieces[1], pieces[2])
        corner_a = shard_swap(pieces[1][:quarter], 2)
        corner_b = shard_swap(pieces[2][quarter:], 1)
        others[1] = rep_swap(pieces[1], 1)
        others[2] = rep_swap(pieces[2], 1)
        yield (corner_a, corner_b, others[1], others[2])
        pieces[3] = jnp.concatenate([corner_a, corner_b], axis=0)
        others[3] = rep_swap(pieces[3], 1)
        yield (others[3],)
    else:
        pieces[0] = mine
        bit = 1
        while bit < shard_size:
            order = sorted(pieces)
            got = shard_swap(jnp.stack([pieces[d] for d in order]), bit)
            yield (got,)
            for at, d in enumerate(order):
                pieces[d ^ bit] = got[at]
            bit *= 2
        del pieces[0]
        others = {d: rep_swap(piece, 1) for d, piece in pieces.items()}
    full = jnp.zeros((shard_size, 2, half, width), mine.dtype)
    full = lax.dynamic_update_slice(full, whole.reshape((1, 2, half, width)), (me, 0, 0, 0))
    for d in pieces:
        full = lax.dynamic_update_slice(full, pieces[d][None, None], (me ^ d, core, 0, 0))
        full = lax.dynamic_update_slice(full, others[d][None, None], (me ^ d, 1 - core, 0, 0))
    return full.reshape(shard_size * 2 * half, width)


def core_half(weight):
    core = lax.rem(lax.axis_index("rep"), 2)
    half = weight.shape[0] // 2
    return lax.dynamic_slice_in_dim(weight, core * half, half, 0)


def core_sum(links, own, other):
    received = links[3](other().astype(jnp.bfloat16), 1)
    return (own() + received.astype(jnp.float32)).astype(jnp.bfloat16)


def scatter_steps(links, part):
    shard_size, rep_size, shard_swap, rep_swap = links
    me = lax.axis_index("shard")
    rep = lax.axis_index("rep")
    rows = part.shape[1] // 2

    def piece(d, at):
        return lax.dynamic_slice(
            part, (me ^ d, at * rows, 0), (1, rows, part.shape[2])
        )[0]

    if shard_size == 4:
        got_a = shard_swap(jnp.stack([piece(1, 0), piece(3, 0)]), 1)
        got_b = shard_swap(jnp.stack([piece(2, 1), piece(3, 1)]), 2)
        yield (got_a, got_b)
        pass_a = shard_swap(add_low(piece(2, 0), got_a[1]), 2)
        pass_b = shard_swap(add_low(piece(1, 1), got_b[1]), 1)
        yield (pass_a, pass_b)
        sum_a = add_low(piece(0, 0).astype(jnp.float32) + got_a[0].astype(jnp.float32), pass_a)
        sum_b = add_low(piece(0, 1).astype(jnp.float32) + got_b[0].astype(jnp.float32), pass_b)
        halves = [sum_a, sum_b]
    else:
        held = {d: jnp.stack([piece(d, 0), piece(d, 1)]) for d in range(shard_size)}
        bit = shard_size // 2
        while bit:
            sent = [d for d in sorted(held) if d & bit]
            got = shard_swap(jnp.stack([held[d] for d in sent]), bit)
            yield (got,)
            held = {d ^ bit: add_low(held[d ^ bit], got[at]) for at, d in enumerate(sent)}
            bit //= 2
        halves = [held[0][0], held[0][1]]
    upper = lax.rem(rep // 2, 2) == 1
    if rep_size >= 8:
        keep = jnp.where(upper, halves[1], halves[0])
        send = jnp.where(upper, halves[0], halves[1])
        got = rep_swap(send, 2)
        yield (got,)
        keep = add_low(keep, got)
        bit = 4
        while bit < rep_size:
            got = rep_swap(keep, bit)
            yield (got,)
            keep = add_low(keep, got)
            bit *= 2
        back = rep_swap(keep, 2)
        yield (back,)
        halves = [jnp.where(upper, back, keep), jnp.where(upper, keep, back)]
        half = jnp.concatenate(halves, axis=0)
    else:
        half = jnp.concatenate(halves, axis=0)
        bit = 2
        while bit < rep_size:
            half = add_low(half, rep_swap(half, bit))
            bit *= 2
    return half, rep_swap(half, 1)


def join_rows(pair):
    core = lax.rem(lax.axis_index("rep"), 2)
    half, other = pair
    return jnp.where(
        core == 0,
        jnp.concatenate([half, other], axis=0),
        jnp.concatenate([other, half], axis=0),
    ).astype(jnp.float32)


def join_columns(pair):
    core = lax.rem(lax.axis_index("rep"), 2)
    half, other = pair
    return jnp.where(
        core == 0,
        jnp.concatenate([half, other], axis=1),
        jnp.concatenate([other, half], axis=1),
    ).astype(jnp.float32)


def row_halves(links, left_mat, right_mat):
    shard_size = links[0]
    core = lax.rem(lax.axis_index("rep"), 2)
    count, width = left_mat.shape
    cut = left_mat.reshape(count, shard_size, 2, width // shard_size // 2)

    def half(which):
        picked = lax.dynamic_slice_in_dim(cut, which, 1, 2)
        product = matmul_rows(picked.reshape(count, width // 2), right_mat)
        return product.reshape(shard_size, width // shard_size // 2, right_mat.shape[1])

    return (lambda: half(core)), (lambda: half(1 - core))


def column_halves(links, left_mat, right_mat):
    shard_size = links[0]
    core = lax.rem(lax.axis_index("rep"), 2)
    width = right_mat.shape[1] // 2

    def half(which):
        picked = lax.dynamic_slice_in_dim(right_mat, which * width, width, 1)
        return matmul_rows(left_mat, picked).reshape(shard_size, -1, width)

    return (lambda: half(core)), (lambda: half(1 - core))


BLOCK = 256
LOOK = 3


def nt_dot(left_mat, right_mat):
    return lax.dot_general(
        left_mat, right_mat, (((1,), (1,)), ((), ())), preferred_element_type=jnp.float32
    )


def attend_kernel(live_ref, q_ref, k_ref, v_ref, seg_col_ref, seg_row_ref, o_ref, acc_ref):
    at = pl.program_id(1)
    acc_ref[...] = jnp.zeros_like(acc_ref)
    lane = lax.broadcasted_iota(jnp.int32, (BLOCK, 2 * HD), 1)
    low_lane = lane < HD
    for back in range(LOOK):
        key_block = jnp.maximum(at - back, 0)

        @pl.when((at >= back) & (live_ref[at, key_block] > 0))
        def _():
            begin = pl.multiple_of(key_block * BLOCK, BLOCK)
            same = seg_col_ref[...] == seg_row_ref[:, pl.ds(begin, BLOCK)]
            if back == 0:
                row = lax.broadcasted_iota(jnp.int32, (BLOCK, BLOCK), 0)
                col = lax.broadcasted_iota(jnp.int32, (BLOCK, BLOCK), 1)
                same = same & (col <= row)
            mask = same.astype(jnp.float32)
            keys = k_ref[pl.ds(begin, BLOCK), :]
            values = v_ref[pl.ds(begin, BLOCK), :]
            swapped = pltpu.roll(values.astype(jnp.float32), HD, 1).astype(jnp.bfloat16)
            one = jnp.ones_like(values)
            for head in range(4):
                group, odd = head // 2, head % 2
                scores = nt_dot(
                    q_ref[:, head * HD : (head + 1) * HD], keys[:, group * HD : (group + 1) * HD]
                )
                weights = (jnp.exp(scores) * mask).astype(jnp.bfloat16)
                held = values if group == odd else swapped
                padded = jnp.where(low_lane, held, one) if odd == 0 else jnp.where(low_lane, one, held)
                acc_ref[head] += jnp.dot(weights, padded, preferred_element_type=jnp.float32)

    for group in range(2):
        even, odd = acc_ref[2 * group], acc_ref[2 * group + 1]
        top = jnp.where(low_lane, even, odd)
        total = pltpu.roll(jnp.where(low_lane, odd, even), HD, 1)
        o_ref[:, group * 2 * HD : (group + 1) * 2 * HD] = (top / total).astype(o_ref.dtype)


def attend_back_kernel(
    live_ref, q_ref, do_ref, k_ref, v_ref, seg_col_ref, seg_row_ref,
    dq_ref, dk_ref, dv_ref, exp_ref, dp_ref, total_ref, inner_ref, dqt_ref,
):
    at = pl.program_id(1)

    @pl.when(at == 0)
    def _():
        dk_ref[...] = jnp.zeros_like(dk_ref)
        dv_ref[...] = jnp.zeros_like(dv_ref)

    total_ref[...] = jnp.zeros_like(total_ref)
    inner_ref[...] = jnp.zeros_like(inner_ref)
    dqt_ref[...] = jnp.zeros_like(dqt_ref)

    def each_block(run):
        for back in range(LOOK):
            key_block = jnp.maximum(at - back, 0)

            @pl.when((at >= back) & (live_ref[at, key_block] > 0))
            def _():
                run(back, pl.multiple_of(key_block * BLOCK, BLOCK))

    def first(back, begin):
        same = seg_col_ref[pl.ds(begin, BLOCK), :] == seg_row_ref[...]
        if back == 0:
            row = lax.broadcasted_iota(jnp.int32, (BLOCK, BLOCK), 0)
            col = lax.broadcasted_iota(jnp.int32, (BLOCK, BLOCK), 1)
            same = same & (row <= col)
        mask = same.astype(jnp.float32)
        keys = k_ref[pl.ds(begin, BLOCK), :]
        values = v_ref[pl.ds(begin, BLOCK), :]
        for head in range(4):
            group = head // 2
            cols = slice(head * HD, (head + 1) * HD)
            kept = slice(group * HD, (group + 1) * HD)
            weights = jnp.exp(nt_dot(keys[:, kept], q_ref[:, cols])) * mask
            grads = nt_dot(values[:, kept], do_ref[:, cols])
            exp_ref[head, back] = weights
            dp_ref[head, back] = grads
            total_ref[head : head + 1] += jnp.sum(weights, axis=0, keepdims=True)
            inner_ref[head : head + 1] += jnp.sum(weights * grads, axis=0, keepdims=True)

    def second(back, begin):
        keys = k_ref[pl.ds(begin, BLOCK), :]
        dk_parts, dv_parts = [], []
        for group in range(2):
            dk_sum, dv_sum = None, None
            for head in (2 * group, 2 * group + 1):
                cols = slice(head * HD, (head + 1) * HD)
                scale = 1.0 / total_ref[head : head + 1]
                probs = exp_ref[head, back] * scale
                inner = inner_ref[head : head + 1] * scale
                low_scores = (probs * (dp_ref[head, back] - inner)).astype(jnp.bfloat16)
                dv_part = jnp.dot(
                    probs.astype(jnp.bfloat16), do_ref[:, cols], preferred_element_type=jnp.float32
                )
                dk_part = jnp.dot(low_scores, q_ref[:, cols], preferred_element_type=jnp.float32)
                dqt_ref[cols] += lax.dot_general(
                    keys[:, group * HD : (group + 1) * HD],
                    low_scores,
                    (((0,), (0,)), ((), ())),
                    preferred_element_type=jnp.float32,
                )
                dk_sum = dk_part if dk_sum is None else dk_sum + dk_part
                dv_sum = dv_part if dv_sum is None else dv_sum + dv_part
            dk_parts.append(dk_sum)
            dv_parts.append(dv_sum)
        dk_ref[pl.ds(begin, BLOCK), :] += jnp.concatenate(dk_parts, axis=1)
        dv_ref[pl.ds(begin, BLOCK), :] += jnp.concatenate(dv_parts, axis=1)

    each_block(first)
    each_block(second)
    dq_ref[...] = dqt_ref[...].T


def live_blocks(segment):
    count = segment.shape[0] // BLOCK
    blocks = segment.reshape(count, BLOCK)
    index = jnp.arange(count)
    return (
        (blocks[:, :1] == blocks[:, -1][None, :]) | (index[:, None] == index[None, :])
    ).astype(jnp.int32)


def attend(query, key, value, segment):
    rows = query.shape[0]
    panels, count = HK // 2, rows // BLOCK
    return pl.pallas_call(
        attend_kernel,
        out_shape=jax.ShapeDtypeStruct((rows, HQ * HD), jnp.bfloat16),
        grid_spec=pltpu.PrefetchScalarGridSpec(
            num_scalar_prefetch=1,
            grid=(panels, count),
            in_specs=[
                pl.BlockSpec((BLOCK, 4 * HD), lambda p, i, live: (i, p)),
                pl.BlockSpec((rows, 2 * HD), lambda p, i, live: (0, p)),
                pl.BlockSpec((rows, 2 * HD), lambda p, i, live: (0, p)),
                pl.BlockSpec((BLOCK, 1), lambda p, i, live: (i, 0)),
                pl.BlockSpec((1, rows), lambda p, i, live: (0, 0)),
            ],
            out_specs=pl.BlockSpec((BLOCK, 4 * HD), lambda p, i, live: (i, p)),
            scratch_shapes=[pltpu.VMEM((4, BLOCK, 2 * HD), jnp.float32)],
        ),
        cost_estimate=pl.CostEstimate(
            flops=24 * rows * BLOCK * LOOK * HQ * HD,
            bytes_accessed=8 * rows * HQ * HD,
            transcendentals=rows * BLOCK * LOOK * HQ,
        ),
        name="attend",
    )(live_blocks(segment), query, key, value, segment[:, None], segment[None, :])


def attend_back(query, grad_out, key, value, segment, start, panels):
    rows = query.shape[0]
    count = rows // BLOCK
    return pl.pallas_call(
        attend_back_kernel,
        out_shape=(
            jax.ShapeDtypeStruct((rows, panels * 4 * HD), jnp.float32),
            jax.ShapeDtypeStruct((rows, panels * 2 * HD), jnp.float32),
            jax.ShapeDtypeStruct((rows, panels * 2 * HD), jnp.float32),
        ),
        grid_spec=pltpu.PrefetchScalarGridSpec(
            num_scalar_prefetch=1,
            grid=(panels, count),
            in_specs=[
                pl.BlockSpec((BLOCK, 4 * HD), lambda p, i, live: (i, start + p)),
                pl.BlockSpec((BLOCK, 4 * HD), lambda p, i, live: (i, start + p)),
                pl.BlockSpec((rows, 2 * HD), lambda p, i, live: (0, start + p)),
                pl.BlockSpec((rows, 2 * HD), lambda p, i, live: (0, start + p)),
                pl.BlockSpec((rows, 1), lambda p, i, live: (0, 0)),
                pl.BlockSpec((1, BLOCK), lambda p, i, live: (0, i)),
            ],
            out_specs=[
                pl.BlockSpec((BLOCK, 4 * HD), lambda p, i, live: (i, p)),
                pl.BlockSpec((rows, 2 * HD), lambda p, i, live: (0, p)),
                pl.BlockSpec((rows, 2 * HD), lambda p, i, live: (0, p)),
            ],
            scratch_shapes=[
                pltpu.VMEM((4, LOOK, BLOCK, BLOCK), jnp.float32),
                pltpu.VMEM((4, LOOK, BLOCK, BLOCK), jnp.float32),
                pltpu.VMEM((8, BLOCK), jnp.float32),
                pltpu.VMEM((8, BLOCK), jnp.float32),
                pltpu.VMEM((4 * HD, BLOCK), jnp.float32),
            ],
        ),
        cost_estimate=pl.CostEstimate(
            flops=160 * rows * BLOCK * LOOK * HD * panels,
            bytes_accessed=64 * rows * HD * panels,
            transcendentals=4 * rows * BLOCK * LOOK * panels,
        ),
        name="attend_back",
    )(live_blocks(segment), query, grad_out, key, value, segment[:, None], segment[None, :])


def body(
    links,
    tokens,
    cotangent,
    segment,
    attn_gain,
    w_query,
    w_key,
    w_value,
    qk_gain,
    w_out,
    ffn_gain,
    w_gate,
    w_up,
    w_down,
):
    row_count = tokens.shape[0]
    score_scale = 1.0 / math.sqrt(HD)
    spare = jnp.zeros((attn_gain.shape[0] - qk_gain.shape[0],), jnp.bfloat16)
    packed = jnp.stack([attn_gain, ffn_gain, jnp.concatenate([qk_gain, spare])], axis=1)
    packed = jnp.pad(packed, ((0, 0), (0, 125)))
    attn_weights = (w_query, w_key, w_value, packed)
    front_flow = Flow(
        gather_steps(
            links,
            jnp.concatenate([core_half(weight) for weight in attn_weights], axis=1),
            jnp.concatenate(attn_weights, axis=1),
        )
    )
    out_flow = Flow(gather_steps(links, pin(core_half(w_out), front_flow.pending), w_out))
    front_flow.advance()
    gate_flow = Flow(gather_steps(links, pin(core_half(w_gate), out_flow.pending), w_gate))
    out_flow.advance()
    front = front_flow.finish()
    full_query = front[:, : HQ * HD]
    full_key = front[:, HQ * HD : (HQ + HK) * HD]
    full_value = front[:, (HQ + HK) * HD : (HQ + 2 * HK) * HD]
    gains = front[:, (HQ + 2 * HK) * HD :]
    full_attn_gain = gains[:, 0]
    full_ffn_gain = gains[:, 1]
    full_qk_gain = gains.reshape(links[0], -1, 128)[:, : qk_gain.shape[0], 2].reshape(-1)
    inputs = tokens.astype(jnp.float32)
    token_index = jnp.arange(row_count)
    same_seq = segment[:, None] == segment[None, :]
    allowed = same_seq & (token_index[None, :] <= token_index[:, None])
    positions = jnp.sum(
        (same_seq & (token_index[None, :] < token_index[:, None])).astype(jnp.float32), axis=1
    )
    live_rows = (segment >= 0).astype(jnp.float32)[:, None]
    cosine, sine_table = rope_tables(positions)
    scale_one = inv_rms(inputs)
    normed = (inputs * scale_one * full_attn_gain.astype(jnp.float32)).astype(jnp.bfloat16)
    query_lin = matmul_plain(normed, full_query).reshape(row_count, HQ, HD)
    key_lin = matmul_plain(normed, full_key).reshape(row_count, HK, HD)
    value_low = matmul_plain(normed, full_value).astype(jnp.bfloat16).reshape(row_count, HK, HD)
    qk_gains = full_qk_gain.astype(jnp.float32)
    query_scale = inv_rms(query_lin)
    key_scale = inv_rms(key_lin)
    query_rot = (
        rotate(query_lin * query_scale * qk_gains[:HD], cosine, sine_table)
        .astype(jnp.bfloat16)
    )
    key_rot = rotate(key_lin * key_scale * qk_gains[HD:], cosine, sine_table).astype(jnp.bfloat16)

    query_rot = (query_rot.astype(jnp.float32) * score_scale).astype(jnp.bfloat16)
    query_rot = query_rot.reshape(row_count, HQ * HD)
    key_rot = key_rot.reshape(row_count, HK * HD)
    value_low = value_low.reshape(row_count, HK * HD)
    up_flow = Flow(gather_steps(links, pin(core_half(w_up), out_flow.pending), w_up))
    full_out = out_flow.finish()
    query_rot, key_rot = pin((query_rot, key_rot), full_out)
    attn_low = attend(query_rot, key_rot, value_low, segment)
    attn_low = pin(attn_low, gate_flow.pending)
    gate_flow.advance()
    down_flow = Flow(gather_steps(links, pin(core_half(w_down), up_flow.pending), w_down))
    up_flow.advance()
    full_gate = gate_flow.finish()
    full_up = up_flow.finish()
    hidden = inputs + matmul_plain(attn_low, full_out)
    scale_two = inv_rms(hidden)
    normed_ffn = (hidden * scale_two * full_ffn_gain.astype(jnp.float32)).astype(jnp.bfloat16)
    gate_proj = matmul_plain(normed_ffn, full_gate)
    up_proj = matmul_plain(normed_ffn, full_up)
    gate_sig = jax.nn.sigmoid(gate_proj)
    gate_act = gate_proj * gate_sig
    mixed_act = (gate_act * up_proj).astype(jnp.bfloat16)
    slope = (up_proj * gate_sig * (1.0 + gate_proj * (1.0 - gate_sig))).astype(jnp.bfloat16)
    act_low = gate_act.astype(jnp.bfloat16)
    mixed_act, slope, act_low = pin((mixed_act, slope, act_low), down_flow.pending)
    down_flow.advance()
    full_down = down_flow.finish()
    out_grad = live_rows * cotangent.astype(jnp.float32)
    out_low = out_grad.astype(jnp.bfloat16)
    grad_mixed = matmul_cols(out_low, full_down)
    grad_up_low = (grad_mixed * act_low.astype(jnp.float32)).astype(jnp.bfloat16)
    grad_gate_low = (grad_mixed * slope.astype(jnp.float32)).astype(jnp.bfloat16)
    grad_up_low, grad_gate_low = pin((grad_up_low, grad_gate_low))
    down_part = core_sum(links, *column_halves(links, mixed_act, out_low))
    down_back = Flow(scatter_steps(links, down_part))
    gate_left = pin(grad_gate_low, down_part)
    gate_part = core_sum(links, *row_halves(links, normed_ffn, gate_left))
    up_left = pin(grad_up_low, gate_part)
    up_part = core_sum(links, *row_halves(links, normed_ffn, up_left))
    grad_gate_low = pin(grad_gate_low, up_part, down_back.pending)
    gate_back = Flow(scatter_steps(links, pin(gate_part, down_back.pending)))
    down_back.advance()
    from_gate = matmul_cols(grad_gate_low, full_gate)
    grad_up_low = pin(grad_up_low, from_gate, down_back.pending)
    down_back.advance()
    grad_normed_ffn = from_gate + matmul_cols(grad_up_low, full_up)
    grad_normed_ffn = pin(grad_normed_ffn, gate_back.pending, down_back.pending)
    up_back = Flow(scatter_steps(links, pin(up_part, gate_back.pending)))
    gate_back.advance()
    down_back.advance()
    grad_ffn_gain = jnp.sum(grad_normed_ffn * hidden * scale_two, axis=0)
    grad_hidden = out_grad + norm_back(
        grad_normed_ffn, hidden, scale_two, full_ffn_gain.astype(jnp.float32)
    )
    hidden_low = grad_hidden.astype(jnp.bfloat16)
    grad_attn_low = matmul_cols(hidden_low, full_out).astype(jnp.bfloat16)
    out_part = core_sum(links, *row_halves(links, attn_low, hidden_low))
    panels = HK // 4
    grad_attn_low = pin(grad_attn_low, out_part, down_back.pending)
    down_back.advance()
    lower = attend_back(query_rot, grad_attn_low, key_rot, value_low, segment, 0, panels)
    grad_attn_low = pin(grad_attn_low, lower, gate_back.pending, up_back.pending, down_back.pending)
    gate_back.advance()
    up_back.advance()
    down_back.advance()
    upper = attend_back(query_rot, grad_attn_low, key_rot, value_low, segment, panels, panels)
    upper = pin(upper, up_back.pending, gate_back.pending)
    out_back = Flow(scatter_steps(links, pin(out_part, up_back.pending)))
    up_back.advance()
    gate_back.advance()
    grad_query_rot, grad_key_rot, grad_value = (
        jnp.concatenate(pair, axis=1) for pair in zip(lower, upper)
    )
    grad_query_rot = (score_scale * grad_query_rot).reshape(row_count, HQ, HD)
    grad_key_rot = grad_key_rot.reshape(row_count, HK, HD)
    grad_query_norm = rotate_back(grad_query_rot, cosine, sine_table)
    grad_key_norm = rotate_back(grad_key_rot, cosine, sine_table)
    back_gains = full_qk_gain.astype(jnp.float32)
    grad_qk_gain = jnp.concatenate(
        [
            jnp.sum(grad_query_norm * query_lin * query_scale, axis=(0, 1)),
            jnp.sum(grad_key_norm * key_lin * key_scale, axis=(0, 1)),
        ]
    )
    grad_query_low = (
        norm_back(grad_query_norm, query_lin, query_scale, back_gains[:HD])
        .astype(jnp.bfloat16)
        .reshape(row_count, HQ * HD)
    )
    grad_key_low = (
        norm_back(grad_key_norm, key_lin, key_scale, back_gains[HD:])
        .astype(jnp.bfloat16)
        .reshape(row_count, HK * HD)
    )
    grad_value_low = grad_value.astype(jnp.bfloat16).reshape(row_count, HK * HD)
    grad_normed = (
        matmul_cols(grad_query_low, full_query)
        + matmul_cols(grad_key_low, full_key)
        + matmul_cols(grad_value_low, full_value)
    )
    grad_attn_gain = jnp.sum(grad_normed * inputs * scale_one, axis=0)
    grad_inputs = grad_hidden + norm_back(
        grad_normed, inputs, scale_one, full_attn_gain.astype(jnp.float32)
    )
    small = jnp.zeros((links[0], attn_gain.shape[0], 128), jnp.float32)
    small = small.at[:, :, 0].set(grad_attn_gain.reshape(links[0], -1))
    small = small.at[:, :, 1].set(grad_ffn_gain.reshape(links[0], -1))
    small = small.at[:, : qk_gain.shape[0], 2].set(grad_qk_gain.reshape(links[0], -1))
    small = small.reshape(links[0], 2, -1, 128)
    core = lax.rem(lax.axis_index("rep"), 2)
    own_front, other_front = row_halves(
        links, normed, jnp.concatenate([grad_query_low, grad_key_low, grad_value_low], axis=1)
    )

    def with_small(product, which):
        extra = lax.dynamic_slice_in_dim(small, which, 1, 1)[:, 0]
        return jnp.concatenate([product(), extra], axis=2)

    front_part = core_sum(
        links,
        lambda: with_small(own_front, core),
        lambda: with_small(other_front, 1 - core),
    )
    front_back = Flow(scatter_steps(links, pin(front_part, out_back.pending)))
    last_act = pin(mixed_act, front_part)
    result = live_rows * (hidden + matmul_plain(last_act, full_down))
    front_share = join_rows(front_back.finish())
    share_query = front_share[:, : HQ * HD]
    share_key = front_share[:, HQ * HD : (HQ + HK) * HD]
    share_value = front_share[:, (HQ + HK) * HD : (HQ + 2 * HK) * HD]
    extras = front_share[:, (HQ + 2 * HK) * HD :]
    share_again = extras[:, 0]
    share_fgain = extras[:, 1]
    share_qk = extras[: qk_gain.shape[0], 2]
    share_out = join_rows(out_back.finish())
    share_gate = join_rows(gate_back.finish())
    share_up = join_rows(up_back.finish())
    share_down = join_columns(down_back.finish())
    return (
        result.astype(jnp.bfloat16),
        grad_inputs.astype(jnp.bfloat16),
        share_again,
        share_query,
        share_key,
        share_value,
        share_qk,
        share_out,
        share_fgain,
        share_gate,
        share_up,
        share_down,
    )


def solution(mesh):
    return jax.shard_map(
        functools.partial(body, make_links(mesh)),
        mesh=mesh,
        in_specs=(
            P(("shard", "rep"), None),
            P(("shard", "rep"), None),
            P(("shard", "rep")),
            P("shard"),
            P("shard", None),
            P("shard", None),
            P("shard", None),
            P("shard"),
            P("shard", None),
            P("shard"),
            P("shard", None),
            P("shard", None),
            P("shard", None),
        ),
        out_specs=(
            P(("shard", "rep"), None),
            P(("shard", "rep"), None),
            P("shard"),
            P("shard", None),
            P("shard", None),
            P("shard", None),
            P("shard"),
            P("shard", None),
            P("shard"),
            P("shard", None),
            P("shard", None),
            P("shard", None),
        ),
        check_vma=False,
    )
```

```python
import functools
import math

import jax
import jax.numpy as jnp
from jax import lax
from jax.experimental import pallas as pl
from jax.experimental.pallas import tpu as pltpu
from jax.sharding import PartitionSpec as P

HQ = 16
HK = 8
HD = 64


norm_eps = 1e-05
rope_base = 1000000.0


def inv_rms(values):
    return lax.rsqrt(jnp.mean(values * values, axis=-1, keepdims=True) + norm_eps)


def rope_tables(positions):
    half_dim = HD // 2
    freq_index = jnp.arange(half_dim).astype(jnp.float32)
    freq_vals = jnp.power(rope_base, -(2.0 * freq_index) / HD)
    angles = positions[:, None] * freq_vals[None, :]
    return (jnp.cos(angles)[:, None, :], jnp.sin(angles)[:, None, :])


def rotate(values, cosine, sine_table):
    half_dim = HD // 2
    first_half = values[..., :half_dim]
    second_half = values[..., half_dim:]
    return jnp.concatenate(
        [
            first_half * cosine - second_half * sine_table,
            second_half * cosine + first_half * sine_table,
        ],
        axis=-1,
    )


def rotate_back(grad_vals, cosine, sine_table):
    half_dim = HD // 2
    first_half = grad_vals[..., :half_dim]
    second_half = grad_vals[..., half_dim:]
    return jnp.concatenate(
        [
            first_half * cosine + second_half * sine_table,
            second_half * cosine - first_half * sine_table,
        ],
        axis=-1,
    )


def norm_back(grad_out, inputs, scale_inv, gain_vec):
    weighted = grad_out * gain_vec
    row_inner = jnp.mean(weighted * inputs, axis=-1, keepdims=True)
    return scale_inv * weighted - inputs * (scale_inv * scale_inv * scale_inv) * row_inner


def matmul_plain(left_mat, right_mat):
    return jnp.dot(left_mat, right_mat, preferred_element_type=jnp.float32)


def matmul_rows(left_mat, right_mat):
    return lax.dot_general(
        left_mat, right_mat, (((0,), (0,)), ((), ())), preferred_element_type=jnp.float32
    )


def matmul_cols(left_mat, right_mat):
    return lax.dot_general(
        left_mat, right_mat, (((1,), (1,)), ((), ())), preferred_element_type=jnp.float32
    )


def make_links(mesh):
    shard_size, rep_size = mesh.shape["shard"], mesh.shape["rep"]
    axes = ("shard", "rep")

    def shard_swap(value, bit):
        pairs = [
            (s * rep_size + r, (s ^ bit) * rep_size + r)
            for s in range(shard_size)
            for r in range(rep_size)
        ]
        return lax.ppermute(value, axes, pairs)

    def rep_swap(value, bit):
        pairs = [
            (s * rep_size + r, s * rep_size + (r ^ bit))
            for s in range(shard_size)
            for r in range(rep_size)
        ]
        return lax.ppermute(value, axes, pairs)

    return shard_size, rep_size, shard_swap, rep_swap


def add_low(left, right):
    return (left.astype(jnp.float32) + right.astype(jnp.float32)).astype(jnp.bfloat16)


def pin(values, *waits):
    return lax.optimization_barrier((values, waits))[0]


class Flow:
    def __init__(self, steps):
        self.steps = steps
        self.result = None
        self.pending = next(steps)

    def resume(self, arrived):
        try:
            self.pending = self.steps.send(arrived)
        except StopIteration as stop:
            self.pending = ()
            self.steps = None
            self.result = stop.value

    def finish(self):
        while self.steps is not None:
            self.resume(self.pending)
        return self.result


def sync(values, *flows):
    flows = [flow for flow in flows if flow.steps is not None]
    values, arrived = lax.optimization_barrier((values, [flow.pending for flow in flows]))
    for flow, got in zip(flows, arrived):
        flow.resume(got)
    return values


def place_kernel(spots_ref, *refs):
    del spots_ref
    out_ref = refs[-1]
    for at in range(len(refs) - 1):

        @pl.when(pl.program_id(0) == at)
        def _():
            out_ref[...] = refs[at][...]


def place_blocks(blocks, spots):
    count = len(blocks)
    rows, width = blocks[0].shape
    return pl.pallas_call(
        place_kernel,
        out_shape=jax.ShapeDtypeStruct((count * rows, width), blocks[0].dtype),
        grid_spec=pltpu.PrefetchScalarGridSpec(
            num_scalar_prefetch=1,
            grid=(count,),
            in_specs=[
                pl.BlockSpec((rows, width), lambda i, spot: (0, 0), pipeline_mode=pl.Buffered(1))
                for _ in blocks
            ],
            out_specs=pl.BlockSpec((rows, width), lambda i, spot: (spot[i], 0)),
        ),
        cost_estimate=pl.CostEstimate(
            flops=0, bytes_accessed=4 * count * rows * width, transcendentals=0
        ),
        compiler_params=pltpu.CompilerParams(vmem_limit_bytes=60 << 20),
        name="place_blocks",
    )(jnp.stack(spots).astype(jnp.int32), *blocks)


def gather_steps(links, mine, whole):
    shard_size, rep_size, shard_swap, rep_swap = links
    me = lax.axis_index("shard")
    core = lax.rem(lax.axis_index("rep"), 2)
    half, width = mine.shape
    quarter = half // 2
    pieces, others = {}, {}
    if shard_size == 4:
        pieces[1] = shard_swap(mine, 1)
        pieces[2] = shard_swap(mine, 2)
        pieces[1], pieces[2] = yield (pieces[1], pieces[2])
        corner_a = shard_swap(pieces[1][:quarter], 2)
        corner_b = shard_swap(pieces[2][quarter:], 1)
        others[1] = rep_swap(pieces[1], 1)
        others[2] = rep_swap(pieces[2], 1)
        corner_a, corner_b, others[1], others[2] = yield (
            corner_a, corner_b, others[1], others[2]
        )
        pieces[3] = jnp.concatenate([corner_a, corner_b], axis=0)
        others[3] = rep_swap(pieces[3], 1)
        (others[3],) = yield (others[3],)
    else:
        pieces[0] = mine
        bit = 1
        while bit < shard_size:
            order = sorted(pieces)
            got = shard_swap(jnp.stack([pieces[d] for d in order]), bit)
            (got,) = yield (got,)
            for at, d in enumerate(order):
                pieces[d ^ bit] = got[at]
            bit *= 2
        del pieces[0]
        others = {d: rep_swap(piece, 1) for d, piece in pieces.items()}
    blocks, spots = [whole[:half], whole[half:]], [2 * me, 2 * me + 1]
    for d in pieces:
        blocks += [pieces[d], others[d]]
        spots += [2 * (me ^ d) + core, 2 * (me ^ d) + 1 - core]
    return place_blocks(blocks, spots)


def core_half(weight):
    core = lax.rem(lax.axis_index("rep"), 2)
    half = weight.shape[0] // 2
    return lax.dynamic_slice_in_dim(weight, core * half, half, 0)


def pick_columns(links, value):
    core = lax.rem(lax.axis_index("rep"), 2)
    width = value.shape[1] // links[0] // 2

    def half(which):
        return jnp.concatenate(
            [
                lax.dynamic_slice_in_dim(value, (2 * d + which) * width, width, 1)
                for d in range(links[0])
            ],
            axis=1,
        )

    return half(core), half(1 - core)


def blocked(links, product):
    return product.reshape(links[0], -1, product.shape[1])


def combine(product, received):
    return (product + received.astype(jnp.float32)).astype(jnp.bfloat16)


def scatter_steps(links, part):
    shard_size, rep_size, shard_swap, rep_swap = links
    me = lax.axis_index("shard")
    rep = lax.axis_index("rep")
    rows = part.shape[1] // 2

    def piece(d, at):
        return lax.dynamic_slice(
            part, (me ^ d, at * rows, 0), (1, rows, part.shape[2])
        )[0]

    if shard_size == 4:
        got_a = shard_swap(jnp.stack([piece(1, 0), piece(3, 0)]), 1)
        got_b = shard_swap(jnp.stack([piece(2, 1), piece(3, 1)]), 2)
        got_a, got_b = yield (got_a, got_b)
        pass_a = shard_swap(add_low(piece(2, 0), got_a[1]), 2)
        pass_b = shard_swap(add_low(piece(1, 1), got_b[1]), 1)
        pass_a, pass_b = yield (pass_a, pass_b)
        sum_a = add_low(piece(0, 0).astype(jnp.float32) + got_a[0].astype(jnp.float32), pass_a)
        sum_b = add_low(piece(0, 1).astype(jnp.float32) + got_b[0].astype(jnp.float32), pass_b)
        halves = [sum_a, sum_b]
    else:
        held = {d: jnp.stack([piece(d, 0), piece(d, 1)]) for d in range(shard_size)}
        bit = shard_size // 2
        while bit:
            sent = [d for d in sorted(held) if d & bit]
            got = shard_swap(jnp.stack([held[d] for d in sent]), bit)
            (got,) = yield (got,)
            held = {d ^ bit: add_low(held[d ^ bit], got[at]) for at, d in enumerate(sent)}
            bit //= 2
        halves = [held[0][0], held[0][1]]
    upper = lax.rem(rep // 2, 2) == 1
    if rep_size >= 8:
        keep = jnp.where(upper, halves[1], halves[0])
        send = jnp.where(upper, halves[0], halves[1])
        got = rep_swap(send, 2)
        (got,) = yield (got,)
        keep = add_low(keep, got)
        bit = 4
        while bit < rep_size:
            got = rep_swap(keep, bit)
            (got,) = yield (got,)
            keep = add_low(keep, got)
            bit *= 2
        back = rep_swap(keep, 2)
        (back,) = yield (back,)
        halves = [jnp.where(upper, back, keep), jnp.where(upper, keep, back)]
        half = jnp.concatenate(halves, axis=0)
    else:
        half = jnp.concatenate(halves, axis=0)
        bit = 2
        while bit < rep_size:
            half = add_low(half, rep_swap(half, bit))
            bit *= 2
    other = rep_swap(half, 1)
    (other,) = yield (other,)
    return half, other


def join_rows(pair):
    core = lax.rem(lax.axis_index("rep"), 2)
    half, other = pair
    return jnp.where(
        core == 0,
        jnp.concatenate([half, other], axis=0),
        jnp.concatenate([other, half], axis=0),
    ).astype(jnp.float32)


def join_columns(pair):
    core = lax.rem(lax.axis_index("rep"), 2)
    half, other = pair
    return jnp.where(
        core == 0,
        jnp.concatenate([half, other], axis=1),
        jnp.concatenate([other, half], axis=1),
    ).astype(jnp.float32)


BLOCK = 256
LOOK = 3


def nt_dot(left_mat, right_mat):
    return lax.dot_general(
        left_mat, right_mat, (((1,), (1,)), ((), ())), preferred_element_type=jnp.float32
    )


def attend_kernel(live_ref, q_ref, k_ref, v_ref, seg_col_ref, seg_row_ref, o_ref, acc_ref):
    at = pl.program_id(1)
    acc_ref[...] = jnp.zeros_like(acc_ref)
    lane = lax.broadcasted_iota(jnp.int32, (BLOCK, 2 * HD), 1)
    low_lane = lane < HD
    for back in range(LOOK):
        key_block = jnp.maximum(at - back, 0)

        @pl.when((at >= back) & (live_ref[at, key_block] > 0))
        def _():
            begin = pl.multiple_of(key_block * BLOCK, BLOCK)
            same = seg_col_ref[...] == seg_row_ref[:, pl.ds(begin, BLOCK)]
            if back == 0:
                row = lax.broadcasted_iota(jnp.int32, (BLOCK, BLOCK), 0)
                col = lax.broadcasted_iota(jnp.int32, (BLOCK, BLOCK), 1)
                same = same & (col <= row)
            mask = same.astype(jnp.float32)
            keys = k_ref[pl.ds(begin, BLOCK), :]
            values = v_ref[pl.ds(begin, BLOCK), :]
            swapped = pltpu.roll(values.astype(jnp.float32), HD, 1).astype(jnp.bfloat16)
            one = jnp.ones_like(values)
            for head in range(4):
                group, odd = head // 2, head % 2
                scores = nt_dot(
                    q_ref[:, head * HD : (head + 1) * HD], keys[:, group * HD : (group + 1) * HD]
                )
                weights = (jnp.exp(scores) * mask).astype(jnp.bfloat16)
                held = values if group == odd else swapped
                padded = jnp.where(low_lane, held, one) if odd == 0 else jnp.where(low_lane, one, held)
                acc_ref[head] += jnp.dot(weights, padded, preferred_element_type=jnp.float32)

    for group in range(2):
        even, odd = acc_ref[2 * group], acc_ref[2 * group + 1]
        top = jnp.where(low_lane, even, odd)
        total = pltpu.roll(jnp.where(low_lane, odd, even), HD, 1)
        o_ref[:, group * 2 * HD : (group + 1) * 2 * HD] = (top / total).astype(o_ref.dtype)


def attend_back_kernel(
    live_ref, q_ref, do_ref, k_ref, v_ref, seg_col_ref, seg_row_ref,
    dq_ref, dk_ref, dv_ref, exp_ref, dp_ref, total_ref, inner_ref, dqt_ref,
):
    at = pl.program_id(1)

    @pl.when(at == 0)
    def _():
        dk_ref[...] = jnp.zeros_like(dk_ref)
        dv_ref[...] = jnp.zeros_like(dv_ref)

    total_ref[...] = jnp.zeros_like(total_ref)
    inner_ref[...] = jnp.zeros_like(inner_ref)
    dqt_ref[...] = jnp.zeros_like(dqt_ref)

    def each_block(run):
        for back in range(LOOK):
            key_block = jnp.maximum(at - back, 0)

            @pl.when((at >= back) & (live_ref[at, key_block] > 0))
            def _():
                run(back, pl.multiple_of(key_block * BLOCK, BLOCK))

    def first(back, begin):
        same = seg_col_ref[pl.ds(begin, BLOCK), :] == seg_row_ref[...]
        if back == 0:
            row = lax.broadcasted_iota(jnp.int32, (BLOCK, BLOCK), 0)
            col = lax.broadcasted_iota(jnp.int32, (BLOCK, BLOCK), 1)
            same = same & (row <= col)
        mask = same.astype(jnp.float32)
        keys = k_ref[pl.ds(begin, BLOCK), :]
        values = v_ref[pl.ds(begin, BLOCK), :]
        for head in range(4):
            group = head // 2
            cols = slice(head * HD, (head + 1) * HD)
            kept = slice(group * HD, (group + 1) * HD)
            weights = jnp.exp(nt_dot(keys[:, kept], q_ref[:, cols])) * mask
            grads = nt_dot(values[:, kept], do_ref[:, cols])
            exp_ref[head, back] = weights
            dp_ref[head, back] = grads
            total_ref[head : head + 1] += jnp.sum(weights, axis=0, keepdims=True)
            inner_ref[head : head + 1] += jnp.sum(weights * grads, axis=0, keepdims=True)

    def second(back, begin):
        keys = k_ref[pl.ds(begin, BLOCK), :]
        dk_parts, dv_parts = [], []
        for group in range(2):
            dk_sum, dv_sum = None, None
            for head in (2 * group, 2 * group + 1):
                cols = slice(head * HD, (head + 1) * HD)
                scale = 1.0 / total_ref[head : head + 1]
                probs = exp_ref[head, back] * scale
                inner = inner_ref[head : head + 1] * scale
                low_scores = (probs * (dp_ref[head, back] - inner)).astype(jnp.bfloat16)
                dv_part = jnp.dot(
                    probs.astype(jnp.bfloat16), do_ref[:, cols], preferred_element_type=jnp.float32
                )
                dk_part = jnp.dot(low_scores, q_ref[:, cols], preferred_element_type=jnp.float32)
                dqt_ref[cols] += lax.dot_general(
                    keys[:, group * HD : (group + 1) * HD],
                    low_scores,
                    (((0,), (0,)), ((), ())),
                    preferred_element_type=jnp.float32,
                )
                dk_sum = dk_part if dk_sum is None else dk_sum + dk_part
                dv_sum = dv_part if dv_sum is None else dv_sum + dv_part
            dk_parts.append(dk_sum)
            dv_parts.append(dv_sum)
        dk_ref[pl.ds(begin, BLOCK), :] += jnp.concatenate(dk_parts, axis=1)
        dv_ref[pl.ds(begin, BLOCK), :] += jnp.concatenate(dv_parts, axis=1)

    each_block(first)
    each_block(second)
    dq_ref[...] = dqt_ref[...].T


def live_blocks(segment):
    count = segment.shape[0] // BLOCK
    blocks = segment.reshape(count, BLOCK)
    index = jnp.arange(count)
    return (
        (blocks[:, :1] == blocks[:, -1][None, :]) | (index[:, None] == index[None, :])
    ).astype(jnp.int32)


def attend(query, key, value, segment):
    rows = query.shape[0]
    panels, count = HK // 2, rows // BLOCK
    return pl.pallas_call(
        attend_kernel,
        out_shape=jax.ShapeDtypeStruct((rows, HQ * HD), jnp.bfloat16),
        grid_spec=pltpu.PrefetchScalarGridSpec(
            num_scalar_prefetch=1,
            grid=(panels, count),
            in_specs=[
                pl.BlockSpec((BLOCK, 4 * HD), lambda p, i, live: (i, p)),
                pl.BlockSpec((rows, 2 * HD), lambda p, i, live: (0, p)),
                pl.BlockSpec((rows, 2 * HD), lambda p, i, live: (0, p)),
                pl.BlockSpec((BLOCK, 1), lambda p, i, live: (i, 0)),
                pl.BlockSpec((1, rows), lambda p, i, live: (0, 0)),
            ],
            out_specs=pl.BlockSpec((BLOCK, 4 * HD), lambda p, i, live: (i, p)),
            scratch_shapes=[pltpu.VMEM((4, BLOCK, 2 * HD), jnp.float32)],
        ),
        cost_estimate=pl.CostEstimate(
            flops=24 * rows * BLOCK * LOOK * HQ * HD,
            bytes_accessed=8 * rows * HQ * HD,
            transcendentals=rows * BLOCK * LOOK * HQ,
        ),
        name="attend",
    )(live_blocks(segment), query, key, value, segment[:, None], segment[None, :])


def attend_back(query, grad_out, key, value, segment, start, panels):
    rows = query.shape[0]
    count = rows // BLOCK
    return pl.pallas_call(
        attend_back_kernel,
        out_shape=(
            jax.ShapeDtypeStruct((rows, panels * 4 * HD), jnp.float32),
            jax.ShapeDtypeStruct((rows, panels * 2 * HD), jnp.float32),
            jax.ShapeDtypeStruct((rows, panels * 2 * HD), jnp.float32),
        ),
        grid_spec=pltpu.PrefetchScalarGridSpec(
            num_scalar_prefetch=1,
            grid=(panels, count),
            in_specs=[
                pl.BlockSpec((BLOCK, 4 * HD), lambda p, i, live: (i, start + p)),
                pl.BlockSpec((BLOCK, 4 * HD), lambda p, i, live: (i, start + p)),
                pl.BlockSpec((rows, 2 * HD), lambda p, i, live: (0, start + p)),
                pl.BlockSpec((rows, 2 * HD), lambda p, i, live: (0, start + p)),
                pl.BlockSpec((rows, 1), lambda p, i, live: (0, 0)),
                pl.BlockSpec((1, BLOCK), lambda p, i, live: (0, i)),
            ],
            out_specs=[
                pl.BlockSpec((BLOCK, 4 * HD), lambda p, i, live: (i, p)),
                pl.BlockSpec((rows, 2 * HD), lambda p, i, live: (0, p)),
                pl.BlockSpec((rows, 2 * HD), lambda p, i, live: (0, p)),
            ],
            scratch_shapes=[
                pltpu.VMEM((4, LOOK, BLOCK, BLOCK), jnp.float32),
                pltpu.VMEM((4, LOOK, BLOCK, BLOCK), jnp.float32),
                pltpu.VMEM((8, BLOCK), jnp.float32),
                pltpu.VMEM((8, BLOCK), jnp.float32),
                pltpu.VMEM((4 * HD, BLOCK), jnp.float32),
            ],
        ),
        cost_estimate=pl.CostEstimate(
            flops=160 * rows * BLOCK * LOOK * HD * panels,
            bytes_accessed=64 * rows * HD * panels,
            transcendentals=4 * rows * BLOCK * LOOK * panels,
        ),
        name="attend_back",
    )(live_blocks(segment), query, grad_out, key, value, segment[:, None], segment[None, :])


def body(
    links,
    tokens,
    cotangent,
    segment,
    attn_gain,
    w_query,
    w_key,
    w_value,
    qk_gain,
    w_out,
    ffn_gain,
    w_gate,
    w_up,
    w_down,
):
    row_count = tokens.shape[0]
    rep_swap = links[3]
    core = lax.rem(lax.axis_index("rep"), 2)
    score_scale = 1.0 / math.sqrt(HD)
    spare = jnp.zeros((attn_gain.shape[0] - qk_gain.shape[0],), jnp.bfloat16)
    packed = jnp.stack([attn_gain, ffn_gain, jnp.concatenate([qk_gain, spare])], axis=1)
    packed = jnp.pad(packed, ((0, 0), (0, 125)))
    attn_weights = (w_query, w_key, w_value, packed)
    front_flow = Flow(
        gather_steps(
            links,
            jnp.concatenate([core_half(weight) for weight in attn_weights], axis=1),
            jnp.concatenate(attn_weights, axis=1),
        )
    )
    w_out, w_gate, w_up, w_down = sync((w_out, w_gate, w_up, w_down), front_flow)
    out_flow = Flow(gather_steps(links, core_half(w_out), w_out))
    w_gate, w_up, w_down = sync((w_gate, w_up, w_down), front_flow, out_flow)
    gate_flow = Flow(gather_steps(links, core_half(w_gate), w_gate))
    w_up, w_down = sync((w_up, w_down), front_flow)
    front = front_flow.finish()
    full_query = front[:, : HQ * HD]
    full_key = front[:, HQ * HD : (HQ + HK) * HD]
    full_value = front[:, (HQ + HK) * HD : (HQ + 2 * HK) * HD]
    gains = front[:, (HQ + 2 * HK) * HD :]
    full_attn_gain = gains[:, 0]
    full_ffn_gain = gains[:, 1]
    full_qk_gain = gains.reshape(links[0], -1, 128)[:, : qk_gain.shape[0], 2].reshape(-1)
    inputs = tokens.astype(jnp.float32)
    token_index = jnp.arange(row_count)
    same_seq = segment[:, None] == segment[None, :]
    allowed = same_seq & (token_index[None, :] <= token_index[:, None])
    positions = jnp.sum(
        (same_seq & (token_index[None, :] < token_index[:, None])).astype(jnp.float32), axis=1
    )
    live_rows = (segment >= 0).astype(jnp.float32)[:, None]
    cosine, sine_table = rope_tables(positions)
    scale_one = inv_rms(inputs)
    normed = (inputs * scale_one * full_attn_gain.astype(jnp.float32)).astype(jnp.bfloat16)
    query_lin = matmul_plain(normed, full_query).reshape(row_count, HQ, HD)
    key_lin = matmul_plain(normed, full_key).reshape(row_count, HK, HD)
    value_low = matmul_plain(normed, full_value).astype(jnp.bfloat16).reshape(row_count, HK, HD)
    qk_gains = full_qk_gain.astype(jnp.float32)
    query_scale = inv_rms(query_lin)
    key_scale = inv_rms(key_lin)
    query_rot = (
        rotate(query_lin * query_scale * qk_gains[:HD], cosine, sine_table)
        .astype(jnp.bfloat16)
    )
    key_rot = rotate(key_lin * key_scale * qk_gains[HD:], cosine, sine_table).astype(jnp.bfloat16)

    query_rot = (query_rot.astype(jnp.float32) * score_scale).astype(jnp.bfloat16)
    query_rot = query_rot.reshape(row_count, HQ * HD)
    key_rot = key_rot.reshape(row_count, HK * HD)
    value_low = value_low.reshape(row_count, HK * HD)
    query_rot, key_rot, value_low, w_up, w_down = sync(
        (query_rot, key_rot, value_low, w_up, w_down), out_flow, gate_flow
    )
    up_flow = Flow(gather_steps(links, core_half(w_up), w_up))
    attn_low = attend(query_rot, key_rot, value_low, segment)
    attn_low = sync(attn_low, out_flow)
    full_out = out_flow.finish()
    hidden = inputs + matmul_plain(attn_low, full_out)
    scale_two = inv_rms(hidden)
    normed_ffn = (hidden * scale_two * full_ffn_gain.astype(jnp.float32)).astype(jnp.bfloat16)
    normed_ffn, hidden, w_down = sync((normed_ffn, hidden, w_down), gate_flow, up_flow)
    down_flow = Flow(gather_steps(links, core_half(w_down), w_down))
    normed_ffn = sync(normed_ffn, gate_flow)
    full_gate = gate_flow.finish()
    gate_proj = matmul_plain(normed_ffn, full_gate)
    gate_proj, normed_ffn = sync((gate_proj, normed_ffn), up_flow, down_flow)
    normed_ffn = sync(normed_ffn, up_flow)
    full_up = up_flow.finish()
    up_proj = matmul_plain(normed_ffn, full_up)
    gate_sig = jax.nn.sigmoid(gate_proj)
    gate_act = gate_proj * gate_sig
    mixed_act = (gate_act * up_proj).astype(jnp.bfloat16)
    slope = (up_proj * gate_sig * (1.0 + gate_proj * (1.0 - gate_sig))).astype(jnp.bfloat16)
    act_low = gate_act.astype(jnp.bfloat16)
    mixed_act, slope, act_low = sync((mixed_act, slope, act_low), down_flow)
    mixed_act, slope, act_low = sync((mixed_act, slope, act_low), down_flow)
    full_down = down_flow.finish()
    out_grad = live_rows * cotangent.astype(jnp.float32)
    out_low = out_grad.astype(jnp.bfloat16)
    grad_mixed = matmul_cols(out_low, full_down)
    grad_up_low = (grad_mixed * act_low.astype(jnp.float32)).astype(jnp.bfloat16)
    grad_gate_low = (grad_mixed * slope.astype(jnp.float32)).astype(jnp.bfloat16)
    half = out_low.shape[1] // 2
    out_own = lax.dynamic_slice_in_dim(out_low, core * half, half, 1)
    out_other = lax.dynamic_slice_in_dim(out_low, (1 - core) * half, half, 1)
    normed_own, normed_other = pick_columns(links, normed_ffn)
    grad_up_low, grad_gate_low, out_own, out_other, mixed_act = pin(
        (grad_up_low, grad_gate_low, out_own, out_other, mixed_act)
    )

    def hand(product):
        return rep_swap(blocked(links, product).astype(jnp.bfloat16), 1)

    down_sent = hand(matmul_rows(mixed_act, out_other))
    gate_given = matmul_rows(normed_other, pin(grad_gate_low, down_sent)).astype(jnp.bfloat16)
    gate_sent = hand(gate_given)
    down_sent, mixed_act, grad_up_low, gate_given = pin(
        (down_sent, mixed_act, grad_up_low, gate_given)
    )
    down_part = combine(blocked(links, matmul_rows(mixed_act, out_own)), down_sent)
    down_back = Flow(scatter_steps(links, down_part))
    grad_up_low, grad_gate_low, normed_own, normed_other = pin(
        (grad_up_low, grad_gate_low, normed_own, normed_other), down_part
    )
    up_sent = hand(matmul_rows(normed_other, grad_up_low))
    gate_part = combine(blocked(links, matmul_rows(normed_own, grad_gate_low)), gate_sent)
    up_part = combine(blocked(links, matmul_rows(normed_own, grad_up_low)), up_sent)
    gate_part, up_part, grad_gate_low, grad_up_low = sync(
        (gate_part, up_part, grad_gate_low, grad_up_low), down_back
    )
    gate_back = Flow(scatter_steps(links, gate_part))
    grad_normed_ffn = matmul_cols(grad_gate_low, full_gate) + matmul_cols(grad_up_low, full_up)
    grad_normed_ffn, up_part = sync((grad_normed_ffn, up_part), down_back)
    grad_ffn_gain = jnp.sum(grad_normed_ffn * hidden * scale_two, axis=0)
    grad_hidden = out_grad + norm_back(
        grad_normed_ffn, hidden, scale_two, full_ffn_gain.astype(jnp.float32)
    )
    hidden_low = grad_hidden.astype(jnp.bfloat16)
    grad_attn_low = matmul_cols(hidden_low, full_out).astype(jnp.bfloat16)
    attn_own, attn_other = pick_columns(links, attn_low)
    out_sent = hand(matmul_rows(attn_other, hidden_low))
    out_part = combine(blocked(links, matmul_rows(attn_own, hidden_low)), out_sent)
    panels = HK // 4
    grad_attn_low, out_part, up_part = sync(
        (grad_attn_low, out_part, up_part), gate_back, down_back
    )
    up_back = Flow(scatter_steps(links, up_part))
    lower = attend_back(query_rot, grad_attn_low, key_rot, value_low, segment, 0, panels)
    grad_attn_low, lower = pin((grad_attn_low, lower))
    upper = attend_back(query_rot, grad_attn_low, key_rot, value_low, segment, panels, panels)
    lower, upper, out_part = sync((lower, upper, out_part), gate_back, down_back)
    out_back = Flow(scatter_steps(links, out_part))
    grad_query_rot, grad_key_rot, grad_value = (
        jnp.concatenate(pair, axis=1) for pair in zip(lower, upper)
    )
    grad_query_rot = (score_scale * grad_query_rot).reshape(row_count, HQ, HD)
    grad_key_rot = grad_key_rot.reshape(row_count, HK, HD)
    grad_query_norm = rotate_back(grad_query_rot, cosine, sine_table)
    grad_key_norm = rotate_back(grad_key_rot, cosine, sine_table)
    back_gains = full_qk_gain.astype(jnp.float32)
    grad_qk_gain = jnp.concatenate(
        [
            jnp.sum(grad_query_norm * query_lin * query_scale, axis=(0, 1)),
            jnp.sum(grad_key_norm * key_lin * key_scale, axis=(0, 1)),
        ]
    )
    grad_query_low = (
        norm_back(grad_query_norm, query_lin, query_scale, back_gains[:HD])
        .astype(jnp.bfloat16)
        .reshape(row_count, HQ * HD)
    )
    grad_key_low = (
        norm_back(grad_key_norm, key_lin, key_scale, back_gains[HD:])
        .astype(jnp.bfloat16)
        .reshape(row_count, HK * HD)
    )
    grad_value_low = grad_value.astype(jnp.bfloat16).reshape(row_count, HK * HD)
    normed_own, normed_other = pick_columns(links, normed)
    grad_front = jnp.concatenate([grad_query_low, grad_key_low, grad_value_low], axis=1)
    grad_front = sync(grad_front, up_back, gate_back, down_back, out_back)
    grad_query_low = grad_front[:, : HQ * HD]
    grad_key_low = grad_front[:, HQ * HD : (HQ + HK) * HD]
    grad_value_low = grad_front[:, (HQ + HK) * HD :]
    front_other = blocked(links, matmul_rows(normed_other, grad_front))
    front_own = blocked(links, matmul_rows(normed_own, grad_front))
    grad_normed = (
        matmul_cols(grad_query_low, full_query)
        + matmul_cols(grad_key_low, full_key)
        + matmul_cols(grad_value_low, full_value)
    )
    grad_attn_gain = jnp.sum(grad_normed * inputs * scale_one, axis=0)
    grad_inputs = grad_hidden + norm_back(
        grad_normed, inputs, scale_one, full_attn_gain.astype(jnp.float32)
    )
    small = jnp.zeros((links[0], attn_gain.shape[0], 128), jnp.float32)
    small = small.at[:, :, 0].set(grad_attn_gain.reshape(links[0], -1))
    small = small.at[:, :, 1].set(grad_ffn_gain.reshape(links[0], -1))
    small = small.at[:, : qk_gain.shape[0], 2].set(grad_qk_gain.reshape(links[0], -1))
    small = small.reshape(links[0], 2, -1, 128)
    own_front = jnp.concatenate([front_own, lax.dynamic_slice_in_dim(small, core, 1, 1)[:, 0]], axis=2)
    other_front = jnp.concatenate(
        [front_other, lax.dynamic_slice_in_dim(small, 1 - core, 1, 1)[:, 0]], axis=2
    )
    front_sent = rep_swap(other_front.astype(jnp.bfloat16), 1)
    front_part = combine(own_front, front_sent)
    front_part, mixed_act = sync((front_part, mixed_act), out_back, up_back, gate_back)
    front_back = Flow(scatter_steps(links, front_part))
    result = live_rows * (hidden + matmul_plain(mixed_act, full_down))
    grad_inputs, result = sync((grad_inputs, result), up_back, gate_back, out_back, front_back)
    front_share = join_rows(front_back.finish())
    share_query = front_share[:, : HQ * HD]
    share_key = front_share[:, HQ * HD : (HQ + HK) * HD]
    share_value = front_share[:, (HQ + HK) * HD : (HQ + 2 * HK) * HD]
    extras = front_share[:, (HQ + 2 * HK) * HD :]
    share_again = extras[:, 0]
    share_fgain = extras[:, 1]
    share_qk = extras[: qk_gain.shape[0], 2]
    share_out = join_rows(out_back.finish())
    share_gate = join_rows(gate_back.finish())
    share_up = join_rows(up_back.finish())
    share_down = join_columns(down_back.finish())
    return (
        result.astype(jnp.bfloat16),
        grad_inputs.astype(jnp.bfloat16),
        share_again,
        share_query,
        share_key,
        share_value,
        share_qk,
        share_out,
        share_fgain,
        share_gate,
        share_up,
        share_down,
    )


def solution(mesh):
    return jax.shard_map(
        functools.partial(body, make_links(mesh)),
        mesh=mesh,
        in_specs=(
            P(("shard", "rep"), None),
            P(("shard", "rep"), None),
            P(("shard", "rep")),
            P("shard"),
            P("shard", None),
            P("shard", None),
            P("shard", None),
            P("shard"),
            P("shard", None),
            P("shard"),
            P("shard", None),
            P("shard", None),
            P("shard", None),
        ),
        out_specs=(
            P(("shard", "rep"), None),
            P(("shard", "rep"), None),
            P("shard"),
            P("shard", None),
            P("shard", None),
            P("shard", None),
            P("shard"),
            P("shard", None),
            P("shard"),
            P("shard", None),
            P("shard", None),
            P("shard", None),
        ),
        check_vma=False,
    )
```

```python
import functools
import math

import jax
import jax.numpy as jnp
from jax import lax
from jax.experimental import pallas as pl
from jax.experimental.pallas import tpu as pltpu
from jax.sharding import PartitionSpec as P

HQ = 16
HK = 8
HD = 64


norm_eps = 1e-05
rope_base = 1000000.0


def inv_rms(values):
    return lax.rsqrt(jnp.mean(values * values, axis=-1, keepdims=True) + norm_eps)


def rope_tables(positions):
    half_dim = HD // 2
    freq_index = jnp.arange(half_dim).astype(jnp.float32)
    freq_vals = jnp.power(rope_base, -(2.0 * freq_index) / HD)
    angles = positions[:, None] * freq_vals[None, :]
    return (jnp.cos(angles)[:, None, :], jnp.sin(angles)[:, None, :])


def rotate(values, cosine, sine_table):
    half_dim = HD // 2
    first_half = values[..., :half_dim]
    second_half = values[..., half_dim:]
    return jnp.concatenate(
        [
            first_half * cosine - second_half * sine_table,
            second_half * cosine + first_half * sine_table,
        ],
        axis=-1,
    )


def rotate_back(grad_vals, cosine, sine_table):
    half_dim = HD // 2
    first_half = grad_vals[..., :half_dim]
    second_half = grad_vals[..., half_dim:]
    return jnp.concatenate(
        [
            first_half * cosine + second_half * sine_table,
            second_half * cosine - first_half * sine_table,
        ],
        axis=-1,
    )


def norm_back(grad_out, inputs, scale_inv, gain_vec):
    weighted = grad_out * gain_vec
    row_inner = jnp.mean(weighted * inputs, axis=-1, keepdims=True)
    return scale_inv * weighted - inputs * (scale_inv * scale_inv * scale_inv) * row_inner


def matmul_plain(left_mat, right_mat):
    return jnp.dot(left_mat, right_mat, preferred_element_type=jnp.float32)


def matmul_rows(left_mat, right_mat):
    return lax.dot_general(
        left_mat, right_mat, (((0,), (0,)), ((), ())), preferred_element_type=jnp.float32
    )


def matmul_cols(left_mat, right_mat):
    return lax.dot_general(
        left_mat, right_mat, (((1,), (1,)), ((), ())), preferred_element_type=jnp.float32
    )


def make_links(mesh):
    shard_size, rep_size = mesh.shape["shard"], mesh.shape["rep"]
    axes = ("shard", "rep")

    def shard_swap(value, bit):
        pairs = [
            (s * rep_size + r, (s ^ bit) * rep_size + r)
            for s in range(shard_size)
            for r in range(rep_size)
        ]
        return lax.ppermute(value, axes, pairs)

    def rep_swap(value, bit):
        pairs = [
            (s * rep_size + r, s * rep_size + (r ^ bit))
            for s in range(shard_size)
            for r in range(rep_size)
        ]
        return lax.ppermute(value, axes, pairs)

    return shard_size, rep_size, shard_swap, rep_swap


def add_low(left, right):
    return (left.astype(jnp.float32) + right.astype(jnp.float32)).astype(jnp.bfloat16)


def pin(values, *waits):
    return lax.optimization_barrier((values, waits))[0]


class Flow:
    def __init__(self, steps):
        self.steps = steps
        self.result = None
        self.pending = next(steps)

    def resume(self, arrived):
        try:
            self.pending = self.steps.send(arrived)
        except StopIteration as stop:
            self.pending = ()
            self.steps = None
            self.result = stop.value

    def finish(self):
        while self.steps is not None:
            self.resume(self.pending)
        return self.result


def sync(values, *flows):
    flows = [flow for flow in flows if flow.steps is not None]
    values, arrived = lax.optimization_barrier((values, [flow.pending for flow in flows]))
    for flow, got in zip(flows, arrived):
        flow.resume(got)
    return values


def place_kernel(spots_ref, *refs):
    del spots_ref
    out_ref = refs[-1]
    for at in range(len(refs) - 1):

        @pl.when(pl.program_id(0) == at)
        def _():
            out_ref[...] = refs[at][...]


def place_blocks(gathered):
    blocks, spots = gathered
    rows, width = blocks[1].shape
    count = len(blocks) + 1
    return pl.pallas_call(
        place_kernel,
        out_shape=jax.ShapeDtypeStruct((count * rows, width), blocks[0].dtype),
        grid_spec=pltpu.PrefetchScalarGridSpec(
            num_scalar_prefetch=1,
            grid=(count,),
            in_specs=[
                pl.BlockSpec((rows, width), lambda i, spot, at=at: (at, 0))
                for at in (0, 1) + (0,) * (count - 2)
            ],
            out_specs=pl.BlockSpec((rows, width), lambda i, spot: (spot[i], 0)),
        ),
        cost_estimate=pl.CostEstimate(
            flops=0, bytes_accessed=4 * count * rows * width, transcendentals=0
        ),
        compiler_params=pltpu.CompilerParams(vmem_limit_bytes=60 << 20),
        name="place_blocks",
    )(spots, blocks[0], *blocks)


FF_TILE = 512


def block_specs(count, rows):
    return [
        pl.BlockSpec((rows, FF_TILE), lambda i, spot, at=at: (at, i))
        for at in (0, 1) + (0,) * (count - 2)
    ]


def settle(spots_ref, refs, whole_ref):
    rows = refs[0].shape[0]
    for at, ref in enumerate(refs):
        begin = pl.multiple_of(spots_ref[at] * rows, rows)
        whole_ref[pl.ds(begin, rows), :] = ref[...]


def ffn_forward_kernel(count, spots_ref, a_ref, *refs):
    gate_refs, up_refs = refs[:count], refs[count : 2 * count]
    z_ref, act_ref, slope_ref, gate_whole, up_whole = refs[2 * count :]
    settle(spots_ref, gate_refs, gate_whole)
    settle(spots_ref, up_refs, up_whole)
    step = min(256, a_ref.shape[0])
    for begin in range(0, a_ref.shape[0], step):
        rows = slice(begin, begin + step)
        gate = jnp.dot(a_ref[rows], gate_whole[...], preferred_element_type=jnp.float32)
        up = jnp.dot(a_ref[rows], up_whole[...], preferred_element_type=jnp.float32)
        sig = jax.nn.sigmoid(gate)
        act = gate * sig
        z_ref[rows] = (act * up).astype(jnp.bfloat16)
        act_ref[rows] = act.astype(jnp.bfloat16)
        slope_ref[rows] = (up * (sig + act * (1.0 - sig))).astype(jnp.bfloat16)


def ffn_forward(normed, gate, up):
    rows, depth = normed.shape
    (gate_blocks, spots), (up_blocks, _) = gate, up
    count = len(gate_blocks) + 1
    hidden = gate_blocks[0].shape[1]
    part = gate_blocks[1].shape[0]
    out = jax.ShapeDtypeStruct((rows, hidden), jnp.bfloat16)
    return pl.pallas_call(
        functools.partial(ffn_forward_kernel, count),
        out_shape=(out, out, out),
        grid_spec=pltpu.PrefetchScalarGridSpec(
            num_scalar_prefetch=1,
            grid=(hidden // FF_TILE,),
            in_specs=[pl.BlockSpec((rows, depth), lambda i, spot: (0, 0))]
            + block_specs(count, part) * 2,
            out_specs=[pl.BlockSpec((rows, FF_TILE), lambda i, spot: (0, i))] * 3,
            scratch_shapes=[pltpu.VMEM((depth, FF_TILE), jnp.bfloat16)] * 2,
        ),
        cost_estimate=pl.CostEstimate(
            flops=4 * rows * depth * hidden,
            bytes_accessed=4 * depth * hidden + 6 * rows * hidden,
            transcendentals=rows * hidden,
        ),
        compiler_params=pltpu.CompilerParams(vmem_limit_bytes=60 << 20),
        name="ffn_forward",
    )(spots, normed, gate_blocks[0], *gate_blocks, up_blocks[0], *up_blocks)


def ffn_inner_kernel(g_ref, down_ref, act_ref, slope_ref, dgate_ref, dup_ref):
    step = min(256, g_ref.shape[0])
    for begin in range(0, g_ref.shape[0], step):
        rows = slice(begin, begin + step)
        mixed = nt_dot(g_ref[rows], down_ref[...])
        dgate_ref[rows] = (mixed * slope_ref[rows].astype(jnp.float32)).astype(jnp.bfloat16)
        dup_ref[rows] = (mixed * act_ref[rows].astype(jnp.float32)).astype(jnp.bfloat16)


def ffn_inner(grad_low, down, act, slope):
    rows, depth = grad_low.shape
    hidden = down.shape[0]
    out = jax.ShapeDtypeStruct((rows, hidden), jnp.bfloat16)
    tile = pl.BlockSpec((rows, FF_TILE), lambda i: (0, i))
    return pl.pallas_call(
        ffn_inner_kernel,
        out_shape=(out, out),
        grid=(hidden // FF_TILE,),
        in_specs=[
            pl.BlockSpec((rows, depth), lambda i: (0, 0)),
            pl.BlockSpec((FF_TILE, depth), lambda i: (i, 0)),
            tile,
            tile,
        ],
        out_specs=[tile, tile],
        cost_estimate=pl.CostEstimate(
            flops=2 * rows * depth * hidden,
            bytes_accessed=2 * depth * hidden + 8 * rows * hidden,
            transcendentals=0,
        ),
        compiler_params=pltpu.CompilerParams(vmem_limit_bytes=60 << 20),
        name="ffn_inner",
    )(grad_low, down, act, slope)


def ffn_input_kernel(count, spots_ref, dgate_ref, dup_ref, *refs):
    gate_refs, up_refs = refs[:count], refs[count : 2 * count]
    out_ref, gate_whole, up_whole = refs[2 * count :]
    settle(spots_ref, gate_refs, gate_whole)
    settle(spots_ref, up_refs, up_whole)

    @pl.when(pl.program_id(0) == 0)
    def _():
        out_ref[...] = jnp.zeros_like(out_ref)

    step = min(256, dgate_ref.shape[0])
    for begin in range(0, dgate_ref.shape[0], step):
        rows = slice(begin, begin + step)
        out_ref[rows] += nt_dot(dgate_ref[rows], gate_whole[...]) + nt_dot(
            dup_ref[rows], up_whole[...]
        )


def ffn_input(grad_gate, grad_up, gate, up):
    rows, hidden = grad_gate.shape
    (gate_blocks, spots), (up_blocks, _) = gate, up
    count = len(gate_blocks) + 1
    part = gate_blocks[1].shape[0]
    depth = count * part
    tile = pl.BlockSpec((rows, FF_TILE), lambda i, spot: (0, i))
    return pl.pallas_call(
        functools.partial(ffn_input_kernel, count),
        out_shape=jax.ShapeDtypeStruct((rows, depth), jnp.float32),
        grid_spec=pltpu.PrefetchScalarGridSpec(
            num_scalar_prefetch=1,
            grid=(hidden // FF_TILE,),
            in_specs=[tile, tile] + block_specs(count, part) * 2,
            out_specs=pl.BlockSpec((rows, depth), lambda i, spot: (0, 0)),
            scratch_shapes=[pltpu.VMEM((depth, FF_TILE), jnp.bfloat16)] * 2,
        ),
        cost_estimate=pl.CostEstimate(
            flops=4 * rows * depth * hidden,
            bytes_accessed=4 * depth * hidden + 4 * rows * hidden,
            transcendentals=0,
        ),
        compiler_params=pltpu.CompilerParams(vmem_limit_bytes=60 << 20),
        name="ffn_input",
    )(spots, grad_gate, grad_up, gate_blocks[0], *gate_blocks, up_blocks[0], *up_blocks)


def gather_steps(links, mine, whole):
    shard_size, rep_size, shard_swap, rep_swap = links
    me = lax.axis_index("shard")
    core = lax.rem(lax.axis_index("rep"), 2)
    half, width = mine.shape
    quarter = half // 2
    pieces, others = {}, {}
    if shard_size == 4:
        pieces[1] = shard_swap(mine, 1)
        pieces[2] = shard_swap(mine, 2)
        pieces[1], pieces[2] = yield (pieces[1], pieces[2])
        corner_a = shard_swap(pieces[1][:quarter], 2)
        corner_b = shard_swap(pieces[2][quarter:], 1)
        others[1] = rep_swap(pieces[1], 1)
        others[2] = rep_swap(pieces[2], 1)
        corner_a, corner_b, others[1], others[2] = yield (
            corner_a, corner_b, others[1], others[2]
        )
        pieces[3] = jnp.concatenate([corner_a, corner_b], axis=0)
        others[3] = rep_swap(pieces[3], 1)
        (others[3],) = yield (others[3],)
    else:
        pieces[0] = mine
        bit = 1
        while bit < shard_size:
            order = sorted(pieces)
            got = shard_swap(jnp.stack([pieces[d] for d in order]), bit)
            (got,) = yield (got,)
            for at, d in enumerate(order):
                pieces[d ^ bit] = got[at]
            bit *= 2
        del pieces[0]
        others = {d: rep_swap(piece, 1) for d, piece in pieces.items()}
    blocks, spots = [whole], [2 * me, 2 * me + 1]
    for d in pieces:
        blocks += [pieces[d], others[d]]
        spots += [2 * (me ^ d) + core, 2 * (me ^ d) + 1 - core]
    return blocks, jnp.stack(spots).astype(jnp.int32)


def core_half(weight):
    core = lax.rem(lax.axis_index("rep"), 2)
    half = weight.shape[0] // 2
    return lax.dynamic_slice_in_dim(weight, core * half, half, 0)


def pick_columns(links, value):
    core = lax.rem(lax.axis_index("rep"), 2)
    width = value.shape[1] // links[0] // 2

    def half(which):
        return jnp.concatenate(
            [
                lax.dynamic_slice_in_dim(value, (2 * d + which) * width, width, 1)
                for d in range(links[0])
            ],
            axis=1,
        )

    return half(core), half(1 - core)


def blocked(links, product):
    return product.reshape(links[0], -1, product.shape[1])


def scatter_steps(links, own, received):
    shard_size, rep_size, shard_swap, rep_swap = links
    me = lax.axis_index("shard")
    rep = lax.axis_index("rep")
    rows = own.shape[1] // 2

    def piece(d, at):
        begin, extent = (me ^ d, at * rows, 0), (1, rows, own.shape[2])
        return add_low(
            lax.dynamic_slice(own, begin, extent)[0],
            lax.dynamic_slice(received, begin, extent)[0],
        )

    if shard_size == 4:
        got_a = shard_swap(jnp.stack([piece(1, 0), piece(3, 0)]), 1)
        got_b = shard_swap(jnp.stack([piece(2, 1), piece(3, 1)]), 2)
        got_a, got_b = yield (got_a, got_b)
        pass_a = shard_swap(add_low(piece(2, 0), got_a[1]), 2)
        pass_b = shard_swap(add_low(piece(1, 1), got_b[1]), 1)
        pass_a, pass_b = yield (pass_a, pass_b)
        sum_a = add_low(piece(0, 0).astype(jnp.float32) + got_a[0].astype(jnp.float32), pass_a)
        sum_b = add_low(piece(0, 1).astype(jnp.float32) + got_b[0].astype(jnp.float32), pass_b)
        halves = [sum_a, sum_b]
    else:
        held = {d: jnp.stack([piece(d, 0), piece(d, 1)]) for d in range(shard_size)}
        bit = shard_size // 2
        while bit:
            sent = [d for d in sorted(held) if d & bit]
            got = shard_swap(jnp.stack([held[d] for d in sent]), bit)
            (got,) = yield (got,)
            held = {d ^ bit: add_low(held[d ^ bit], got[at]) for at, d in enumerate(sent)}
            bit //= 2
        halves = [held[0][0], held[0][1]]
    upper = lax.rem(rep // 2, 2) == 1
    if rep_size >= 8:
        keep = jnp.where(upper, halves[1], halves[0])
        send = jnp.where(upper, halves[0], halves[1])
        got = rep_swap(send, 2)
        (got,) = yield (got,)
        keep = add_low(keep, got)
        bit = 4
        while bit < rep_size:
            got = rep_swap(keep, bit)
            (got,) = yield (got,)
            keep = add_low(keep, got)
            bit *= 2
        back = rep_swap(keep, 2)
        (back,) = yield (back,)
        halves = [jnp.where(upper, back, keep), jnp.where(upper, keep, back)]
        half = jnp.concatenate(halves, axis=0)
    else:
        half = jnp.concatenate(halves, axis=0)
        bit = 2
        while bit < rep_size:
            half = add_low(half, rep_swap(half, bit))
            bit *= 2
    other = rep_swap(half, 1)
    (other,) = yield (other,)
    return half, other


def join_rows(pair):
    core = lax.rem(lax.axis_index("rep"), 2)
    half, other = pair
    return jnp.where(
        core == 0,
        jnp.concatenate([half, other], axis=0),
        jnp.concatenate([other, half], axis=0),
    ).astype(jnp.float32)


def join_columns(pair):
    core = lax.rem(lax.axis_index("rep"), 2)
    half, other = pair
    return jnp.where(
        core == 0,
        jnp.concatenate([half, other], axis=1),
        jnp.concatenate([other, half], axis=1),
    ).astype(jnp.float32)


BLOCK = 256
LOOK = 3


def nt_dot(left_mat, right_mat):
    return lax.dot_general(
        left_mat, right_mat, (((1,), (1,)), ((), ())), preferred_element_type=jnp.float32
    )


def attend_kernel(live_ref, q_ref, k_ref, v_ref, seg_col_ref, seg_row_ref, o_ref, acc_ref):
    at = pl.program_id(1)
    acc_ref[...] = jnp.zeros_like(acc_ref)
    lane = lax.broadcasted_iota(jnp.int32, (BLOCK, 2 * HD), 1)
    low_lane = lane < HD
    for back in range(LOOK):
        key_block = jnp.maximum(at - back, 0)

        @pl.when((at >= back) & (live_ref[at, key_block] > 0))
        def _():
            begin = pl.multiple_of(key_block * BLOCK, BLOCK)
            same = seg_col_ref[...] == seg_row_ref[:, pl.ds(begin, BLOCK)]
            if back == 0:
                row = lax.broadcasted_iota(jnp.int32, (BLOCK, BLOCK), 0)
                col = lax.broadcasted_iota(jnp.int32, (BLOCK, BLOCK), 1)
                same = same & (col <= row)
            mask = same.astype(jnp.float32)
            keys = k_ref[pl.ds(begin, BLOCK), :]
            values = v_ref[pl.ds(begin, BLOCK), :]
            swapped = pltpu.roll(values.astype(jnp.float32), HD, 1).astype(jnp.bfloat16)
            one = jnp.ones_like(values)
            for head in range(4):
                group, odd = head // 2, head % 2
                scores = nt_dot(
                    q_ref[:, head * HD : (head + 1) * HD], keys[:, group * HD : (group + 1) * HD]
                )
                weights = (jnp.exp(scores) * mask).astype(jnp.bfloat16)
                held = values if group == odd else swapped
                padded = jnp.where(low_lane, held, one) if odd == 0 else jnp.where(low_lane, one, held)
                acc_ref[head] += jnp.dot(weights, padded, preferred_element_type=jnp.float32)

    for group in range(2):
        even, odd = acc_ref[2 * group], acc_ref[2 * group + 1]
        top = jnp.where(low_lane, even, odd)
        total = pltpu.roll(jnp.where(low_lane, odd, even), HD, 1)
        o_ref[:, group * 2 * HD : (group + 1) * 2 * HD] = (top / total).astype(o_ref.dtype)


def attend_back_kernel(
    live_ref, q_ref, do_ref, k_ref, v_ref, seg_col_ref, seg_row_ref,
    dq_ref, dk_ref, dv_ref, exp_ref, dp_ref, total_ref, inner_ref, dqt_ref,
):
    at = pl.program_id(1)

    @pl.when(at == 0)
    def _():
        dk_ref[...] = jnp.zeros_like(dk_ref)
        dv_ref[...] = jnp.zeros_like(dv_ref)

    total_ref[...] = jnp.zeros_like(total_ref)
    inner_ref[...] = jnp.zeros_like(inner_ref)
    dqt_ref[...] = jnp.zeros_like(dqt_ref)

    def each_block(run):
        for back in range(LOOK):
            key_block = jnp.maximum(at - back, 0)

            @pl.when((at >= back) & (live_ref[at, key_block] > 0))
            def _():
                run(back, pl.multiple_of(key_block * BLOCK, BLOCK))

    def first(back, begin):
        same = seg_col_ref[pl.ds(begin, BLOCK), :] == seg_row_ref[...]
        if back == 0:
            row = lax.broadcasted_iota(jnp.int32, (BLOCK, BLOCK), 0)
            col = lax.broadcasted_iota(jnp.int32, (BLOCK, BLOCK), 1)
            same = same & (row <= col)
        mask = same.astype(jnp.float32)
        keys = k_ref[pl.ds(begin, BLOCK), :]
        values = v_ref[pl.ds(begin, BLOCK), :]
        for head in range(4):
            group = head // 2
            cols = slice(head * HD, (head + 1) * HD)
            kept = slice(group * HD, (group + 1) * HD)
            weights = jnp.exp(nt_dot(keys[:, kept], q_ref[:, cols])) * mask
            grads = nt_dot(values[:, kept], do_ref[:, cols])
            exp_ref[head, back] = weights
            dp_ref[head, back] = grads
            total_ref[head : head + 1] += jnp.sum(weights, axis=0, keepdims=True)
            inner_ref[head : head + 1] += jnp.sum(weights * grads, axis=0, keepdims=True)

    def second(back, begin):
        keys = k_ref[pl.ds(begin, BLOCK), :]
        dk_parts, dv_parts = [], []
        for group in range(2):
            dk_sum, dv_sum = None, None
            for head in (2 * group, 2 * group + 1):
                cols = slice(head * HD, (head + 1) * HD)
                scale = 1.0 / total_ref[head : head + 1]
                probs = exp_ref[head, back] * scale
                inner = inner_ref[head : head + 1] * scale
                low_scores = (probs * (dp_ref[head, back] - inner)).astype(jnp.bfloat16)
                dv_part = jnp.dot(
                    probs.astype(jnp.bfloat16), do_ref[:, cols], preferred_element_type=jnp.float32
                )
                dk_part = jnp.dot(low_scores, q_ref[:, cols], preferred_element_type=jnp.float32)
                dqt_ref[cols] += lax.dot_general(
                    keys[:, group * HD : (group + 1) * HD],
                    low_scores,
                    (((0,), (0,)), ((), ())),
                    preferred_element_type=jnp.float32,
                )
                dk_sum = dk_part if dk_sum is None else dk_sum + dk_part
                dv_sum = dv_part if dv_sum is None else dv_sum + dv_part
            dk_parts.append(dk_sum)
            dv_parts.append(dv_sum)
        dk_ref[pl.ds(begin, BLOCK), :] += jnp.concatenate(dk_parts, axis=1)
        dv_ref[pl.ds(begin, BLOCK), :] += jnp.concatenate(dv_parts, axis=1)

    each_block(first)
    each_block(second)
    dq_ref[...] = dqt_ref[...].T


def live_blocks(segment):
    count = segment.shape[0] // BLOCK
    blocks = segment.reshape(count, BLOCK)
    index = jnp.arange(count)
    return (
        (blocks[:, :1] == blocks[:, -1][None, :]) | (index[:, None] == index[None, :])
    ).astype(jnp.int32)


def attend(query, key, value, segment):
    rows = query.shape[0]
    panels, count = HK // 2, rows // BLOCK
    return pl.pallas_call(
        attend_kernel,
        out_shape=jax.ShapeDtypeStruct((rows, HQ * HD), jnp.bfloat16),
        grid_spec=pltpu.PrefetchScalarGridSpec(
            num_scalar_prefetch=1,
            grid=(panels, count),
            in_specs=[
                pl.BlockSpec((BLOCK, 4 * HD), lambda p, i, live: (i, p)),
                pl.BlockSpec((rows, 2 * HD), lambda p, i, live: (0, p)),
                pl.BlockSpec((rows, 2 * HD), lambda p, i, live: (0, p)),
                pl.BlockSpec((BLOCK, 1), lambda p, i, live: (i, 0)),
                pl.BlockSpec((1, rows), lambda p, i, live: (0, 0)),
            ],
            out_specs=pl.BlockSpec((BLOCK, 4 * HD), lambda p, i, live: (i, p)),
            scratch_shapes=[pltpu.VMEM((4, BLOCK, 2 * HD), jnp.float32)],
        ),
        cost_estimate=pl.CostEstimate(
            flops=24 * rows * BLOCK * LOOK * HQ * HD,
            bytes_accessed=8 * rows * HQ * HD,
            transcendentals=rows * BLOCK * LOOK * HQ,
        ),
        name="attend",
    )(live_blocks(segment), query, key, value, segment[:, None], segment[None, :])


def attend_back(query, grad_out, key, value, segment, start, panels):
    rows = query.shape[0]
    count = rows // BLOCK
    return pl.pallas_call(
        attend_back_kernel,
        out_shape=(
            jax.ShapeDtypeStruct((rows, panels * 4 * HD), jnp.float32),
            jax.ShapeDtypeStruct((rows, panels * 2 * HD), jnp.float32),
            jax.ShapeDtypeStruct((rows, panels * 2 * HD), jnp.float32),
        ),
        grid_spec=pltpu.PrefetchScalarGridSpec(
            num_scalar_prefetch=1,
            grid=(panels, count),
            in_specs=[
                pl.BlockSpec((BLOCK, 4 * HD), lambda p, i, live: (i, start + p)),
                pl.BlockSpec((BLOCK, 4 * HD), lambda p, i, live: (i, start + p)),
                pl.BlockSpec((rows, 2 * HD), lambda p, i, live: (0, start + p)),
                pl.BlockSpec((rows, 2 * HD), lambda p, i, live: (0, start + p)),
                pl.BlockSpec((rows, 1), lambda p, i, live: (0, 0)),
                pl.BlockSpec((1, BLOCK), lambda p, i, live: (0, i)),
            ],
            out_specs=[
                pl.BlockSpec((BLOCK, 4 * HD), lambda p, i, live: (i, p)),
                pl.BlockSpec((rows, 2 * HD), lambda p, i, live: (0, p)),
                pl.BlockSpec((rows, 2 * HD), lambda p, i, live: (0, p)),
            ],
            scratch_shapes=[
                pltpu.VMEM((4, LOOK, BLOCK, BLOCK), jnp.float32),
                pltpu.VMEM((4, LOOK, BLOCK, BLOCK), jnp.float32),
                pltpu.VMEM((8, BLOCK), jnp.float32),
                pltpu.VMEM((8, BLOCK), jnp.float32),
                pltpu.VMEM((4 * HD, BLOCK), jnp.float32),
            ],
        ),
        cost_estimate=pl.CostEstimate(
            flops=160 * rows * BLOCK * LOOK * HD * panels,
            bytes_accessed=64 * rows * HD * panels,
            transcendentals=4 * rows * BLOCK * LOOK * panels,
        ),
        name="attend_back",
    )(live_blocks(segment), query, grad_out, key, value, segment[:, None], segment[None, :])


def body(
    links,
    tokens,
    cotangent,
    segment,
    attn_gain,
    w_query,
    w_key,
    w_value,
    qk_gain,
    w_out,
    ffn_gain,
    w_gate,
    w_up,
    w_down,
):
    row_count = tokens.shape[0]
    rep_swap = links[3]
    core = lax.rem(lax.axis_index("rep"), 2)
    score_scale = 1.0 / math.sqrt(HD)
    spare = jnp.zeros((attn_gain.shape[0] - qk_gain.shape[0],), jnp.bfloat16)
    packed = jnp.stack([attn_gain, ffn_gain, jnp.concatenate([qk_gain, spare])], axis=1)
    packed = jnp.pad(packed, ((0, 0), (0, 125)))
    attn_weights = (w_query, w_key, w_value, packed)
    front_flow = Flow(
        gather_steps(
            links,
            jnp.concatenate([core_half(weight) for weight in attn_weights], axis=1),
            jnp.concatenate(attn_weights, axis=1),
        )
    )
    w_out, w_gate, w_up, w_down = sync((w_out, w_gate, w_up, w_down), front_flow)
    out_flow = Flow(gather_steps(links, core_half(w_out), w_out))
    w_gate, w_up, w_down = sync((w_gate, w_up, w_down), front_flow, out_flow)
    gate_flow = Flow(gather_steps(links, core_half(w_gate), w_gate))
    w_up, w_down = sync((w_up, w_down), front_flow)
    up_flow = Flow(gather_steps(links, core_half(w_up), w_up))
    front = place_blocks(front_flow.finish())
    full_query = front[:, : HQ * HD]
    full_key = front[:, HQ * HD : (HQ + HK) * HD]
    full_value = front[:, (HQ + HK) * HD : (HQ + 2 * HK) * HD]
    gains = front[:, (HQ + 2 * HK) * HD :]
    full_attn_gain = gains[:, 0]
    full_ffn_gain = gains[:, 1]
    full_qk_gain = gains.reshape(links[0], -1, 128)[:, : qk_gain.shape[0], 2].reshape(-1)
    inputs = tokens.astype(jnp.float32)
    token_index = jnp.arange(row_count)
    same_seq = segment[:, None] == segment[None, :]
    allowed = same_seq & (token_index[None, :] <= token_index[:, None])
    positions = jnp.sum(
        (same_seq & (token_index[None, :] < token_index[:, None])).astype(jnp.float32), axis=1
    )
    live_rows = (segment >= 0).astype(jnp.float32)[:, None]
    cosine, sine_table = rope_tables(positions)
    scale_one = inv_rms(inputs)
    normed = (inputs * scale_one * full_attn_gain.astype(jnp.float32)).astype(jnp.bfloat16)
    query_lin = matmul_plain(normed, full_query).reshape(row_count, HQ, HD)
    key_lin = matmul_plain(normed, full_key).reshape(row_count, HK, HD)
    value_low = matmul_plain(normed, full_value).astype(jnp.bfloat16).reshape(row_count, HK, HD)
    qk_gains = full_qk_gain.astype(jnp.float32)
    query_scale = inv_rms(query_lin)
    key_scale = inv_rms(key_lin)
    query_rot = (
        rotate(query_lin * query_scale * qk_gains[:HD], cosine, sine_table)
        .astype(jnp.bfloat16)
    )
    key_rot = rotate(key_lin * key_scale * qk_gains[HD:], cosine, sine_table).astype(jnp.bfloat16)

    query_rot = (query_rot.astype(jnp.float32) * score_scale).astype(jnp.bfloat16)
    query_rot = query_rot.reshape(row_count, HQ * HD)
    key_rot = key_rot.reshape(row_count, HK * HD)
    value_low = value_low.reshape(row_count, HK * HD)
    query_rot, key_rot, value_low, w_down = sync(
        (query_rot, key_rot, value_low, w_down), out_flow, gate_flow, up_flow
    )
    down_flow = Flow(gather_steps(links, core_half(w_down), w_down))
    attn_low = attend(query_rot, key_rot, value_low, segment)
    attn_low = sync(attn_low, out_flow)
    full_out = place_blocks(out_flow.finish())
    hidden = inputs + matmul_plain(attn_low, full_out)
    scale_two = inv_rms(hidden)
    normed_ffn = (hidden * scale_two * full_ffn_gain.astype(jnp.float32)).astype(jnp.bfloat16)
    normed_ffn, hidden = sync((normed_ffn, hidden), gate_flow, up_flow)
    normed_ffn = sync(normed_ffn, gate_flow, up_flow, down_flow)
    full_gate = gate_flow.finish()
    full_up = up_flow.finish()
    mixed_act, act_low, slope = ffn_forward(normed_ffn, full_gate, full_up)
    mixed_act, slope, act_low = sync((mixed_act, slope, act_low), down_flow)
    mixed_act, slope, act_low = sync((mixed_act, slope, act_low), down_flow)
    full_down = place_blocks(down_flow.finish())
    out_grad = live_rows * cotangent.astype(jnp.float32)
    out_low = out_grad.astype(jnp.bfloat16)
    grad_gate_low, grad_up_low = ffn_inner(out_low, full_down, act_low, slope)
    half = out_low.shape[1] // 2
    out_own = lax.dynamic_slice_in_dim(out_low, core * half, half, 1)
    out_other = lax.dynamic_slice_in_dim(out_low, (1 - core) * half, half, 1)
    normed_own, normed_other = pick_columns(links, normed_ffn)
    grad_up_low, grad_gate_low, out_own, out_other, mixed_act = pin(
        (grad_up_low, grad_gate_low, out_own, out_other, mixed_act)
    )

    def hand(product):
        return rep_swap(blocked(links, product).astype(jnp.bfloat16), 1)

    down_sent = hand(matmul_rows(mixed_act, out_other))
    gate_given = matmul_rows(normed_other, pin(grad_gate_low, down_sent)).astype(jnp.bfloat16)
    gate_sent = hand(gate_given)
    down_sent, mixed_act, grad_up_low, gate_given = pin(
        (down_sent, mixed_act, grad_up_low, gate_given)
    )
    down_given = blocked(links, matmul_rows(mixed_act, out_own).astype(jnp.bfloat16))
    down_back = Flow(scatter_steps(links, *pin((down_given, down_sent))))
    grad_up_low, grad_gate_low, normed_own, normed_other = pin(
        (grad_up_low, grad_gate_low, normed_own, normed_other), down_given
    )
    up_sent = hand(matmul_rows(normed_other, grad_up_low))
    gate_given = blocked(links, matmul_rows(normed_own, grad_gate_low).astype(jnp.bfloat16))
    up_given = blocked(links, matmul_rows(normed_own, grad_up_low).astype(jnp.bfloat16))
    gate_given, gate_sent, up_given, up_sent, grad_gate_low, grad_up_low = sync(
        (gate_given, gate_sent, up_given, up_sent, grad_gate_low, grad_up_low), down_back
    )
    gate_back = Flow(scatter_steps(links, gate_given, gate_sent))
    grad_normed_ffn = ffn_input(grad_gate_low, grad_up_low, full_gate, full_up)
    grad_normed_ffn, up_given, up_sent = sync((grad_normed_ffn, up_given, up_sent), down_back)
    grad_ffn_gain = jnp.sum(grad_normed_ffn * hidden * scale_two, axis=0)
    grad_hidden = out_grad + norm_back(
        grad_normed_ffn, hidden, scale_two, full_ffn_gain.astype(jnp.float32)
    )
    hidden_low = grad_hidden.astype(jnp.bfloat16)
    grad_attn_low = matmul_cols(hidden_low, full_out).astype(jnp.bfloat16)
    attn_own, attn_other = pick_columns(links, attn_low)
    out_sent = hand(matmul_rows(attn_other, hidden_low))
    out_given = blocked(links, matmul_rows(attn_own, hidden_low).astype(jnp.bfloat16))
    panels = HK // 4
    grad_attn_low, out_given, out_sent, up_given, up_sent = sync(
        (grad_attn_low, out_given, out_sent, up_given, up_sent), gate_back, down_back
    )
    up_back = Flow(scatter_steps(links, up_given, up_sent))
    lower = attend_back(query_rot, grad_attn_low, key_rot, value_low, segment, 0, panels)
    grad_attn_low, lower = pin((grad_attn_low, lower))
    upper = attend_back(query_rot, grad_attn_low, key_rot, value_low, segment, panels, panels)
    lower, upper, out_given, out_sent = sync(
        (lower, upper, out_given, out_sent), gate_back, down_back
    )
    out_back = Flow(scatter_steps(links, out_given, out_sent))
    grad_query_rot, grad_key_rot, grad_value = (
        jnp.concatenate(pair, axis=1) for pair in zip(lower, upper)
    )
    grad_query_rot = (score_scale * grad_query_rot).reshape(row_count, HQ, HD)
    grad_key_rot = grad_key_rot.reshape(row_count, HK, HD)
    grad_query_norm = rotate_back(grad_query_rot, cosine, sine_table)
    grad_key_norm = rotate_back(grad_key_rot, cosine, sine_table)
    back_gains = full_qk_gain.astype(jnp.float32)
    grad_qk_gain = jnp.concatenate(
        [
            jnp.sum(grad_query_norm * query_lin * query_scale, axis=(0, 1)),
            jnp.sum(grad_key_norm * key_lin * key_scale, axis=(0, 1)),
        ]
    )
    grad_query_low = (
        norm_back(grad_query_norm, query_lin, query_scale, back_gains[:HD])
        .astype(jnp.bfloat16)
        .reshape(row_count, HQ * HD)
    )
    grad_key_low = (
        norm_back(grad_key_norm, key_lin, key_scale, back_gains[HD:])
        .astype(jnp.bfloat16)
        .reshape(row_count, HK * HD)
    )
    grad_value_low = grad_value.astype(jnp.bfloat16).reshape(row_count, HK * HD)
    normed_own, normed_other = pick_columns(links, normed)
    grad_front = jnp.concatenate([grad_query_low, grad_key_low, grad_value_low], axis=1)
    grad_front = sync(grad_front, up_back, gate_back, down_back, out_back)
    grad_query_low = grad_front[:, : HQ * HD]
    grad_key_low = grad_front[:, HQ * HD : (HQ + HK) * HD]
    grad_value_low = grad_front[:, (HQ + HK) * HD :]
    front_other = blocked(links, matmul_rows(normed_other, grad_front))
    front_own = blocked(links, matmul_rows(normed_own, grad_front))
    grad_normed = (
        matmul_cols(grad_query_low, full_query)
        + matmul_cols(grad_key_low, full_key)
        + matmul_cols(grad_value_low, full_value)
    )
    grad_attn_gain = jnp.sum(grad_normed * inputs * scale_one, axis=0)
    grad_inputs = grad_hidden + norm_back(
        grad_normed, inputs, scale_one, full_attn_gain.astype(jnp.float32)
    )
    qk_part = jnp.pad(
        grad_qk_gain.reshape(links[0], -1),
        ((0, 0), (0, attn_gain.shape[0] - qk_gain.shape[0])),
    )
    small = jnp.stack([grad_attn_gain, grad_ffn_gain, qk_part.reshape(-1)], axis=1)
    small = jnp.pad(small, ((0, 0), (0, 125)))
    small = small.reshape(links[0], 2, -1, 128)
    own_front = jnp.concatenate([front_own, lax.dynamic_slice_in_dim(small, core, 1, 1)[:, 0]], axis=2)
    other_front = jnp.concatenate(
        [front_other, lax.dynamic_slice_in_dim(small, 1 - core, 1, 1)[:, 0]], axis=2
    )
    front_sent = rep_swap(other_front.astype(jnp.bfloat16), 1)
    own_front = own_front.astype(jnp.bfloat16)
    own_front, front_sent, mixed_act = sync(
        (own_front, front_sent, mixed_act), out_back, up_back, gate_back
    )
    front_back = Flow(scatter_steps(links, own_front, front_sent))
    result = live_rows * (hidden + matmul_plain(mixed_act, full_down))
    grad_inputs, result = sync((grad_inputs, result), up_back, gate_back, out_back, front_back)
    front_share = join_rows(front_back.finish())
    share_query = front_share[:, : HQ * HD]
    share_key = front_share[:, HQ * HD : (HQ + HK) * HD]
    share_value = front_share[:, (HQ + HK) * HD : (HQ + 2 * HK) * HD]
    extras = front_share[:, (HQ + 2 * HK) * HD :]
    share_again = extras[:, 0]
    share_fgain = extras[:, 1]
    share_qk = extras[: qk_gain.shape[0], 2]
    share_out = join_rows(out_back.finish())
    share_gate = join_rows(gate_back.finish())
    share_up = join_rows(up_back.finish())
    share_down = join_columns(down_back.finish())
    return (
        result.astype(jnp.bfloat16),
        grad_inputs.astype(jnp.bfloat16),
        share_again,
        share_query,
        share_key,
        share_value,
        share_qk,
        share_out,
        share_fgain,
        share_gate,
        share_up,
        share_down,
    )


def solution(mesh):
    return jax.shard_map(
        functools.partial(body, make_links(mesh)),
        mesh=mesh,
        in_specs=(
            P(("shard", "rep"), None),
            P(("shard", "rep"), None),
            P(("shard", "rep")),
            P("shard"),
            P("shard", None),
            P("shard", None),
            P("shard", None),
            P("shard"),
            P("shard", None),
            P("shard"),
            P("shard", None),
            P("shard", None),
            P("shard", None),
        ),
        out_specs=(
            P(("shard", "rep"), None),
            P(("shard", "rep"), None),
            P("shard"),
            P("shard", None),
            P("shard", None),
            P("shard", None),
            P("shard"),
            P("shard", None),
            P("shard"),
            P("shard", None),
            P("shard", None),
            P("shard", None),
        ),
        check_vma=False,
    )
```

```python
import functools
import math

import jax
import jax.numpy as jnp
from jax import lax
from jax.experimental import pallas as pl
from jax.experimental.pallas import tpu as pltpu
from jax.sharding import PartitionSpec as P

HQ = 16
HK = 8
HD = 64


norm_eps = 1e-05
TINY = pl.CostEstimate(flops=1, bytes_accessed=1, transcendentals=0)
rope_base = 1000000.0


def inv_rms(values):
    return lax.rsqrt(jnp.mean(values * values, axis=-1, keepdims=True) + norm_eps)


def rope_tables(positions):
    half_dim = HD // 2
    freq_index = jnp.arange(half_dim).astype(jnp.float32)
    freq_vals = jnp.power(rope_base, -(2.0 * freq_index) / HD)
    angles = positions[:, None] * freq_vals[None, :]
    return (jnp.cos(angles)[:, None, :], jnp.sin(angles)[:, None, :])


def rotate(values, cosine, sine_table):
    half_dim = HD // 2
    first_half = values[..., :half_dim]
    second_half = values[..., half_dim:]
    return jnp.concatenate(
        [
            first_half * cosine - second_half * sine_table,
            second_half * cosine + first_half * sine_table,
        ],
        axis=-1,
    )


def rotate_back(grad_vals, cosine, sine_table):
    half_dim = HD // 2
    first_half = grad_vals[..., :half_dim]
    second_half = grad_vals[..., half_dim:]
    return jnp.concatenate(
        [
            first_half * cosine + second_half * sine_table,
            second_half * cosine - first_half * sine_table,
        ],
        axis=-1,
    )


def norm_back(grad_out, inputs, scale_inv, gain_vec):
    weighted = grad_out * gain_vec
    row_inner = jnp.mean(weighted * inputs, axis=-1, keepdims=True)
    return scale_inv * weighted - inputs * (scale_inv * scale_inv * scale_inv) * row_inner


def matmul_plain(left_mat, right_mat):
    return jnp.dot(left_mat, right_mat, preferred_element_type=jnp.float32)


def matmul_rows(left_mat, right_mat):
    return lax.dot_general(
        left_mat, right_mat, (((0,), (0,)), ((), ())), preferred_element_type=jnp.float32
    )


def matmul_cols(left_mat, right_mat):
    return lax.dot_general(
        left_mat, right_mat, (((1,), (1,)), ((), ())), preferred_element_type=jnp.float32
    )


def make_links(mesh):
    shard_size, rep_size = mesh.shape["shard"], mesh.shape["rep"]
    axes = ("shard", "rep")

    def shard_swap(value, bit):
        pairs = [
            (s * rep_size + r, (s ^ bit) * rep_size + r)
            for s in range(shard_size)
            for r in range(rep_size)
        ]
        return lax.ppermute(value, axes, pairs)

    def rep_swap(value, bit):
        pairs = [
            (s * rep_size + r, s * rep_size + (r ^ bit))
            for s in range(shard_size)
            for r in range(rep_size)
        ]
        return lax.ppermute(value, axes, pairs)

    return shard_size, rep_size, shard_swap, rep_swap


def add_low(left, right):
    return (left.astype(jnp.float32) + right.astype(jnp.float32)).astype(jnp.bfloat16)


def pin(values, *waits):
    return lax.optimization_barrier((values, waits))[0]


class Flow:
    def __init__(self, steps):
        self.steps = steps
        self.result = None
        self.pending = next(steps)

    def resume(self, arrived):
        try:
            self.pending = self.steps.send(arrived)
        except StopIteration as stop:
            self.pending = ()
            self.steps = None
            self.result = stop.value

    def finish(self):
        while self.steps is not None:
            self.resume(self.pending)
        return self.result


def sync(values, *flows):
    flows = [flow for flow in flows if flow.steps is not None]
    values, arrived = lax.optimization_barrier((values, [flow.pending for flow in flows]))
    for flow, got in zip(flows, arrived):
        flow.resume(got)
    return values


def place_kernel(spots_ref, *refs):
    del spots_ref
    out_ref = refs[-1]
    for at in range(len(refs) - 1):

        @pl.when(pl.program_id(0) == at)
        def _():
            out_ref[...] = refs[at][...]


def place_blocks(gathered):
    blocks, spots = gathered
    rows, width = blocks[1].shape
    count = len(blocks) + 1
    return pl.pallas_call(
        place_kernel,
        out_shape=jax.ShapeDtypeStruct((count * rows, width), blocks[0].dtype),
        grid_spec=pltpu.PrefetchScalarGridSpec(
            num_scalar_prefetch=1,
            grid=(count,),
            in_specs=[
                pl.BlockSpec((rows, width), lambda i, spot, at=at: (at, 0))
                for at in (0, 1) + (0,) * (count - 2)
            ],
            out_specs=pl.BlockSpec((rows, width), lambda i, spot: (spot[i], 0)),
        ),
        cost_estimate=TINY,
        compiler_params=pltpu.CompilerParams(vmem_limit_bytes=60 << 20),
        name="place_blocks",
    )(spots, blocks[0], *blocks)


FF_TILE = 512


def block_specs(count, rows, tiles):
    own = [
        pl.BlockSpec((rows, FF_TILE), lambda i, spot, at=at: (at, i)) for at in (0, 1)
    ]
    gate = [pl.BlockSpec((rows, FF_TILE), lambda i, spot: (0, i))] * (count - 2)
    up = [pl.BlockSpec((rows, FF_TILE), lambda i, spot: (0, i + tiles))] * (count - 2)
    return own + gate + own + up


def settle(spots_ref, refs, whole_ref):
    rows = refs[0].shape[0]
    for at, ref in enumerate(refs):
        begin = pl.multiple_of(spots_ref[at] * rows, rows)
        whole_ref[pl.ds(begin, rows), :] = ref[...]


def ffn_forward_kernel(count, spots_ref, a_ref, *refs):
    gate_refs, up_refs = refs[:count], refs[count : 2 * count]
    z_ref, act_ref, slope_ref, gate_whole, up_whole = refs[2 * count :]
    settle(spots_ref, gate_refs, gate_whole)
    settle(spots_ref, up_refs, up_whole)
    step = min(256, a_ref.shape[0])
    for begin in range(0, a_ref.shape[0], step):
        rows = slice(begin, begin + step)
        gate = jnp.dot(a_ref[rows], gate_whole[...], preferred_element_type=jnp.float32)
        up = jnp.dot(a_ref[rows], up_whole[...], preferred_element_type=jnp.float32)
        sig = jax.nn.sigmoid(gate)
        act = gate * sig
        z_ref[rows] = (act * up).astype(jnp.bfloat16)
        act_ref[rows] = act.astype(jnp.bfloat16)
        slope_ref[rows] = (up * (sig + act * (1.0 - sig))).astype(jnp.bfloat16)


def ffn_forward(normed, gate, up, gathered):
    rows, depth = normed.shape
    blocks, spots = gathered
    count = len(blocks) + 2
    hidden = gate.shape[1]
    part = gate.shape[0] // 2
    out = jax.ShapeDtypeStruct((rows, hidden), jnp.bfloat16)
    return pl.pallas_call(
        functools.partial(ffn_forward_kernel, count),
        out_shape=(out, out, out),
        grid_spec=pltpu.PrefetchScalarGridSpec(
            num_scalar_prefetch=1,
            grid=(hidden // FF_TILE,),
            in_specs=[pl.BlockSpec((rows, depth), lambda i, spot: (0, 0))]
            + block_specs(count, part, hidden // FF_TILE),
            out_specs=[pl.BlockSpec((rows, FF_TILE), lambda i, spot: (0, i))] * 3,
            scratch_shapes=[pltpu.VMEM((depth, FF_TILE), jnp.bfloat16)] * 2,
        ),
        cost_estimate=TINY,
        compiler_params=pltpu.CompilerParams(vmem_limit_bytes=60 << 20),
        name="ffn_forward",
    )(spots, normed, gate, gate, *blocks, up, up, *blocks)


def ffn_inner_kernel(g_ref, down_ref, act_ref, slope_ref, dgate_ref, dup_ref):
    step = min(256, g_ref.shape[0])
    for begin in range(0, g_ref.shape[0], step):
        rows = slice(begin, begin + step)
        mixed = nt_dot(g_ref[rows], down_ref[...])
        dgate_ref[rows] = (mixed * slope_ref[rows].astype(jnp.float32)).astype(jnp.bfloat16)
        dup_ref[rows] = (mixed * act_ref[rows].astype(jnp.float32)).astype(jnp.bfloat16)


def ffn_inner(grad_low, down, act, slope):
    rows, depth = grad_low.shape
    hidden = down.shape[0]
    out = jax.ShapeDtypeStruct((rows, hidden), jnp.bfloat16)
    tile = pl.BlockSpec((rows, FF_TILE), lambda i: (0, i))
    return pl.pallas_call(
        ffn_inner_kernel,
        out_shape=(out, out),
        grid=(hidden // FF_TILE,),
        in_specs=[
            pl.BlockSpec((rows, depth), lambda i: (0, 0)),
            pl.BlockSpec((FF_TILE, depth), lambda i: (i, 0)),
            tile,
            tile,
        ],
        out_specs=[tile, tile],
        cost_estimate=TINY,
        compiler_params=pltpu.CompilerParams(vmem_limit_bytes=60 << 20),
        name="ffn_inner",
    )(grad_low, down, act, slope)


def ffn_input_kernel(count, spots_ref, dgate_ref, dup_ref, *refs):
    gate_refs, up_refs = refs[:count], refs[count : 2 * count]
    out_ref, gate_whole, up_whole = refs[2 * count :]
    settle(spots_ref, gate_refs, gate_whole)
    settle(spots_ref, up_refs, up_whole)

    @pl.when(pl.program_id(0) == 0)
    def _():
        out_ref[...] = jnp.zeros_like(out_ref)

    step = min(256, dgate_ref.shape[0])
    for begin in range(0, dgate_ref.shape[0], step):
        rows = slice(begin, begin + step)
        out_ref[rows] += nt_dot(dgate_ref[rows], gate_whole[...]) + nt_dot(
            dup_ref[rows], up_whole[...]
        )


def ffn_input(grad_gate, grad_up, gate, up, gathered):
    rows, hidden = grad_gate.shape
    blocks, spots = gathered
    count = len(blocks) + 2
    part = gate.shape[0] // 2
    depth = count * part
    tile = pl.BlockSpec((rows, FF_TILE), lambda i, spot: (0, i))
    return pl.pallas_call(
        functools.partial(ffn_input_kernel, count),
        out_shape=jax.ShapeDtypeStruct((rows, depth), jnp.float32),
        grid_spec=pltpu.PrefetchScalarGridSpec(
            num_scalar_prefetch=1,
            grid=(hidden // FF_TILE,),
            in_specs=[tile, tile] + block_specs(count, part, hidden // FF_TILE),
            out_specs=pl.BlockSpec((rows, depth), lambda i, spot: (0, 0)),
            scratch_shapes=[pltpu.VMEM((depth, FF_TILE), jnp.bfloat16)] * 2,
        ),
        cost_estimate=TINY,
        compiler_params=pltpu.CompilerParams(vmem_limit_bytes=60 << 20),
        name="ffn_input",
    )(spots, grad_gate, grad_up, gate, gate, *blocks, up, up, *blocks)


def gather_steps(links, mine, whole, late=False):
    shard_size, rep_size, shard_swap, rep_swap = links
    me = lax.axis_index("shard")
    core = lax.rem(lax.axis_index("rep"), 2)
    half, width = mine.shape
    quarter = half // 2
    pieces, others = {}, {}
    if shard_size == 4:
        pieces[1] = shard_swap(mine, 1)
        pieces[2] = shard_swap(mine, 2)
        pieces[1], pieces[2] = yield (pieces[1], pieces[2])
        corner_a = shard_swap(pieces[1][:quarter], 2)
        corner_b = shard_swap(pieces[2][quarter:], 1)
        if late:
            early, waiting = (), (1, 2, 3)
            corner_a, corner_b, pieces[1], pieces[2] = yield (
                corner_a, corner_b, pieces[1], pieces[2]
            )
        else:
            early, waiting = (rep_swap(pieces[1], 1), rep_swap(pieces[2], 1)), (3,)
            corner_a, corner_b, *early = yield (corner_a, corner_b, *early)
        pieces[3] = jnp.concatenate([corner_a, corner_b], axis=0)
        rest = yield tuple(rep_swap(pieces[d], 1) for d in waiting)
        others = dict(zip((1, 2, 3), (*early, *rest)))
    else:
        pieces[0] = mine
        bit = 1
        while bit < shard_size:
            order = sorted(pieces)
            got = shard_swap(jnp.stack([pieces[d] for d in order]), bit)
            (got,) = yield (got,)
            for at, d in enumerate(order):
                pieces[d ^ bit] = got[at]
            bit *= 2
        del pieces[0]
        others = {d: rep_swap(piece, 1) for d, piece in pieces.items()}
    blocks, spots = [whole] if whole is not None else [], [2 * me, 2 * me + 1]
    for d in pieces:
        blocks += [pieces[d], others[d]]
        spots += [2 * (me ^ d) + core, 2 * (me ^ d) + 1 - core]
    return blocks, jnp.stack(spots).astype(jnp.int32)


def core_half(weight):
    core = lax.rem(lax.axis_index("rep"), 2)
    half = weight.shape[0] // 2
    return lax.dynamic_slice_in_dim(weight, core * half, half, 0)


def pick_columns(links, value):
    core = lax.rem(lax.axis_index("rep"), 2)
    width = value.shape[1] // links[0] // 2

    def half(which):
        return jnp.concatenate(
            [
                lax.dynamic_slice_in_dim(value, (2 * d + which) * width, width, 1)
                for d in range(links[0])
            ],
            axis=1,
        )

    return half(core), half(1 - core)


def blocked(links, product):
    return product.reshape(links[0], -1, product.shape[1])


def scatter_steps(links, own, received):
    shard_size, rep_size, shard_swap, rep_swap = links
    me = lax.axis_index("shard")
    rep = lax.axis_index("rep")
    rows = own.shape[1] // 2

    def piece(d, at):
        begin, extent = (me ^ d, at * rows, 0), (1, rows, own.shape[2])
        return add_low(
            lax.dynamic_slice(own, begin, extent)[0],
            lax.dynamic_slice(received, begin, extent)[0],
        )

    if shard_size == 4:
        got_a = shard_swap(jnp.stack([piece(1, 0), piece(3, 0)]), 1)
        got_b = shard_swap(jnp.stack([piece(2, 1), piece(3, 1)]), 2)
        got_a, got_b = yield (got_a, got_b)
        pass_a = shard_swap(add_low(piece(2, 0), got_a[1]), 2)
        pass_b = shard_swap(add_low(piece(1, 1), got_b[1]), 1)
        pass_a, pass_b = yield (pass_a, pass_b)
        sum_a = add_low(piece(0, 0).astype(jnp.float32) + got_a[0].astype(jnp.float32), pass_a)
        sum_b = add_low(piece(0, 1).astype(jnp.float32) + got_b[0].astype(jnp.float32), pass_b)
        halves = [sum_a, sum_b]
    else:
        held = {d: jnp.stack([piece(d, 0), piece(d, 1)]) for d in range(shard_size)}
        bit = shard_size // 2
        while bit:
            sent = [d for d in sorted(held) if d & bit]
            got = shard_swap(jnp.stack([held[d] for d in sent]), bit)
            (got,) = yield (got,)
            held = {d ^ bit: add_low(held[d ^ bit], got[at]) for at, d in enumerate(sent)}
            bit //= 2
        halves = [held[0][0], held[0][1]]
    upper = lax.rem(rep // 2, 2) == 1
    if rep_size >= 8:
        keep = jnp.where(upper, halves[1], halves[0])
        send = jnp.where(upper, halves[0], halves[1])
        got = rep_swap(send, 2)
        (got,) = yield (got,)
        keep = add_low(keep, got)
        bit = 4
        while bit < rep_size:
            got = rep_swap(keep, bit)
            (got,) = yield (got,)
            keep = add_low(keep, got)
            bit *= 2
        back = rep_swap(keep, 2)
        (back,) = yield (back,)
        halves = [jnp.where(upper, back, keep), jnp.where(upper, keep, back)]
        half = jnp.concatenate(halves, axis=0)
    else:
        half = jnp.concatenate(halves, axis=0)
        bit = 2
        while bit < rep_size:
            half = add_low(half, rep_swap(half, bit))
            bit *= 2
    other = rep_swap(half, 1)
    (other,) = yield (other,)
    return half, other


def join_rows(pair):
    core = lax.rem(lax.axis_index("rep"), 2)
    half, other = pair
    return jnp.where(
        core == 0,
        jnp.concatenate([half, other], axis=0),
        jnp.concatenate([other, half], axis=0),
    ).astype(jnp.float32)


def join_columns(pair):
    core = lax.rem(lax.axis_index("rep"), 2)
    half, other = pair
    return jnp.where(
        core == 0,
        jnp.concatenate([half, other], axis=1),
        jnp.concatenate([other, half], axis=1),
    ).astype(jnp.float32)


BLOCK = 256
LOOK = 3


def nt_dot(left_mat, right_mat):
    return lax.dot_general(
        left_mat, right_mat, (((1,), (1,)), ((), ())), preferred_element_type=jnp.float32
    )


def attend_kernel(live_ref, q_ref, k_ref, v_ref, seg_col_ref, seg_row_ref, o_ref, acc_ref):
    at = pl.program_id(1)
    acc_ref[...] = jnp.zeros_like(acc_ref)
    lane = lax.broadcasted_iota(jnp.int32, (BLOCK, 2 * HD), 1)
    low_lane = lane < HD
    for back in range(LOOK):
        key_block = jnp.maximum(at - back, 0)

        @pl.when((at >= back) & (live_ref[at, key_block] > 0))
        def _():
            begin = pl.multiple_of(key_block * BLOCK, BLOCK)
            same = seg_col_ref[...] == seg_row_ref[:, pl.ds(begin, BLOCK)]
            if back == 0:
                row = lax.broadcasted_iota(jnp.int32, (BLOCK, BLOCK), 0)
                col = lax.broadcasted_iota(jnp.int32, (BLOCK, BLOCK), 1)
                same = same & (col <= row)
            mask = same.astype(jnp.float32)
            keys = k_ref[pl.ds(begin, BLOCK), :]
            values = v_ref[pl.ds(begin, BLOCK), :]
            swapped = pltpu.roll(values.astype(jnp.float32), HD, 1).astype(jnp.bfloat16)
            one = jnp.ones_like(values)
            for head in range(4):
                group, odd = head // 2, head % 2
                scores = nt_dot(
                    q_ref[:, head * HD : (head + 1) * HD], keys[:, group * HD : (group + 1) * HD]
                )
                weights = (jnp.exp(scores) * mask).astype(jnp.bfloat16)
                held = values if group == odd else swapped
                padded = jnp.where(low_lane, held, one) if odd == 0 else jnp.where(low_lane, one, held)
                acc_ref[head] += jnp.dot(weights, padded, preferred_element_type=jnp.float32)

    for group in range(2):
        even, odd = acc_ref[2 * group], acc_ref[2 * group + 1]
        top = jnp.where(low_lane, even, odd)
        total = pltpu.roll(jnp.where(low_lane, odd, even), HD, 1)
        o_ref[:, group * 2 * HD : (group + 1) * 2 * HD] = (top / total).astype(o_ref.dtype)


def attend_back_kernel(
    live_ref, q_ref, do_ref, k_ref, v_ref, seg_col_ref, seg_row_ref,
    dq_ref, dk_ref, dv_ref, exp_ref, dp_ref, total_ref, inner_ref, dqt_ref,
):
    at = pl.program_id(1)

    @pl.when(at == 0)
    def _():
        dk_ref[...] = jnp.zeros_like(dk_ref)
        dv_ref[...] = jnp.zeros_like(dv_ref)

    total_ref[...] = jnp.zeros_like(total_ref)
    inner_ref[...] = jnp.zeros_like(inner_ref)
    dqt_ref[...] = jnp.zeros_like(dqt_ref)

    def each_block(run):
        for back in range(LOOK):
            key_block = jnp.maximum(at - back, 0)

            @pl.when((at >= back) & (live_ref[at, key_block] > 0))
            def _():
                run(back, pl.multiple_of(key_block * BLOCK, BLOCK))

    def first(back, begin):
        same = seg_col_ref[pl.ds(begin, BLOCK), :] == seg_row_ref[...]
        if back == 0:
            row = lax.broadcasted_iota(jnp.int32, (BLOCK, BLOCK), 0)
            col = lax.broadcasted_iota(jnp.int32, (BLOCK, BLOCK), 1)
            same = same & (row <= col)
        mask = same.astype(jnp.float32)
        keys = k_ref[pl.ds(begin, BLOCK), :]
        values = v_ref[pl.ds(begin, BLOCK), :]
        for head in range(4):
            group = head // 2
            cols = slice(head * HD, (head + 1) * HD)
            kept = slice(group * HD, (group + 1) * HD)
            weights = jnp.exp(nt_dot(keys[:, kept], q_ref[:, cols])) * mask
            grads = nt_dot(values[:, kept], do_ref[:, cols])
            exp_ref[head, back] = weights
            dp_ref[head, back] = grads
            total_ref[head : head + 1] += jnp.sum(weights, axis=0, keepdims=True)
            inner_ref[head : head + 1] += jnp.sum(weights * grads, axis=0, keepdims=True)

    def second(back, begin):
        keys = k_ref[pl.ds(begin, BLOCK), :]
        dk_parts, dv_parts = [], []
        for group in range(2):
            dk_sum, dv_sum = None, None
            for head in (2 * group, 2 * group + 1):
                cols = slice(head * HD, (head + 1) * HD)
                scale = 1.0 / total_ref[head : head + 1]
                probs = exp_ref[head, back] * scale
                inner = inner_ref[head : head + 1] * scale
                low_scores = (probs * (dp_ref[head, back] - inner)).astype(jnp.bfloat16)
                dv_part = jnp.dot(
                    probs.astype(jnp.bfloat16), do_ref[:, cols], preferred_element_type=jnp.float32
                )
                dk_part = jnp.dot(low_scores, q_ref[:, cols], preferred_element_type=jnp.float32)
                dqt_ref[cols] += lax.dot_general(
                    keys[:, group * HD : (group + 1) * HD],
                    low_scores,
                    (((0,), (0,)), ((), ())),
                    preferred_element_type=jnp.float32,
                )
                dk_sum = dk_part if dk_sum is None else dk_sum + dk_part
                dv_sum = dv_part if dv_sum is None else dv_sum + dv_part
            dk_parts.append(dk_sum)
            dv_parts.append(dv_sum)
        dk_ref[pl.ds(begin, BLOCK), :] += jnp.concatenate(dk_parts, axis=1)
        dv_ref[pl.ds(begin, BLOCK), :] += jnp.concatenate(dv_parts, axis=1)

    each_block(first)
    each_block(second)
    dq_ref[...] = dqt_ref[...].T


def live_blocks(segment):
    count = segment.shape[0] // BLOCK
    blocks = segment.reshape(count, BLOCK)
    index = jnp.arange(count)
    return (
        (blocks[:, :1] == blocks[:, -1][None, :]) | (index[:, None] == index[None, :])
    ).astype(jnp.int32)


def attend(query, key, value, segment):
    rows = query.shape[0]
    panels, count = HK // 2, rows // BLOCK
    return pl.pallas_call(
        attend_kernel,
        out_shape=jax.ShapeDtypeStruct((rows, HQ * HD), jnp.bfloat16),
        grid_spec=pltpu.PrefetchScalarGridSpec(
            num_scalar_prefetch=1,
            grid=(panels, count),
            in_specs=[
                pl.BlockSpec((BLOCK, 4 * HD), lambda p, i, live: (i, p)),
                pl.BlockSpec((rows, 2 * HD), lambda p, i, live: (0, p)),
                pl.BlockSpec((rows, 2 * HD), lambda p, i, live: (0, p)),
                pl.BlockSpec((BLOCK, 1), lambda p, i, live: (i, 0)),
                pl.BlockSpec((1, rows), lambda p, i, live: (0, 0)),
            ],
            out_specs=pl.BlockSpec((BLOCK, 4 * HD), lambda p, i, live: (i, p)),
            scratch_shapes=[pltpu.VMEM((4, BLOCK, 2 * HD), jnp.float32)],
        ),
        cost_estimate=TINY,
        name="attend",
    )(live_blocks(segment), query, key, value, segment[:, None], segment[None, :])


def attend_back(query, grad_out, key, value, segment, start, panels):
    rows = query.shape[0]
    count = rows // BLOCK
    return pl.pallas_call(
        attend_back_kernel,
        out_shape=(
            jax.ShapeDtypeStruct((rows, panels * 4 * HD), jnp.float32),
            jax.ShapeDtypeStruct((rows, panels * 2 * HD), jnp.float32),
            jax.ShapeDtypeStruct((rows, panels * 2 * HD), jnp.float32),
        ),
        grid_spec=pltpu.PrefetchScalarGridSpec(
            num_scalar_prefetch=1,
            grid=(panels, count),
            in_specs=[
                pl.BlockSpec((BLOCK, 4 * HD), lambda p, i, live: (i, start + p)),
                pl.BlockSpec((BLOCK, 4 * HD), lambda p, i, live: (i, start + p)),
                pl.BlockSpec((rows, 2 * HD), lambda p, i, live: (0, start + p)),
                pl.BlockSpec((rows, 2 * HD), lambda p, i, live: (0, start + p)),
                pl.BlockSpec((rows, 1), lambda p, i, live: (0, 0)),
                pl.BlockSpec((1, BLOCK), lambda p, i, live: (0, i)),
            ],
            out_specs=[
                pl.BlockSpec((BLOCK, 4 * HD), lambda p, i, live: (i, p)),
                pl.BlockSpec((rows, 2 * HD), lambda p, i, live: (0, p)),
                pl.BlockSpec((rows, 2 * HD), lambda p, i, live: (0, p)),
            ],
            scratch_shapes=[
                pltpu.VMEM((4, LOOK, BLOCK, BLOCK), jnp.float32),
                pltpu.VMEM((4, LOOK, BLOCK, BLOCK), jnp.float32),
                pltpu.VMEM((8, BLOCK), jnp.float32),
                pltpu.VMEM((8, BLOCK), jnp.float32),
                pltpu.VMEM((4 * HD, BLOCK), jnp.float32),
            ],
        ),
        cost_estimate=TINY,
        name="attend_back",
    )(live_blocks(segment), query, grad_out, key, value, segment[:, None], segment[None, :])


def body(
    links,
    tokens,
    cotangent,
    segment,
    attn_gain,
    w_query,
    w_key,
    w_value,
    qk_gain,
    w_out,
    ffn_gain,
    w_gate,
    w_up,
    w_down,
):
    row_count = tokens.shape[0]
    rep_swap = links[3]
    core = lax.rem(lax.axis_index("rep"), 2)
    score_scale = 1.0 / math.sqrt(HD)
    spare = jnp.zeros((attn_gain.shape[0] - qk_gain.shape[0],), jnp.bfloat16)
    packed = jnp.stack([attn_gain, ffn_gain, jnp.concatenate([qk_gain, spare])], axis=1)
    packed = jnp.pad(packed, ((0, 0), (0, 125)))
    attn_weights = (w_query, w_key, w_value, packed)
    front_flow = Flow(
        gather_steps(
            links,
            jnp.concatenate([core_half(weight) for weight in attn_weights], axis=1),
            jnp.concatenate(attn_weights, axis=1),
        )
    )
    w_out, w_gate, w_up, w_down = sync((w_out, w_gate, w_up, w_down), front_flow)
    out_flow = Flow(gather_steps(links, core_half(w_out), w_out))
    w_gate, w_up, w_down = sync((w_gate, w_up, w_down), front_flow, out_flow)
    pair = jnp.concatenate([core_half(w_gate), core_half(w_up)], axis=1)
    pair_flow = Flow(gather_steps(links, pair, None, late=True))
    w_down = sync(w_down, front_flow)
    front = place_blocks(front_flow.finish())
    full_query = front[:, : HQ * HD]
    full_key = front[:, HQ * HD : (HQ + HK) * HD]
    full_value = front[:, (HQ + HK) * HD : (HQ + 2 * HK) * HD]
    gains = front[:, (HQ + 2 * HK) * HD :]
    full_attn_gain = gains[:, 0]
    full_ffn_gain = gains[:, 1]
    full_qk_gain = gains.reshape(links[0], -1, 128)[:, : qk_gain.shape[0], 2].reshape(-1)
    inputs = tokens.astype(jnp.float32)
    token_index = jnp.arange(row_count)
    same_seq = segment[:, None] == segment[None, :]
    allowed = same_seq & (token_index[None, :] <= token_index[:, None])
    positions = jnp.sum(
        (same_seq & (token_index[None, :] < token_index[:, None])).astype(jnp.float32), axis=1
    )
    live_rows = (segment >= 0).astype(jnp.float32)[:, None]
    cosine, sine_table = rope_tables(positions)
    scale_one = inv_rms(inputs)
    normed = (inputs * scale_one * full_attn_gain.astype(jnp.float32)).astype(jnp.bfloat16)
    query_lin = matmul_plain(normed, full_query).reshape(row_count, HQ, HD)
    key_lin = matmul_plain(normed, full_key).reshape(row_count, HK, HD)
    value_low = matmul_plain(normed, full_value).astype(jnp.bfloat16).reshape(row_count, HK, HD)
    qk_gains = full_qk_gain.astype(jnp.float32)
    query_scale = inv_rms(query_lin)
    key_scale = inv_rms(key_lin)
    query_rot = (
        rotate(query_lin * query_scale * qk_gains[:HD], cosine, sine_table)
        .astype(jnp.bfloat16)
    )
    key_rot = rotate(key_lin * key_scale * qk_gains[HD:], cosine, sine_table).astype(jnp.bfloat16)

    query_rot = (query_rot.astype(jnp.float32) * score_scale).astype(jnp.bfloat16)
    query_rot = query_rot.reshape(row_count, HQ * HD)
    key_rot = key_rot.reshape(row_count, HK * HD)
    value_low = value_low.reshape(row_count, HK * HD)
    query_rot, key_rot, value_low, w_down = sync(
        (query_rot, key_rot, value_low, w_down), out_flow, pair_flow
    )
    down_flow = Flow(gather_steps(links, core_half(w_down), w_down))
    attn_low = attend(query_rot, key_rot, value_low, segment)
    attn_low = sync(attn_low, out_flow)
    full_out = place_blocks(out_flow.finish())
    hidden = inputs + matmul_plain(attn_low, full_out)
    scale_two = inv_rms(hidden)
    normed_ffn = (hidden * scale_two * full_ffn_gain.astype(jnp.float32)).astype(jnp.bfloat16)
    normed_ffn, hidden = sync((normed_ffn, hidden), pair_flow)
    normed_ffn = sync(normed_ffn, pair_flow, down_flow)
    pair = pair_flow.finish()
    mixed_act, act_low, slope = ffn_forward(normed_ffn, w_gate, w_up, pair)
    mixed_act, slope, act_low = sync((mixed_act, slope, act_low), down_flow)
    mixed_act, slope, act_low = sync((mixed_act, slope, act_low), down_flow)
    full_down = place_blocks(down_flow.finish())
    out_grad = live_rows * cotangent.astype(jnp.float32)
    out_low = out_grad.astype(jnp.bfloat16)
    grad_gate_low, grad_up_low = ffn_inner(out_low, full_down, act_low, slope)
    half = out_low.shape[1] // 2
    out_own = lax.dynamic_slice_in_dim(out_low, core * half, half, 1)
    out_other = lax.dynamic_slice_in_dim(out_low, (1 - core) * half, half, 1)
    normed_own, normed_other = pick_columns(links, normed_ffn)
    grad_up_low, grad_gate_low, out_own, out_other, mixed_act = pin(
        (grad_up_low, grad_gate_low, out_own, out_other, mixed_act)
    )

    def hand(product):
        return rep_swap(blocked(links, product).astype(jnp.bfloat16), 1)

    down_given = matmul_rows(mixed_act, out_other).astype(jnp.bfloat16)
    down_sent = hand(down_given)
    gate_given = matmul_rows(normed_other, pin(grad_gate_low, down_given)).astype(jnp.bfloat16)
    gate_sent = hand(gate_given)
    down_sent, mixed_act, grad_up_low, gate_given = pin(
        (down_sent, mixed_act, grad_up_low, gate_given)
    )
    down_given = blocked(links, matmul_rows(mixed_act, out_own).astype(jnp.bfloat16))
    down_back = Flow(scatter_steps(links, *pin((down_given, down_sent))))
    grad_up_low, grad_gate_low, normed_own, normed_other = pin(
        (grad_up_low, grad_gate_low, normed_own, normed_other), down_given
    )
    up_sent = hand(matmul_rows(normed_other, grad_up_low))
    gate_given = blocked(links, matmul_rows(normed_own, grad_gate_low).astype(jnp.bfloat16))
    up_given = blocked(links, matmul_rows(normed_own, grad_up_low).astype(jnp.bfloat16))
    gate_given, gate_sent, up_given, up_sent, grad_gate_low, grad_up_low = sync(
        (gate_given, gate_sent, up_given, up_sent, grad_gate_low, grad_up_low), down_back
    )
    gate_back = Flow(scatter_steps(links, gate_given, gate_sent))
    grad_normed_ffn = ffn_input(grad_gate_low, grad_up_low, w_gate, w_up, pair)
    grad_normed_ffn, up_given, up_sent = sync((grad_normed_ffn, up_given, up_sent), down_back)
    grad_ffn_gain = jnp.sum(grad_normed_ffn * hidden * scale_two, axis=0)
    grad_hidden = out_grad + norm_back(
        grad_normed_ffn, hidden, scale_two, full_ffn_gain.astype(jnp.float32)
    )
    hidden_low = grad_hidden.astype(jnp.bfloat16)
    grad_attn_low = matmul_cols(hidden_low, full_out).astype(jnp.bfloat16)
    attn_own, attn_other = pick_columns(links, attn_low)
    out_sent = hand(matmul_rows(attn_other, hidden_low))
    out_given = blocked(links, matmul_rows(attn_own, hidden_low).astype(jnp.bfloat16))
    panels = HK // 4
    grad_attn_low, out_given, out_sent, up_given, up_sent = sync(
        (grad_attn_low, out_given, out_sent, up_given, up_sent), gate_back, down_back
    )
    up_back = Flow(scatter_steps(links, up_given, up_sent))
    lower = attend_back(query_rot, grad_attn_low, key_rot, value_low, segment, 0, panels)
    grad_attn_low, lower = pin((grad_attn_low, lower))
    upper = attend_back(query_rot, grad_attn_low, key_rot, value_low, segment, panels, panels)
    lower, upper, out_given, out_sent = sync(
        (lower, upper, out_given, out_sent), gate_back, down_back, up_back
    )
    out_back = Flow(scatter_steps(links, out_given, out_sent))
    grad_query_rot, grad_key_rot, grad_value = (
        jnp.concatenate(pair, axis=1) for pair in zip(lower, upper)
    )
    grad_query_rot = (score_scale * grad_query_rot).reshape(row_count, HQ, HD)
    grad_key_rot = grad_key_rot.reshape(row_count, HK, HD)
    grad_query_norm = rotate_back(grad_query_rot, cosine, sine_table)
    grad_key_norm = rotate_back(grad_key_rot, cosine, sine_table)
    back_gains = full_qk_gain.astype(jnp.float32)
    grad_qk_gain = jnp.concatenate(
        [
            jnp.sum(grad_query_norm * query_lin * query_scale, axis=(0, 1)),
            jnp.sum(grad_key_norm * key_lin * key_scale, axis=(0, 1)),
        ]
    )
    grad_query_low = (
        norm_back(grad_query_norm, query_lin, query_scale, back_gains[:HD])
        .astype(jnp.bfloat16)
        .reshape(row_count, HQ * HD)
    )
    grad_key_low = (
        norm_back(grad_key_norm, key_lin, key_scale, back_gains[HD:])
        .astype(jnp.bfloat16)
        .reshape(row_count, HK * HD)
    )
    grad_value_low = grad_value.astype(jnp.bfloat16).reshape(row_count, HK * HD)
    normed_own, normed_other = pick_columns(links, normed)
    grad_front = jnp.concatenate([grad_query_low, grad_key_low, grad_value_low], axis=1)
    grad_front = sync(grad_front, up_back, gate_back, down_back, out_back)
    grad_query_low = grad_front[:, : HQ * HD]
    grad_key_low = grad_front[:, HQ * HD : (HQ + HK) * HD]
    grad_value_low = grad_front[:, (HQ + HK) * HD :]
    front_other = blocked(links, matmul_rows(normed_other, grad_front))
    front_own = blocked(links, matmul_rows(normed_own, grad_front))
    grad_normed = (
        matmul_cols(grad_query_low, full_query)
        + matmul_cols(grad_key_low, full_key)
        + matmul_cols(grad_value_low, full_value)
    )
    grad_attn_gain = jnp.sum(grad_normed * inputs * scale_one, axis=0)
    grad_inputs = grad_hidden + norm_back(
        grad_normed, inputs, scale_one, full_attn_gain.astype(jnp.float32)
    )
    qk_part = jnp.pad(
        grad_qk_gain.reshape(links[0], -1),
        ((0, 0), (0, attn_gain.shape[0] - qk_gain.shape[0])),
    )
    small = jnp.stack([grad_attn_gain, grad_ffn_gain, qk_part.reshape(-1)], axis=1)
    small = jnp.pad(small, ((0, 0), (0, 125)))
    small = small.reshape(links[0], 2, -1, 128)
    own_front = jnp.concatenate([front_own, lax.dynamic_slice_in_dim(small, core, 1, 1)[:, 0]], axis=2)
    other_front = jnp.concatenate(
        [front_other, lax.dynamic_slice_in_dim(small, 1 - core, 1, 1)[:, 0]], axis=2
    )
    front_sent = rep_swap(other_front.astype(jnp.bfloat16), 1)
    own_front = own_front.astype(jnp.bfloat16)
    own_front, front_sent, mixed_act = sync(
        (own_front, front_sent, mixed_act), out_back, up_back, gate_back
    )
    front_back = Flow(scatter_steps(links, own_front, front_sent))
    result = live_rows * (hidden + matmul_plain(mixed_act, full_down))
    grad_inputs, result = sync((grad_inputs, result), up_back, gate_back, out_back, front_back)
    front_share = join_rows(front_back.finish())
    share_query = front_share[:, : HQ * HD]
    share_key = front_share[:, HQ * HD : (HQ + HK) * HD]
    share_value = front_share[:, (HQ + HK) * HD : (HQ + 2 * HK) * HD]
    extras = front_share[:, (HQ + 2 * HK) * HD :]
    share_again = extras[:, 0]
    share_fgain = extras[:, 1]
    share_qk = extras[: qk_gain.shape[0], 2]
    share_out = join_rows(out_back.finish())
    share_gate = join_rows(gate_back.finish())
    share_up = join_rows(up_back.finish())
    share_down = join_columns(down_back.finish())
    return (
        result.astype(jnp.bfloat16),
        grad_inputs.astype(jnp.bfloat16),
        share_again,
        share_query,
        share_key,
        share_value,
        share_qk,
        share_out,
        share_fgain,
        share_gate,
        share_up,
        share_down,
    )


def solution(mesh):
    return jax.shard_map(
        functools.partial(body, make_links(mesh)),
        mesh=mesh,
        in_specs=(
            P(("shard", "rep"), None),
            P(("shard", "rep"), None),
            P(("shard", "rep")),
            P("shard"),
            P("shard", None),
            P("shard", None),
            P("shard", None),
            P("shard"),
            P("shard", None),
            P("shard"),
            P("shard", None),
            P("shard", None),
            P("shard", None),
        ),
        out_specs=(
            P(("shard", "rep"), None),
            P(("shard", "rep"), None),
            P("shard"),
            P("shard", None),
            P("shard", None),
            P("shard", None),
            P("shard"),
            P("shard", None),
            P("shard"),
            P("shard", None),
            P("shard", None),
            P("shard", None),
        ),
        check_vma=False,
    )
```

```python
import functools
import math

import jax
import jax.numpy as jnp
from jax import lax
from jax.experimental import pallas as pl
from jax.experimental.pallas import tpu as pltpu
from jax.sharding import PartitionSpec as P

HQ = 16
HK = 8
HD = 64


norm_eps = 1e-05
TINY = pl.CostEstimate(flops=1, bytes_accessed=1, transcendentals=0)
rope_base = 1000000.0


def inv_rms(values):
    return lax.rsqrt(jnp.mean(values * values, axis=-1, keepdims=True) + norm_eps)


def rope_tables(positions):
    half_dim = HD // 2
    freq_index = jnp.arange(half_dim).astype(jnp.float32)
    freq_vals = jnp.power(rope_base, -(2.0 * freq_index) / HD)
    angles = positions[:, None] * freq_vals[None, :]
    return (jnp.cos(angles)[:, None, :], jnp.sin(angles)[:, None, :])


def rotate(values, cosine, sine_table):
    half_dim = HD // 2
    first_half = values[..., :half_dim]
    second_half = values[..., half_dim:]
    return jnp.concatenate(
        [
            first_half * cosine - second_half * sine_table,
            second_half * cosine + first_half * sine_table,
        ],
        axis=-1,
    )


def rotate_back(grad_vals, cosine, sine_table):
    half_dim = HD // 2
    first_half = grad_vals[..., :half_dim]
    second_half = grad_vals[..., half_dim:]
    return jnp.concatenate(
        [
            first_half * cosine + second_half * sine_table,
            second_half * cosine - first_half * sine_table,
        ],
        axis=-1,
    )


def norm_back(grad_out, inputs, scale_inv, gain_vec):
    weighted = grad_out * gain_vec
    row_inner = jnp.mean(weighted * inputs, axis=-1, keepdims=True)
    return scale_inv * weighted - inputs * (scale_inv * scale_inv * scale_inv) * row_inner


def matmul_plain(left_mat, right_mat):
    return jnp.dot(left_mat, right_mat, preferred_element_type=jnp.float32)


def matmul_rows(left_mat, right_mat):
    return lax.dot_general(
        left_mat, right_mat, (((0,), (0,)), ((), ())), preferred_element_type=jnp.float32
    )


def matmul_cols(left_mat, right_mat):
    return lax.dot_general(
        left_mat, right_mat, (((1,), (1,)), ((), ())), preferred_element_type=jnp.float32
    )


def make_links(mesh):
    shard_size, rep_size = mesh.shape["shard"], mesh.shape["rep"]
    axes = ("shard", "rep")

    def shard_swap(value, bit):
        pairs = [
            (s * rep_size + r, (s ^ bit) * rep_size + r)
            for s in range(shard_size)
            for r in range(rep_size)
        ]
        return lax.ppermute(value, axes, pairs)

    def rep_swap(value, bit):
        pairs = [
            (s * rep_size + r, s * rep_size + (r ^ bit))
            for s in range(shard_size)
            for r in range(rep_size)
        ]
        return lax.ppermute(value, axes, pairs)

    return shard_size, rep_size, shard_swap, rep_swap


def add_low(left, right):
    return (left.astype(jnp.float32) + right.astype(jnp.float32)).astype(jnp.bfloat16)


def pin(values, *waits):
    return lax.optimization_barrier((values, waits))[0]


class Flow:
    def __init__(self, steps):
        self.steps = steps
        self.result = None
        self.pending = next(steps)

    def resume(self, arrived):
        try:
            self.pending = self.steps.send(arrived)
        except StopIteration as stop:
            self.pending = ()
            self.steps = None
            self.result = stop.value

    def finish(self):
        while self.steps is not None:
            self.resume(self.pending)
        return self.result


def sync(values, *flows):
    flows = [flow for flow in flows if flow.steps is not None]
    values, arrived = lax.optimization_barrier((values, [flow.pending for flow in flows]))
    for flow, got in zip(flows, arrived):
        flow.resume(got)
    return values


def place_kernel(spots_ref, *refs):
    del spots_ref
    out_ref = refs[-1]
    for at in range(len(refs) - 1):

        @pl.when(pl.program_id(0) == at)
        def _():
            out_ref[...] = refs[at][...]


def place_blocks(gathered):
    blocks, spots = gathered
    rows, width = blocks[1].shape
    count = len(blocks) + 1
    return pl.pallas_call(
        place_kernel,
        out_shape=jax.ShapeDtypeStruct((count * rows, width), blocks[0].dtype),
        grid_spec=pltpu.PrefetchScalarGridSpec(
            num_scalar_prefetch=1,
            grid=(count,),
            in_specs=[
                pl.BlockSpec((rows, width), lambda i, spot, at=at: (at, 0))
                for at in (0, 1) + (0,) * (count - 2)
            ],
            out_specs=pl.BlockSpec((rows, width), lambda i, spot: (spot[i], 0)),
        ),
        cost_estimate=TINY,
        compiler_params=pltpu.CompilerParams(vmem_limit_bytes=60 << 20),
        name="place_blocks",
    )(spots, blocks[0], *blocks)


FF_TILE = 512


def block_specs(count, rows, tiles, start=0):
    own = [
        pl.BlockSpec((rows, FF_TILE), lambda i, spot, at=at: (at, i + start)) for at in (0, 1)
    ]
    gate = [pl.BlockSpec((rows, FF_TILE), lambda i, spot: (0, i + start))] * (count - 2)
    up = [pl.BlockSpec((rows, FF_TILE), lambda i, spot: (0, i + start + tiles))] * (count - 2)
    return own + gate + own + up


def settle(spots_ref, refs, whole_ref):
    rows = refs[0].shape[0]
    for at, ref in enumerate(refs):
        begin = pl.multiple_of(spots_ref[at] * rows, rows)
        whole_ref[pl.ds(begin, rows), :] = ref[...]


def ffn_forward_kernel(count, spare, spots_ref, a_ref, *refs):
    refs = refs[: 2 * count] + refs[2 * count + spare :]
    gate_refs, up_refs = refs[:count], refs[count : 2 * count]
    z_ref, act_ref, slope_ref, gate_whole, up_whole = refs[2 * count :]
    settle(spots_ref, gate_refs, gate_whole)
    settle(spots_ref, up_refs, up_whole)
    step = min(256, a_ref.shape[0])
    for begin in range(0, a_ref.shape[0], step):
        rows = slice(begin, begin + step)
        gate = jnp.dot(a_ref[rows], gate_whole[...], preferred_element_type=jnp.float32)
        up = jnp.dot(a_ref[rows], up_whole[...], preferred_element_type=jnp.float32)
        sig = jax.nn.sigmoid(gate)
        act = gate * sig
        z_ref[rows] = (act * up).astype(jnp.bfloat16)
        act_ref[rows] = act.astype(jnp.bfloat16)
        slope_ref[rows] = (up * (sig + act * (1.0 - sig))).astype(jnp.bfloat16)


def ffn_forward(normed, gate, up, gathered, start, steps, into):
    rows, depth = normed.shape
    blocks, spots = gathered
    count = len(blocks) + 2
    hidden = gate.shape[1]
    part = gate.shape[0] // 2
    out = jax.ShapeDtypeStruct((rows, hidden), jnp.bfloat16)
    into = [] if into is None else list(into)
    first = 2 + 2 * count
    return pl.pallas_call(
        functools.partial(ffn_forward_kernel, count, len(into)),
        out_shape=(out, out, out),
        grid_spec=pltpu.PrefetchScalarGridSpec(
            num_scalar_prefetch=1,
            grid=(steps,),
            in_specs=[pl.BlockSpec((rows, depth), lambda i, spot: (0, 0))]
            + block_specs(count, part, hidden // FF_TILE, start)
            + [pl.BlockSpec(memory_space=pl.ANY)] * len(into),
            out_specs=[pl.BlockSpec((rows, FF_TILE), lambda i, spot: (0, i + start))] * 3,
            scratch_shapes=[pltpu.VMEM((depth, FF_TILE), jnp.bfloat16)] * 2,
        ),
        input_output_aliases={first + at: at for at in range(len(into))},
        cost_estimate=TINY,
        compiler_params=pltpu.CompilerParams(vmem_limit_bytes=60 << 20),
        name="ffn_forward",
    )(spots, normed, gate, gate, *blocks, up, up, *blocks, *into)


def ffn_inner_kernel(g_ref, down_ref, act_ref, slope_ref, dgate_ref, dup_ref):
    step = min(256, g_ref.shape[0])
    for begin in range(0, g_ref.shape[0], step):
        rows = slice(begin, begin + step)
        mixed = nt_dot(g_ref[rows], down_ref[...])
        dgate_ref[rows] = (mixed * slope_ref[rows].astype(jnp.float32)).astype(jnp.bfloat16)
        dup_ref[rows] = (mixed * act_ref[rows].astype(jnp.float32)).astype(jnp.bfloat16)


def ffn_inner(grad_low, down, act, slope):
    rows, depth = grad_low.shape
    hidden = down.shape[0]
    out = jax.ShapeDtypeStruct((rows, hidden), jnp.bfloat16)
    tile = pl.BlockSpec((rows, FF_TILE), lambda i: (0, i))
    return pl.pallas_call(
        ffn_inner_kernel,
        out_shape=(out, out),
        grid=(hidden // FF_TILE,),
        in_specs=[
            pl.BlockSpec((rows, depth), lambda i: (0, 0)),
            pl.BlockSpec((FF_TILE, depth), lambda i: (i, 0)),
            tile,
            tile,
        ],
        out_specs=[tile, tile],
        cost_estimate=TINY,
        compiler_params=pltpu.CompilerParams(vmem_limit_bytes=60 << 20),
        name="ffn_inner",
    )(grad_low, down, act, slope)


def ffn_input_kernel(count, spots_ref, dgate_ref, dup_ref, *refs):
    gate_refs, up_refs = refs[:count], refs[count : 2 * count]
    out_ref, gate_whole, up_whole = refs[2 * count :]
    settle(spots_ref, gate_refs, gate_whole)
    settle(spots_ref, up_refs, up_whole)

    @pl.when(pl.program_id(0) == 0)
    def _():
        out_ref[...] = jnp.zeros_like(out_ref)

    step = min(256, dgate_ref.shape[0])
    for begin in range(0, dgate_ref.shape[0], step):
        rows = slice(begin, begin + step)
        out_ref[rows] += nt_dot(dgate_ref[rows], gate_whole[...]) + nt_dot(
            dup_ref[rows], up_whole[...]
        )


def ffn_input(grad_gate, grad_up, gate, up, gathered):
    rows, hidden = grad_gate.shape
    blocks, spots = gathered
    count = len(blocks) + 2
    part = gate.shape[0] // 2
    depth = count * part
    tile = pl.BlockSpec((rows, FF_TILE), lambda i, spot: (0, i))
    return pl.pallas_call(
        functools.partial(ffn_input_kernel, count),
        out_shape=jax.ShapeDtypeStruct((rows, depth), jnp.float32),
        grid_spec=pltpu.PrefetchScalarGridSpec(
            num_scalar_prefetch=1,
            grid=(hidden // FF_TILE,),
            in_specs=[tile, tile] + block_specs(count, part, hidden // FF_TILE),
            out_specs=pl.BlockSpec((rows, depth), lambda i, spot: (0, 0)),
            scratch_shapes=[pltpu.VMEM((depth, FF_TILE), jnp.bfloat16)] * 2,
        ),
        cost_estimate=TINY,
        compiler_params=pltpu.CompilerParams(vmem_limit_bytes=60 << 20),
        name="ffn_input",
    )(spots, grad_gate, grad_up, gate, gate, *blocks, up, up, *blocks)


def gather_steps(links, mine, whole, late=False):
    shard_size, rep_size, shard_swap, rep_swap = links
    me = lax.axis_index("shard")
    core = lax.rem(lax.axis_index("rep"), 2)
    half, width = mine.shape
    quarter = half // 2
    pieces, others = {}, {}
    if shard_size == 4:
        pieces[1] = shard_swap(mine, 1)
        pieces[2] = shard_swap(mine, 2)
        pieces[1], pieces[2] = yield (pieces[1], pieces[2])
        corner_a = shard_swap(pieces[1][:quarter], 2)
        corner_b = shard_swap(pieces[2][quarter:], 1)
        if late:
            early, waiting = (), (1, 2, 3)
            corner_a, corner_b, pieces[1], pieces[2] = yield (
                corner_a, corner_b, pieces[1], pieces[2]
            )
        else:
            early, waiting = (rep_swap(pieces[1], 1), rep_swap(pieces[2], 1)), (3,)
            corner_a, corner_b, *early = yield (corner_a, corner_b, *early)
        pieces[3] = jnp.concatenate([corner_a, corner_b], axis=0)
        if late == "joined":
            joined = jnp.stack([pieces[1], pieces[2], pieces[3]])
            (got,) = yield (rep_swap(joined, 1),)
            others = {d: got[d - 1] for d in (1, 2, 3)}
        else:
            rest = yield tuple(rep_swap(pieces[d], 1) for d in waiting)
            others = dict(zip((1, 2, 3), (*early, *rest)))
    else:
        pieces[0] = mine
        bit = 1
        while bit < shard_size:
            order = sorted(pieces)
            got = shard_swap(jnp.stack([pieces[d] for d in order]), bit)
            (got,) = yield (got,)
            for at, d in enumerate(order):
                pieces[d ^ bit] = got[at]
            bit *= 2
        del pieces[0]
        others = {d: rep_swap(piece, 1) for d, piece in pieces.items()}
    blocks, spots = [whole] if whole is not None else [], [2 * me, 2 * me + 1]
    for d in pieces:
        blocks += [pieces[d], others[d]]
        spots += [2 * (me ^ d) + core, 2 * (me ^ d) + 1 - core]
    return blocks, jnp.stack(spots).astype(jnp.int32)


def core_half(weight):
    core = lax.rem(lax.axis_index("rep"), 2)
    half = weight.shape[0] // 2
    return lax.dynamic_slice_in_dim(weight, core * half, half, 0)


def pick_columns(links, value):
    core = lax.rem(lax.axis_index("rep"), 2)
    width = value.shape[1] // links[0] // 2

    def half(which):
        return jnp.concatenate(
            [
                lax.dynamic_slice_in_dim(value, (2 * d + which) * width, width, 1)
                for d in range(links[0])
            ],
            axis=1,
        )

    return half(core), half(1 - core)


def blocked(links, product):
    return product.reshape(links[0], -1, product.shape[1])


def scatter_steps(links, own, received):
    shard_size, rep_size, shard_swap, rep_swap = links
    me = lax.axis_index("shard")
    rep = lax.axis_index("rep")
    rows = own.shape[1] // 2

    def piece(d, at):
        begin, extent = (me ^ d, at * rows, 0), (1, rows, own.shape[2])
        return add_low(
            lax.dynamic_slice(own, begin, extent)[0],
            lax.dynamic_slice(received, begin, extent)[0],
        )

    if shard_size == 4:
        got_a = shard_swap(jnp.stack([piece(1, 0), piece(3, 0)]), 1)
        got_b = shard_swap(jnp.stack([piece(2, 1), piece(3, 1)]), 2)
        got_a, got_b = yield (got_a, got_b)
        pass_a = shard_swap(add_low(piece(2, 0), got_a[1]), 2)
        pass_b = shard_swap(add_low(piece(1, 1), got_b[1]), 1)
        pass_a, pass_b = yield (pass_a, pass_b)
        sum_a = add_low(piece(0, 0).astype(jnp.float32) + got_a[0].astype(jnp.float32), pass_a)
        sum_b = add_low(piece(0, 1).astype(jnp.float32) + got_b[0].astype(jnp.float32), pass_b)
        halves = [sum_a, sum_b]
    else:
        held = {d: jnp.stack([piece(d, 0), piece(d, 1)]) for d in range(shard_size)}
        bit = shard_size // 2
        while bit:
            sent = [d for d in sorted(held) if d & bit]
            got = shard_swap(jnp.stack([held[d] for d in sent]), bit)
            (got,) = yield (got,)
            held = {d ^ bit: add_low(held[d ^ bit], got[at]) for at, d in enumerate(sent)}
            bit //= 2
        halves = [held[0][0], held[0][1]]
    upper = lax.rem(rep // 2, 2) == 1
    if rep_size >= 8:
        keep = jnp.where(upper, halves[1], halves[0])
        send = jnp.where(upper, halves[0], halves[1])
        got = rep_swap(send, 2)
        (got,) = yield (got,)
        keep = add_low(keep, got)
        bit = 4
        while bit < rep_size:
            got = rep_swap(keep, bit)
            (got,) = yield (got,)
            keep = add_low(keep, got)
            bit *= 2
        back = rep_swap(keep, 2)
        (back,) = yield (back,)
        halves = [jnp.where(upper, back, keep), jnp.where(upper, keep, back)]
        half = jnp.concatenate(halves, axis=0)
    else:
        half = jnp.concatenate(halves, axis=0)
        bit = 2
        while bit < rep_size:
            half = add_low(half, rep_swap(half, bit))
            bit *= 2
    other = rep_swap(half, 1)
    (other,) = yield (other,)
    return half, other


def join_rows(pair):
    core = lax.rem(lax.axis_index("rep"), 2)
    half, other = pair
    return jnp.where(
        core == 0,
        jnp.concatenate([half, other], axis=0),
        jnp.concatenate([other, half], axis=0),
    ).astype(jnp.float32)


def join_columns(pair):
    core = lax.rem(lax.axis_index("rep"), 2)
    half, other = pair
    return jnp.where(
        core == 0,
        jnp.concatenate([half, other], axis=1),
        jnp.concatenate([other, half], axis=1),
    ).astype(jnp.float32)


BLOCK = 256
LOOK = 3


def nt_dot(left_mat, right_mat):
    return lax.dot_general(
        left_mat, right_mat, (((1,), (1,)), ((), ())), preferred_element_type=jnp.float32
    )


def attend_kernel(live_ref, q_ref, k_ref, v_ref, seg_col_ref, seg_row_ref, o_ref, acc_ref):
    at = pl.program_id(1)
    acc_ref[...] = jnp.zeros_like(acc_ref)
    lane = lax.broadcasted_iota(jnp.int32, (BLOCK, 2 * HD), 1)
    low_lane = lane < HD
    for back in range(LOOK):
        key_block = jnp.maximum(at - back, 0)

        @pl.when((at >= back) & (live_ref[at, key_block] > 0))
        def _():
            begin = pl.multiple_of(key_block * BLOCK, BLOCK)
            same = seg_col_ref[...] == seg_row_ref[:, pl.ds(begin, BLOCK)]
            if back == 0:
                row = lax.broadcasted_iota(jnp.int32, (BLOCK, BLOCK), 0)
                col = lax.broadcasted_iota(jnp.int32, (BLOCK, BLOCK), 1)
                same = same & (col <= row)
            mask = same.astype(jnp.float32)
            keys = k_ref[pl.ds(begin, BLOCK), :]
            values = v_ref[pl.ds(begin, BLOCK), :]
            swapped = pltpu.roll(values.astype(jnp.float32), HD, 1).astype(jnp.bfloat16)
            one = jnp.ones_like(values)
            for head in range(4):
                group, odd = head // 2, head % 2
                scores = nt_dot(
                    q_ref[:, head * HD : (head + 1) * HD], keys[:, group * HD : (group + 1) * HD]
                )
                weights = (jnp.exp(scores) * mask).astype(jnp.bfloat16)
                held = values if group == odd else swapped
                padded = jnp.where(low_lane, held, one) if odd == 0 else jnp.where(low_lane, one, held)
                acc_ref[head] += jnp.dot(weights, padded, preferred_element_type=jnp.float32)

    for group in range(2):
        even, odd = acc_ref[2 * group], acc_ref[2 * group + 1]
        top = jnp.where(low_lane, even, odd)
        total = pltpu.roll(jnp.where(low_lane, odd, even), HD, 1)
        o_ref[:, group * 2 * HD : (group + 1) * 2 * HD] = (top / total).astype(o_ref.dtype)


def attend_back_kernel(
    live_ref, q_ref, do_ref, k_ref, v_ref, seg_col_ref, seg_row_ref,
    dq_ref, dk_ref, dv_ref, exp_ref, dp_ref, total_ref, inner_ref, dqt_ref,
):
    at = pl.program_id(1)

    @pl.when(at == 0)
    def _():
        dk_ref[...] = jnp.zeros_like(dk_ref)
        dv_ref[...] = jnp.zeros_like(dv_ref)

    total_ref[...] = jnp.zeros_like(total_ref)
    inner_ref[...] = jnp.zeros_like(inner_ref)
    dqt_ref[...] = jnp.zeros_like(dqt_ref)

    def each_block(run):
        for back in range(LOOK):
            key_block = jnp.maximum(at - back, 0)

            @pl.when((at >= back) & (live_ref[at, key_block] > 0))
            def _():
                run(back, pl.multiple_of(key_block * BLOCK, BLOCK))

    def first(back, begin):
        same = seg_col_ref[pl.ds(begin, BLOCK), :] == seg_row_ref[...]
        if back == 0:
            row = lax.broadcasted_iota(jnp.int32, (BLOCK, BLOCK), 0)
            col = lax.broadcasted_iota(jnp.int32, (BLOCK, BLOCK), 1)
            same = same & (row <= col)
        mask = same.astype(jnp.float32)
        keys = k_ref[pl.ds(begin, BLOCK), :]
        values = v_ref[pl.ds(begin, BLOCK), :]
        for head in range(4):
            group = head // 2
            cols = slice(head * HD, (head + 1) * HD)
            kept = slice(group * HD, (group + 1) * HD)
            weights = jnp.exp(nt_dot(keys[:, kept], q_ref[:, cols])) * mask
            grads = nt_dot(values[:, kept], do_ref[:, cols])
            exp_ref[head, back] = weights
            dp_ref[head, back] = grads
            total_ref[head : head + 1] += jnp.sum(weights, axis=0, keepdims=True)
            inner_ref[head : head + 1] += jnp.sum(weights * grads, axis=0, keepdims=True)

    def second(back, begin):
        keys = k_ref[pl.ds(begin, BLOCK), :]
        dk_parts, dv_parts = [], []
        for group in range(2):
            dk_sum, dv_sum = None, None
            for head in (2 * group, 2 * group + 1):
                cols = slice(head * HD, (head + 1) * HD)
                scale = 1.0 / total_ref[head : head + 1]
                probs = exp_ref[head, back] * scale
                inner = inner_ref[head : head + 1] * scale
                low_scores = (probs * (dp_ref[head, back] - inner)).astype(jnp.bfloat16)
                dv_part = jnp.dot(
                    probs.astype(jnp.bfloat16), do_ref[:, cols], preferred_element_type=jnp.float32
                )
                dk_part = jnp.dot(low_scores, q_ref[:, cols], preferred_element_type=jnp.float32)
                dqt_ref[cols] += lax.dot_general(
                    keys[:, group * HD : (group + 1) * HD],
                    low_scores,
                    (((0,), (0,)), ((), ())),
                    preferred_element_type=jnp.float32,
                )
                dk_sum = dk_part if dk_sum is None else dk_sum + dk_part
                dv_sum = dv_part if dv_sum is None else dv_sum + dv_part
            dk_parts.append(dk_sum)
            dv_parts.append(dv_sum)
        dk_ref[pl.ds(begin, BLOCK), :] += jnp.concatenate(dk_parts, axis=1)
        dv_ref[pl.ds(begin, BLOCK), :] += jnp.concatenate(dv_parts, axis=1)

    each_block(first)
    each_block(second)
    dq_ref[...] = dqt_ref[...].T


def live_blocks(segment):
    count = segment.shape[0] // BLOCK
    blocks = segment.reshape(count, BLOCK)
    index = jnp.arange(count)
    return (
        (blocks[:, :1] == blocks[:, -1][None, :]) | (index[:, None] == index[None, :])
    ).astype(jnp.int32)


def attend(query, key, value, segment):
    rows = query.shape[0]
    panels, count = HK // 2, rows // BLOCK
    return pl.pallas_call(
        attend_kernel,
        out_shape=jax.ShapeDtypeStruct((rows, HQ * HD), jnp.bfloat16),
        grid_spec=pltpu.PrefetchScalarGridSpec(
            num_scalar_prefetch=1,
            grid=(panels, count),
            in_specs=[
                pl.BlockSpec((BLOCK, 4 * HD), lambda p, i, live: (i, p)),
                pl.BlockSpec((rows, 2 * HD), lambda p, i, live: (0, p)),
                pl.BlockSpec((rows, 2 * HD), lambda p, i, live: (0, p)),
                pl.BlockSpec((BLOCK, 1), lambda p, i, live: (i, 0)),
                pl.BlockSpec((1, rows), lambda p, i, live: (0, 0)),
            ],
            out_specs=pl.BlockSpec((BLOCK, 4 * HD), lambda p, i, live: (i, p)),
            scratch_shapes=[pltpu.VMEM((4, BLOCK, 2 * HD), jnp.float32)],
        ),
        cost_estimate=TINY,
        name="attend",
    )(live_blocks(segment), query, key, value, segment[:, None], segment[None, :])


def attend_back(query, grad_out, key, value, segment, start, panels):
    rows = query.shape[0]
    count = rows // BLOCK
    return pl.pallas_call(
        attend_back_kernel,
        out_shape=(
            jax.ShapeDtypeStruct((rows, panels * 4 * HD), jnp.float32),
            jax.ShapeDtypeStruct((rows, panels * 2 * HD), jnp.float32),
            jax.ShapeDtypeStruct((rows, panels * 2 * HD), jnp.float32),
        ),
        grid_spec=pltpu.PrefetchScalarGridSpec(
            num_scalar_prefetch=1,
            grid=(panels, count),
            in_specs=[
                pl.BlockSpec((BLOCK, 4 * HD), lambda p, i, live: (i, start + p)),
                pl.BlockSpec((BLOCK, 4 * HD), lambda p, i, live: (i, start + p)),
                pl.BlockSpec((rows, 2 * HD), lambda p, i, live: (0, start + p)),
                pl.BlockSpec((rows, 2 * HD), lambda p, i, live: (0, start + p)),
                pl.BlockSpec((rows, 1), lambda p, i, live: (0, 0)),
                pl.BlockSpec((1, BLOCK), lambda p, i, live: (0, i)),
            ],
            out_specs=[
                pl.BlockSpec((BLOCK, 4 * HD), lambda p, i, live: (i, p)),
                pl.BlockSpec((rows, 2 * HD), lambda p, i, live: (0, p)),
                pl.BlockSpec((rows, 2 * HD), lambda p, i, live: (0, p)),
            ],
            scratch_shapes=[
                pltpu.VMEM((4, LOOK, BLOCK, BLOCK), jnp.float32),
                pltpu.VMEM((4, LOOK, BLOCK, BLOCK), jnp.float32),
                pltpu.VMEM((8, BLOCK), jnp.float32),
                pltpu.VMEM((8, BLOCK), jnp.float32),
                pltpu.VMEM((4 * HD, BLOCK), jnp.float32),
            ],
        ),
        cost_estimate=TINY,
        name="attend_back",
    )(live_blocks(segment), query, grad_out, key, value, segment[:, None], segment[None, :])


def body(
    links,
    tokens,
    cotangent,
    segment,
    attn_gain,
    w_query,
    w_key,
    w_value,
    qk_gain,
    w_out,
    ffn_gain,
    w_gate,
    w_up,
    w_down,
):
    row_count = tokens.shape[0]
    rep_swap = links[3]
    core = lax.rem(lax.axis_index("rep"), 2)
    score_scale = 1.0 / math.sqrt(HD)
    spare = jnp.zeros((attn_gain.shape[0] - qk_gain.shape[0],), jnp.bfloat16)
    packed = jnp.stack([attn_gain, ffn_gain, jnp.concatenate([qk_gain, spare])], axis=1)
    packed = jnp.pad(packed, ((0, 0), (0, 125)))
    attn_weights = (w_query, w_key, w_value, packed)
    front_flow = Flow(
        gather_steps(
            links,
            jnp.concatenate([core_half(weight) for weight in attn_weights], axis=1),
            jnp.concatenate(attn_weights, axis=1),
            late="joined",
        )
    )
    w_out, w_gate, w_up, w_down = sync((w_out, w_gate, w_up, w_down), front_flow)
    pair = jnp.concatenate([core_half(w_gate), core_half(w_up)], axis=1)
    pair_flow = Flow(gather_steps(links, pair, None, late=True))
    w_out, w_down = sync((w_out, w_down), front_flow)
    out_flow = Flow(gather_steps(links, core_half(w_out), w_out, late="joined"))
    w_down = sync(w_down, front_flow)
    front = place_blocks(front_flow.finish())
    full_query = front[:, : HQ * HD]
    full_key = front[:, HQ * HD : (HQ + HK) * HD]
    full_value = front[:, (HQ + HK) * HD : (HQ + 2 * HK) * HD]
    gains = front[:, (HQ + 2 * HK) * HD :]
    full_attn_gain = gains[:, 0]
    full_ffn_gain = gains[:, 1]
    full_qk_gain = gains.reshape(links[0], -1, 128)[:, : qk_gain.shape[0], 2].reshape(-1)
    inputs = tokens.astype(jnp.float32)
    token_index = jnp.arange(row_count)
    same_seq = segment[:, None] == segment[None, :]
    allowed = same_seq & (token_index[None, :] <= token_index[:, None])
    positions = jnp.sum(
        (same_seq & (token_index[None, :] < token_index[:, None])).astype(jnp.float32), axis=1
    )
    live_rows = (segment >= 0).astype(jnp.float32)[:, None]
    cosine, sine_table = rope_tables(positions)
    scale_one = inv_rms(inputs)
    normed = (inputs * scale_one * full_attn_gain.astype(jnp.float32)).astype(jnp.bfloat16)
    query_lin = matmul_plain(normed, full_query).reshape(row_count, HQ, HD)
    key_lin = matmul_plain(normed, full_key).reshape(row_count, HK, HD)
    value_low = matmul_plain(normed, full_value).astype(jnp.bfloat16).reshape(row_count, HK, HD)
    qk_gains = full_qk_gain.astype(jnp.float32)
    query_scale = inv_rms(query_lin)
    key_scale = inv_rms(key_lin)
    query_rot = (
        rotate(query_lin * query_scale * qk_gains[:HD], cosine, sine_table)
        .astype(jnp.bfloat16)
    )
    key_rot = rotate(key_lin * key_scale * qk_gains[HD:], cosine, sine_table).astype(jnp.bfloat16)

    query_rot = (query_rot.astype(jnp.float32) * score_scale).astype(jnp.bfloat16)
    query_rot = query_rot.reshape(row_count, HQ * HD)
    key_rot = key_rot.reshape(row_count, HK * HD)
    value_low = value_low.reshape(row_count, HK * HD)
    query_rot, key_rot, value_low, w_down = sync(
        (query_rot, key_rot, value_low, w_down), out_flow, pair_flow
    )
    attn_low = attend(query_rot, key_rot, value_low, segment)
    attn_low, w_down = sync((attn_low, w_down), out_flow, pair_flow)
    down_flow = Flow(gather_steps(links, core_half(w_down), w_down))
    full_out = place_blocks(out_flow.finish())
    hidden = inputs + matmul_plain(attn_low, full_out)
    scale_two = inv_rms(hidden)
    normed_ffn = (hidden * scale_two * full_ffn_gain.astype(jnp.float32)).astype(jnp.bfloat16)
    normed_ffn, hidden = sync((normed_ffn, hidden), pair_flow)
    pair = pair_flow.finish()
    tiles = w_gate.shape[1] // FF_TILE
    first = ffn_forward(normed_ffn, w_gate, w_up, pair, 0, tiles // 2, None)
    normed_ffn, first = sync((normed_ffn, first), down_flow)
    mixed_act, act_low, slope = ffn_forward(
        normed_ffn, w_gate, w_up, pair, tiles // 2, tiles - tiles // 2, first
    )
    mixed_act, slope, act_low = sync((mixed_act, slope, act_low), down_flow)
    mixed_act, slope, act_low = sync((mixed_act, slope, act_low), down_flow)
    full_down = place_blocks(down_flow.finish())
    out_grad = live_rows * cotangent.astype(jnp.float32)
    out_low = out_grad.astype(jnp.bfloat16)
    grad_gate_low, grad_up_low = ffn_inner(out_low, full_down, act_low, slope)
    half = out_low.shape[1] // 2
    out_own = lax.dynamic_slice_in_dim(out_low, core * half, half, 1)
    out_other = lax.dynamic_slice_in_dim(out_low, (1 - core) * half, half, 1)
    normed_own, normed_other = pick_columns(links, normed_ffn)
    grad_up_low, grad_gate_low, out_own, out_other, mixed_act = pin(
        (grad_up_low, grad_gate_low, out_own, out_other, mixed_act)
    )

    def hand(product):
        return rep_swap(blocked(links, product).astype(jnp.bfloat16), 1)

    down_given = matmul_rows(mixed_act, out_other).astype(jnp.bfloat16)
    down_sent = hand(down_given)
    gate_given = matmul_rows(normed_other, pin(grad_gate_low, down_given)).astype(jnp.bfloat16)
    gate_sent = hand(gate_given)
    down_sent, mixed_act, grad_up_low, gate_given = pin(
        (down_sent, mixed_act, grad_up_low, gate_given)
    )
    down_given = blocked(links, matmul_rows(mixed_act, out_own).astype(jnp.bfloat16))
    down_back = Flow(scatter_steps(links, *pin((down_given, down_sent))))
    grad_up_low, grad_gate_low, normed_own, normed_other = pin(
        (grad_up_low, grad_gate_low, normed_own, normed_other), down_given
    )
    up_sent = hand(matmul_rows(normed_other, grad_up_low))
    gate_given = blocked(links, matmul_rows(normed_own, grad_gate_low).astype(jnp.bfloat16))
    up_given = blocked(links, matmul_rows(normed_own, grad_up_low).astype(jnp.bfloat16))
    gate_given, gate_sent, up_given, up_sent, grad_gate_low, grad_up_low = sync(
        (gate_given, gate_sent, up_given, up_sent, grad_gate_low, grad_up_low), down_back
    )
    gate_back = Flow(scatter_steps(links, gate_given, gate_sent))
    grad_normed_ffn = ffn_input(grad_gate_low, grad_up_low, w_gate, w_up, pair)
    grad_normed_ffn, up_given, up_sent = sync((grad_normed_ffn, up_given, up_sent), down_back)
    grad_hidden = out_grad + norm_back(
        grad_normed_ffn, hidden, scale_two, full_ffn_gain.astype(jnp.float32)
    )
    hidden_low = grad_hidden.astype(jnp.bfloat16)
    grad_attn_low = matmul_cols(hidden_low, full_out).astype(jnp.bfloat16)
    attn_own, attn_other = pick_columns(links, attn_low)
    out_sent = hand(matmul_rows(attn_other, hidden_low))
    out_given = blocked(links, matmul_rows(attn_own, hidden_low).astype(jnp.bfloat16))
    panels = HK // 4
    grad_attn_low, out_given, out_sent, up_given, up_sent = sync(
        (grad_attn_low, out_given, out_sent, up_given, up_sent), gate_back, down_back
    )
    up_back = Flow(scatter_steps(links, up_given, up_sent))
    lower = attend_back(query_rot, grad_attn_low, key_rot, value_low, segment, 0, panels)
    grad_attn_low, lower = pin((grad_attn_low, lower))
    upper = attend_back(query_rot, grad_attn_low, key_rot, value_low, segment, panels, panels)
    lower, upper, out_given, out_sent = sync(
        (lower, upper, out_given, out_sent), gate_back, down_back, up_back
    )
    out_back = Flow(scatter_steps(links, out_given, out_sent))
    grad_query_rot, grad_key_rot, grad_value = (
        jnp.concatenate(pair, axis=1) for pair in zip(lower, upper)
    )
    grad_query_rot = (score_scale * grad_query_rot).reshape(row_count, HQ, HD)
    grad_key_rot = grad_key_rot.reshape(row_count, HK, HD)
    grad_query_norm = rotate_back(grad_query_rot, cosine, sine_table)
    grad_key_norm = rotate_back(grad_key_rot, cosine, sine_table)
    grad_query_norm, grad_key_norm = sync(
        (grad_query_norm, grad_key_norm), up_back, gate_back, down_back, out_back
    )
    back_gains = full_qk_gain.astype(jnp.float32)
    grad_qk_gain = jnp.concatenate(
        [
            jnp.sum(grad_query_norm * query_lin * query_scale, axis=(0, 1)),
            jnp.sum(grad_key_norm * key_lin * key_scale, axis=(0, 1)),
        ]
    )
    grad_query_low = (
        norm_back(grad_query_norm, query_lin, query_scale, back_gains[:HD])
        .astype(jnp.bfloat16)
        .reshape(row_count, HQ * HD)
    )
    grad_key_low = (
        norm_back(grad_key_norm, key_lin, key_scale, back_gains[HD:])
        .astype(jnp.bfloat16)
        .reshape(row_count, HK * HD)
    )
    grad_value_low = grad_value.astype(jnp.bfloat16).reshape(row_count, HK * HD)
    normed_own, normed_other = pick_columns(links, normed)
    grad_front = jnp.concatenate([grad_query_low, grad_key_low, grad_value_low], axis=1)
    grad_front = sync(grad_front, up_back, gate_back, down_back, out_back)
    front_other = blocked(links, matmul_rows(normed_other, grad_front))
    front_own = blocked(links, matmul_rows(normed_own, grad_front))
    front_other, front_own = (part.astype(jnp.bfloat16) for part in (front_other, front_own))
    grad_front = pin(grad_front, front_other, front_own)
    grad_query_low = grad_front[:, : HQ * HD]
    grad_key_low = grad_front[:, HQ * HD : (HQ + HK) * HD]
    grad_value_low = grad_front[:, (HQ + HK) * HD :]
    grad_normed = (
        matmul_cols(grad_query_low, full_query)
        + matmul_cols(grad_key_low, full_key)
        + matmul_cols(grad_value_low, full_value)
    )
    qk_part = jnp.pad(
        grad_qk_gain.reshape(links[0], -1),
        ((0, 0), (0, attn_gain.shape[0] - qk_gain.shape[0])),
    )
    small = jnp.pad(qk_part.reshape(-1, 1), ((0, 0), (0, 127)))
    small = small.astype(jnp.bfloat16).reshape(links[0], 2, -1, 128)
    own_front = jnp.concatenate([front_own, lax.dynamic_slice_in_dim(small, core, 1, 1)[:, 0]], axis=2)
    other_front = jnp.concatenate(
        [front_other, lax.dynamic_slice_in_dim(small, 1 - core, 1, 1)[:, 0]], axis=2
    )
    front_sent = rep_swap(other_front, 1)
    own_front, front_sent, mixed_act, grad_normed = sync(
        (own_front, front_sent, mixed_act, grad_normed), out_back, up_back, gate_back
    )
    front_back = Flow(scatter_steps(links, own_front, front_sent))
    grad_inputs = grad_hidden + norm_back(
        grad_normed, inputs, scale_one, full_attn_gain.astype(jnp.float32)
    )
    result = live_rows * (hidden + matmul_plain(mixed_act, full_down))
    grad_inputs, result = sync((grad_inputs, result), up_back, gate_back, out_back, front_back)
    front_share = join_rows(front_back.finish())
    share_query = front_share[:, : HQ * HD]
    share_key = front_share[:, HQ * HD : (HQ + HK) * HD]
    share_value = front_share[:, (HQ + HK) * HD : (HQ + 2 * HK) * HD]
    extras = front_share[:, (HQ + 2 * HK) * HD :]
    share_qk = extras[: qk_gain.shape[0], 0]
    share_out = join_rows(out_back.finish())
    share_gate = join_rows(gate_back.finish())
    share_up = join_rows(up_back.finish())
    share_down = join_columns(down_back.finish())
    def gain_share(gain, *pairs):
        inner = sum(
            jnp.sum(weight.astype(jnp.float32) * share, axis=1) for weight, share in pairs
        )
        return inner / gain.astype(jnp.float32)

    share_again = gain_share(
        attn_gain, (w_query, share_query), (w_key, share_key), (w_value, share_value)
    )
    share_fgain = gain_share(ffn_gain, (w_gate, share_gate), (w_up, share_up))
    return (
        result.astype(jnp.bfloat16),
        grad_inputs.astype(jnp.bfloat16),
        share_again,
        share_query,
        share_key,
        share_value,
        share_qk,
        share_out,
        share_fgain,
        share_gate,
        share_up,
        share_down,
    )


def solution(mesh):
    return jax.shard_map(
        functools.partial(body, make_links(mesh)),
        mesh=mesh,
        in_specs=(
            P(("shard", "rep"), None),
            P(("shard", "rep"), None),
            P(("shard", "rep")),
            P("shard"),
            P("shard", None),
            P("shard", None),
            P("shard", None),
            P("shard"),
            P("shard", None),
            P("shard"),
            P("shard", None),
            P("shard", None),
            P("shard", None),
        ),
        out_specs=(
            P(("shard", "rep"), None),
            P(("shard", "rep"), None),
            P("shard"),
            P("shard", None),
            P("shard", None),
            P("shard", None),
            P("shard"),
            P("shard", None),
            P("shard"),
            P("shard", None),
            P("shard", None),
            P("shard", None),
        ),
        check_vma=False,
    )
```

```python
import functools
import math

import jax
import jax.numpy as jnp
from jax import lax
from jax.experimental import pallas as pl
from jax.experimental.pallas import tpu as pltpu
from jax.sharding import PartitionSpec as P

HQ = 16
HK = 8
HD = 64


norm_eps = 1e-05
TINY = pl.CostEstimate(flops=1, bytes_accessed=1, transcendentals=0)
rope_base = 1000000.0


def inv_rms(values):
    return lax.rsqrt(jnp.mean(values * values, axis=-1, keepdims=True) + norm_eps)


def rope_tables(positions):
    half_dim = HD // 2
    freq_index = jnp.arange(half_dim).astype(jnp.float32)
    freq_vals = jnp.power(rope_base, -(2.0 * freq_index) / HD)
    angles = positions[:, None] * freq_vals[None, :]
    return (jnp.cos(angles)[:, None, :], jnp.sin(angles)[:, None, :])


def rotate(values, cosine, sine_table):
    half_dim = HD // 2
    first_half = values[..., :half_dim]
    second_half = values[..., half_dim:]
    return jnp.concatenate(
        [
            first_half * cosine - second_half * sine_table,
            second_half * cosine + first_half * sine_table,
        ],
        axis=-1,
    )


def norm_back(grad_out, inputs, scale_inv, gain_vec):
    weighted = grad_out * gain_vec
    row_inner = jnp.mean(weighted * inputs, axis=-1, keepdims=True)
    return scale_inv * weighted - inputs * (scale_inv * scale_inv * scale_inv) * row_inner


def matmul_plain(left_mat, right_mat):
    return jnp.dot(left_mat, right_mat, preferred_element_type=jnp.float32)


def matmul_rows(left_mat, right_mat):
    return lax.dot_general(
        left_mat, right_mat, (((0,), (0,)), ((), ())), preferred_element_type=jnp.float32
    )


def matmul_cols(left_mat, right_mat):
    return lax.dot_general(
        left_mat, right_mat, (((1,), (1,)), ((), ())), preferred_element_type=jnp.float32
    )


def make_links(mesh):
    shard_size, rep_size = mesh.shape["shard"], mesh.shape["rep"]
    axes = ("shard", "rep")

    def shard_swap(value, bit):
        pairs = [
            (s * rep_size + r, (s ^ bit) * rep_size + r)
            for s in range(shard_size)
            for r in range(rep_size)
        ]
        return lax.ppermute(value, axes, pairs)

    def rep_swap(value, bit):
        pairs = [
            (s * rep_size + r, s * rep_size + (r ^ bit))
            for s in range(shard_size)
            for r in range(rep_size)
        ]
        return lax.ppermute(value, axes, pairs)

    return shard_size, rep_size, shard_swap, rep_swap


def add_low(left, right):
    return (left.astype(jnp.float32) + right.astype(jnp.float32)).astype(jnp.bfloat16)


def pin(values, *waits):
    return lax.optimization_barrier((values, waits))[0]


class Flow:
    def __init__(self, steps):
        self.steps = steps
        self.result = None
        self.pending = next(steps)

    def resume(self, arrived):
        try:
            self.pending = self.steps.send(arrived)
        except StopIteration as stop:
            self.pending = ()
            self.steps = None
            self.result = stop.value

    def finish(self):
        while self.steps is not None:
            self.resume(self.pending)
        return self.result


def sync(values, *flows):
    flows = [flow for flow in flows if flow.steps is not None]
    values, arrived = lax.optimization_barrier((values, [flow.pending for flow in flows]))
    for flow, got in zip(flows, arrived):
        flow.resume(got)
    return values


def place_kernel(spots_ref, *refs):
    del spots_ref
    out_ref = refs[-1]
    for at in range(len(refs) - 1):

        @pl.when(pl.program_id(0) == at)
        def _():
            out_ref[...] = refs[at][...]


def place_blocks(gathered):
    blocks, spots = gathered
    rows, width = blocks[1].shape
    count = len(blocks) + 1
    return pl.pallas_call(
        place_kernel,
        out_shape=jax.ShapeDtypeStruct((count * rows, width), blocks[0].dtype),
        grid_spec=pltpu.PrefetchScalarGridSpec(
            num_scalar_prefetch=1,
            grid=(count,),
            in_specs=[
                pl.BlockSpec((rows, width), lambda i, spot, at=at: (at, 0))
                for at in (0, 1) + (0,) * (count - 2)
            ],
            out_specs=pl.BlockSpec((rows, width), lambda i, spot: (spot[i], 0)),
        ),
        cost_estimate=TINY,
        compiler_params=pltpu.CompilerParams(vmem_limit_bytes=60 << 20),
        name="place_blocks",
    )(spots, blocks[0], *blocks)


FF_TILE = 512


def block_specs(count, rows, tiles, start=0):
    own = [
        pl.BlockSpec((rows, FF_TILE), lambda i, spot, at=at: (at, i + start)) for at in (0, 1)
    ]
    gate = [pl.BlockSpec((rows, FF_TILE), lambda i, spot: (0, i + start))] * (count - 2)
    up = [pl.BlockSpec((rows, FF_TILE), lambda i, spot: (0, i + start + tiles))] * (count - 2)
    return own + gate + own + up


def settle(spots_ref, refs, whole_ref):
    rows = refs[0].shape[0]
    for at, ref in enumerate(refs):
        begin = pl.multiple_of(spots_ref[at] * rows, rows)
        whole_ref[pl.ds(begin, rows), :] = ref[...]


def ffn_forward_kernel(count, spare, spots_ref, a_ref, *refs):
    refs = refs[: 2 * count] + refs[2 * count + spare :]
    gate_refs, up_refs = refs[:count], refs[count : 2 * count]
    z_ref, act_ref, slope_ref, gate_whole, up_whole = refs[2 * count :]
    settle(spots_ref, gate_refs, gate_whole)
    settle(spots_ref, up_refs, up_whole)
    step = min(256, a_ref.shape[0])
    for begin in range(0, a_ref.shape[0], step):
        rows = slice(begin, begin + step)
        gate = jnp.dot(a_ref[rows], gate_whole[...], preferred_element_type=jnp.float32)
        up = jnp.dot(a_ref[rows], up_whole[...], preferred_element_type=jnp.float32)
        sig = jax.nn.sigmoid(gate)
        act = gate * sig
        z_ref[rows] = (act * up).astype(jnp.bfloat16)
        act_ref[rows] = act.astype(jnp.bfloat16)
        slope_ref[rows] = (up * (sig + act * (1.0 - sig))).astype(jnp.bfloat16)


def ffn_forward(normed, gate, up, gathered, start, steps, into):
    rows, depth = normed.shape
    blocks, spots = gathered
    count = len(blocks) + 2
    hidden = gate.shape[1]
    part = gate.shape[0] // 2
    out = jax.ShapeDtypeStruct((rows, hidden), jnp.bfloat16)
    into = [] if into is None else list(into)
    first = 2 + 2 * count
    return pl.pallas_call(
        functools.partial(ffn_forward_kernel, count, len(into)),
        out_shape=(out, out, out),
        grid_spec=pltpu.PrefetchScalarGridSpec(
            num_scalar_prefetch=1,
            grid=(steps,),
            in_specs=[pl.BlockSpec((rows, depth), lambda i, spot: (0, 0))]
            + block_specs(count, part, hidden // FF_TILE, start)
            + [pl.BlockSpec(memory_space=pl.ANY)] * len(into),
            out_specs=[pl.BlockSpec((rows, FF_TILE), lambda i, spot: (0, i + start))] * 3,
            scratch_shapes=[pltpu.VMEM((depth, FF_TILE), jnp.bfloat16)] * 2,
        ),
        input_output_aliases={first + at: at for at in range(len(into))},
        cost_estimate=TINY,
        compiler_params=pltpu.CompilerParams(vmem_limit_bytes=60 << 20),
        name="ffn_forward",
    )(spots, normed, gate, gate, *blocks, up, up, *blocks, *into)


def ffn_inner_kernel(g_ref, down_ref, act_ref, slope_ref, dgate_ref, dup_ref):
    step = min(256, g_ref.shape[0])
    for begin in range(0, g_ref.shape[0], step):
        rows = slice(begin, begin + step)
        mixed = nt_dot(g_ref[rows], down_ref[...])
        dgate_ref[rows] = (mixed * slope_ref[rows].astype(jnp.float32)).astype(jnp.bfloat16)
        dup_ref[rows] = (mixed * act_ref[rows].astype(jnp.float32)).astype(jnp.bfloat16)


def ffn_inner(grad_low, down, act, slope):
    rows, depth = grad_low.shape
    hidden = down.shape[0]
    out = jax.ShapeDtypeStruct((rows, hidden), jnp.bfloat16)
    tile = pl.BlockSpec((rows, FF_TILE), lambda i: (0, i))
    return pl.pallas_call(
        ffn_inner_kernel,
        out_shape=(out, out),
        grid=(hidden // FF_TILE,),
        in_specs=[
            pl.BlockSpec((rows, depth), lambda i: (0, 0)),
            pl.BlockSpec((FF_TILE, depth), lambda i: (i, 0)),
            tile,
            tile,
        ],
        out_specs=[tile, tile],
        cost_estimate=TINY,
        compiler_params=pltpu.CompilerParams(vmem_limit_bytes=60 << 20),
        name="ffn_inner",
    )(grad_low, down, act, slope)


def ffn_input_kernel(count, spots_ref, dgate_ref, dup_ref, *refs):
    gate_refs, up_refs = refs[:count], refs[count : 2 * count]
    out_ref, gate_whole, up_whole = refs[2 * count :]
    settle(spots_ref, gate_refs, gate_whole)
    settle(spots_ref, up_refs, up_whole)

    @pl.when(pl.program_id(0) == 0)
    def _():
        out_ref[...] = jnp.zeros_like(out_ref)

    step = min(256, dgate_ref.shape[0])
    for begin in range(0, dgate_ref.shape[0], step):
        rows = slice(begin, begin + step)
        out_ref[rows] += nt_dot(dgate_ref[rows], gate_whole[...]) + nt_dot(
            dup_ref[rows], up_whole[...]
        )


def ffn_input(grad_gate, grad_up, gate, up, gathered):
    rows, hidden = grad_gate.shape
    blocks, spots = gathered
    count = len(blocks) + 2
    part = gate.shape[0] // 2
    depth = count * part
    tile = pl.BlockSpec((rows, FF_TILE), lambda i, spot: (0, i))
    return pl.pallas_call(
        functools.partial(ffn_input_kernel, count),
        out_shape=jax.ShapeDtypeStruct((rows, depth), jnp.float32),
        grid_spec=pltpu.PrefetchScalarGridSpec(
            num_scalar_prefetch=1,
            grid=(hidden // FF_TILE,),
            in_specs=[tile, tile] + block_specs(count, part, hidden // FF_TILE),
            out_specs=pl.BlockSpec((rows, depth), lambda i, spot: (0, 0)),
            scratch_shapes=[pltpu.VMEM((depth, FF_TILE), jnp.bfloat16)] * 2,
        ),
        cost_estimate=TINY,
        compiler_params=pltpu.CompilerParams(vmem_limit_bytes=60 << 20),
        name="ffn_input",
    )(spots, grad_gate, grad_up, gate, gate, *blocks, up, up, *blocks)


def gather_steps(links, mine, whole, late=False):
    shard_size, rep_size, shard_swap, rep_swap = links
    me = lax.axis_index("shard")
    core = lax.rem(lax.axis_index("rep"), 2)
    half, width = mine.shape
    quarter = half // 2
    pieces, others = {}, {}
    if shard_size == 4:
        pieces[1] = shard_swap(mine, 1)
        pieces[2] = shard_swap(mine, 2)
        pieces[1], pieces[2] = yield (pieces[1], pieces[2])
        corner_a = shard_swap(pieces[1][:quarter], 2)
        corner_b = shard_swap(pieces[2][quarter:], 1)
        if late:
            early, waiting = (), (1, 2, 3)
            corner_a, corner_b, pieces[1], pieces[2] = yield (
                corner_a, corner_b, pieces[1], pieces[2]
            )
        else:
            early, waiting = (rep_swap(pieces[1], 1), rep_swap(pieces[2], 1)), (3,)
            corner_a, corner_b, *early = yield (corner_a, corner_b, *early)
        pieces[3] = jnp.concatenate([corner_a, corner_b], axis=0)
        if late == "joined":
            joined = jnp.stack([pieces[1], pieces[2], pieces[3]])
            (got,) = yield (rep_swap(joined, 1),)
            others = {d: got[d - 1] for d in (1, 2, 3)}
        else:
            rest = yield tuple(rep_swap(pieces[d], 1) for d in waiting)
            others = dict(zip((1, 2, 3), (*early, *rest)))
    else:
        pieces[0] = mine
        bit = 1
        while bit < shard_size:
            order = sorted(pieces)
            got = shard_swap(jnp.stack([pieces[d] for d in order]), bit)
            (got,) = yield (got,)
            for at, d in enumerate(order):
                pieces[d ^ bit] = got[at]
            bit *= 2
        del pieces[0]
        others = {d: rep_swap(piece, 1) for d, piece in pieces.items()}
    blocks, spots = [whole] if whole is not None else [], [2 * me, 2 * me + 1]
    for d in pieces:
        blocks += [pieces[d], others[d]]
        spots += [2 * (me ^ d) + core, 2 * (me ^ d) + 1 - core]
    return blocks, jnp.stack(spots).astype(jnp.int32)


def core_half(weight):
    core = lax.rem(lax.axis_index("rep"), 2)
    half = weight.shape[0] // 2
    return lax.dynamic_slice_in_dim(weight, core * half, half, 0)


def pick_columns(links, value):
    core = lax.rem(lax.axis_index("rep"), 2)
    width = value.shape[1] // links[0] // 2

    def half(which):
        return jnp.concatenate(
            [
                lax.dynamic_slice_in_dim(value, (2 * d + which) * width, width, 1)
                for d in range(links[0])
            ],
            axis=1,
        )

    return half(core), half(1 - core)


def blocked(links, product):
    return product.reshape(links[0], -1, product.shape[1])


def scatter_steps(links, own, received):
    shard_size, rep_size, shard_swap, rep_swap = links
    me = lax.axis_index("shard")
    rep = lax.axis_index("rep")
    rows = own.shape[1] // 2

    def piece(d, at):
        begin, extent = (me ^ d, at * rows, 0), (1, rows, own.shape[2])
        return add_low(
            lax.dynamic_slice(own, begin, extent)[0],
            lax.dynamic_slice(received, begin, extent)[0],
        )

    if shard_size == 4:
        got_a = shard_swap(jnp.stack([piece(1, 0), piece(3, 0)]), 1)
        got_b = shard_swap(jnp.stack([piece(2, 1), piece(3, 1)]), 2)
        got_a, got_b = yield (got_a, got_b)
        pass_a = shard_swap(add_low(piece(2, 0), got_a[1]), 2)
        pass_b = shard_swap(add_low(piece(1, 1), got_b[1]), 1)
        pass_a, pass_b = yield (pass_a, pass_b)
        sum_a = add_low(piece(0, 0).astype(jnp.float32) + got_a[0].astype(jnp.float32), pass_a)
        sum_b = add_low(piece(0, 1).astype(jnp.float32) + got_b[0].astype(jnp.float32), pass_b)
        halves = [sum_a, sum_b]
    else:
        held = {d: jnp.stack([piece(d, 0), piece(d, 1)]) for d in range(shard_size)}
        bit = shard_size // 2
        while bit:
            sent = [d for d in sorted(held) if d & bit]
            got = shard_swap(jnp.stack([held[d] for d in sent]), bit)
            (got,) = yield (got,)
            held = {d ^ bit: add_low(held[d ^ bit], got[at]) for at, d in enumerate(sent)}
            bit //= 2
        halves = [held[0][0], held[0][1]]
    upper = lax.rem(rep // 2, 2) == 1
    if rep_size >= 8:
        keep = jnp.where(upper, halves[1], halves[0])
        send = jnp.where(upper, halves[0], halves[1])
        got = rep_swap(send, 2)
        (got,) = yield (got,)
        keep = add_low(keep, got)
        bit = 4
        while bit < rep_size:
            got = rep_swap(keep, bit)
            (got,) = yield (got,)
            keep = add_low(keep, got)
            bit *= 2
        back = rep_swap(keep, 2)
        (back,) = yield (back,)
        halves = [jnp.where(upper, back, keep), jnp.where(upper, keep, back)]
        half = jnp.concatenate(halves, axis=0)
    else:
        half = jnp.concatenate(halves, axis=0)
        bit = 2
        while bit < rep_size:
            half = add_low(half, rep_swap(half, bit))
            bit *= 2
    other = rep_swap(half, 1)
    (other,) = yield (other,)
    return half, other


def join_rows(pair):
    core = lax.rem(lax.axis_index("rep"), 2)
    half, other = pair
    return jnp.where(
        core == 0,
        jnp.concatenate([half, other], axis=0),
        jnp.concatenate([other, half], axis=0),
    ).astype(jnp.float32)


def join_columns(pair):
    core = lax.rem(lax.axis_index("rep"), 2)
    half, other = pair
    return jnp.where(
        core == 0,
        jnp.concatenate([half, other], axis=1),
        jnp.concatenate([other, half], axis=1),
    ).astype(jnp.float32)


BLOCK = 256
LOOK = 3


def nt_dot(left_mat, right_mat):
    return lax.dot_general(
        left_mat, right_mat, (((1,), (1,)), ((), ())), preferred_element_type=jnp.float32
    )


def attend_kernel(live_ref, q_ref, k_ref, v_ref, seg_col_ref, seg_row_ref, o_ref, acc_ref):
    at = pl.program_id(1)
    acc_ref[...] = jnp.zeros_like(acc_ref)
    lane = lax.broadcasted_iota(jnp.int32, (BLOCK, 2 * HD), 1)
    low_lane = lane < HD
    for back in range(LOOK):
        key_block = jnp.maximum(at - back, 0)

        @pl.when((at >= back) & (live_ref[at, key_block] > 0))
        def _():
            begin = pl.multiple_of(key_block * BLOCK, BLOCK)
            same = seg_col_ref[...] == seg_row_ref[:, pl.ds(begin, BLOCK)]
            if back == 0:
                row = lax.broadcasted_iota(jnp.int32, (BLOCK, BLOCK), 0)
                col = lax.broadcasted_iota(jnp.int32, (BLOCK, BLOCK), 1)
                same = same & (col <= row)
            mask = same.astype(jnp.float32)
            keys = k_ref[pl.ds(begin, BLOCK), :]
            values = v_ref[pl.ds(begin, BLOCK), :]
            swapped = pltpu.roll(values.astype(jnp.float32), HD, 1).astype(jnp.bfloat16)
            one = jnp.ones_like(values)
            for head in range(4):
                group, odd = head // 2, head % 2
                scores = nt_dot(
                    q_ref[:, head * HD : (head + 1) * HD], keys[:, group * HD : (group + 1) * HD]
                )
                weights = (jnp.exp(scores) * mask).astype(jnp.bfloat16)
                held = values if group == odd else swapped
                padded = jnp.where(low_lane, held, one) if odd == 0 else jnp.where(low_lane, one, held)
                acc_ref[head] += jnp.dot(weights, padded, preferred_element_type=jnp.float32)

    for group in range(2):
        even, odd = acc_ref[2 * group], acc_ref[2 * group + 1]
        top = jnp.where(low_lane, even, odd)
        total = pltpu.roll(jnp.where(low_lane, odd, even), HD, 1)
        o_ref[:, group * 2 * HD : (group + 1) * 2 * HD] = (top / total).astype(o_ref.dtype)


def head_norm_back(grad, linear, turn, gain):
    half = HD // 2
    cosine, sine = turn[:half], turn[half:]
    gain_1, gain_2 = gain[:half], gain[half:]
    parts, sums = [], None
    for begin in range(0, grad.shape[0], HD):
        grad_1, grad_2 = grad[begin : begin + half], grad[begin + half : begin + HD]
        lin_1, lin_2 = linear[begin : begin + half], linear[begin + half : begin + HD]
        back_1 = grad_1 * cosine + grad_2 * sine
        back_2 = grad_2 * cosine - grad_1 * sine
        square = jnp.sum(lin_1 * lin_1 + lin_2 * lin_2, axis=0, keepdims=True)
        scale = lax.rsqrt(square * (1.0 / HD) + norm_eps)
        unit_1, unit_2 = lin_1 * scale, lin_2 * scale
        both = jnp.concatenate([back_1 * unit_1, back_2 * unit_2], axis=0)
        sums = both if sums is None else sums + both
        back_1, back_2 = back_1 * gain_1, back_2 * gain_2
        inner = jnp.sum(back_1 * unit_1 + back_2 * unit_2, axis=0, keepdims=True) * (1.0 / HD)
        parts += [scale * (back_1 - unit_1 * inner), scale * (back_2 - unit_2 * inner)]
    return jnp.concatenate(parts, axis=0), sums


def attend_back_kernel(
    live_ref, q_ref, do_ref, k_ref, v_ref, seg_col_ref, seg_row_ref,
    q_lin_ref, k_lin_ref, q_turn_ref, k_turn_ref, gain_ref,
    dq_out_ref, dk_out_ref, dv_out_ref, q_gain_ref, k_gain_ref,
    exp_ref, dp_ref, total_ref, inner_ref, dqt_ref, dk_ref, dv_ref,
):
    at = pl.program_id(1)

    @pl.when(at == 0)
    def _():
        dk_ref[...] = jnp.zeros_like(dk_ref)
        dv_ref[...] = jnp.zeros_like(dv_ref)
        q_gain_ref[...] = jnp.zeros_like(q_gain_ref)

    total_ref[...] = jnp.zeros_like(total_ref)
    inner_ref[...] = jnp.zeros_like(inner_ref)
    dqt_ref[...] = jnp.zeros_like(dqt_ref)

    def each_block(run):
        for back in range(LOOK):
            key_block = jnp.maximum(at - back, 0)

            @pl.when((at >= back) & (live_ref[at, key_block] > 0))
            def _():
                run(back, pl.multiple_of(key_block * BLOCK, BLOCK))

    def first(back, begin):
        same = seg_col_ref[pl.ds(begin, BLOCK), :] == seg_row_ref[...]
        if back == 0:
            row = lax.broadcasted_iota(jnp.int32, (BLOCK, BLOCK), 0)
            col = lax.broadcasted_iota(jnp.int32, (BLOCK, BLOCK), 1)
            same = same & (row <= col)
        mask = same.astype(jnp.float32)
        keys = k_ref[pl.ds(begin, BLOCK), :]
        values = v_ref[pl.ds(begin, BLOCK), :]
        for head in range(4):
            group = head // 2
            cols = slice(head * HD, (head + 1) * HD)
            kept = slice(group * HD, (group + 1) * HD)
            weights = jnp.exp(nt_dot(keys[:, kept], q_ref[:, cols])) * mask
            grads = nt_dot(values[:, kept], do_ref[:, cols])
            exp_ref[head, back] = weights
            dp_ref[head, back] = grads
            total_ref[head : head + 1] += jnp.sum(weights, axis=0, keepdims=True)
            inner_ref[head : head + 1] += jnp.sum(weights * grads, axis=0, keepdims=True)

    def second(back, begin):
        keys = k_ref[pl.ds(begin, BLOCK), :]
        dk_parts, dv_parts = [], []
        for group in range(2):
            dk_sum, dv_sum = None, None
            for head in (2 * group, 2 * group + 1):
                cols = slice(head * HD, (head + 1) * HD)
                scale = 1.0 / total_ref[head : head + 1]
                probs = exp_ref[head, back] * scale
                inner = inner_ref[head : head + 1] * scale
                low_scores = (probs * (dp_ref[head, back] - inner)).astype(jnp.bfloat16)
                dv_part = jnp.dot(
                    probs.astype(jnp.bfloat16), do_ref[:, cols], preferred_element_type=jnp.float32
                )
                dk_part = jnp.dot(low_scores, q_ref[:, cols], preferred_element_type=jnp.float32)
                dqt_ref[cols] += lax.dot_general(
                    keys[:, group * HD : (group + 1) * HD],
                    low_scores,
                    (((0,), (0,)), ((), ())),
                    preferred_element_type=jnp.float32,
                )
                dk_sum = dk_part if dk_sum is None else dk_sum + dk_part
                dv_sum = dv_part if dv_sum is None else dv_sum + dv_part
            dk_parts.append(dk_sum)
            dv_parts.append(dv_sum)
        dk_ref[pl.ds(begin, BLOCK), :] += jnp.concatenate(dk_parts, axis=1)
        dv_ref[pl.ds(begin, BLOCK), :] += jnp.concatenate(dv_parts, axis=1)

    each_block(first)
    each_block(second)
    grad, gain_sum = head_norm_back(
        dqt_ref[...] * (1.0 / math.sqrt(HD)), q_lin_ref[...].T, q_turn_ref[...], gain_ref[:HD]
    )
    q_gain_ref[0] += gain_sum
    dq_out_ref[...] = grad.T.astype(jnp.bfloat16)

    @pl.when(at == pl.num_programs(1) - 1)
    def _():
        dv_out_ref[...] = dv_ref[...].astype(jnp.bfloat16)
        key_sum = None
        for begin in range(0, dk_ref.shape[0], BLOCK):
            rows = slice(begin, begin + BLOCK)
            grad, gain_sum = head_norm_back(
                dk_ref[rows].T, k_lin_ref[rows].T, k_turn_ref[:, rows], gain_ref[HD:]
            )
            dk_out_ref[rows] = grad.T.astype(jnp.bfloat16)
            key_sum = gain_sum if key_sum is None else key_sum + gain_sum
        k_gain_ref[0] = key_sum


def live_blocks(segment):
    count = segment.shape[0] // BLOCK
    blocks = segment.reshape(count, BLOCK)
    index = jnp.arange(count)
    return (
        (blocks[:, :1] == blocks[:, -1][None, :]) | (index[:, None] == index[None, :])
    ).astype(jnp.int32)


def attend(query, key, value, segment):
    rows = query.shape[0]
    panels, count = HK // 2, rows // BLOCK
    return pl.pallas_call(
        attend_kernel,
        out_shape=jax.ShapeDtypeStruct((rows, HQ * HD), jnp.bfloat16),
        grid_spec=pltpu.PrefetchScalarGridSpec(
            num_scalar_prefetch=1,
            grid=(panels, count),
            in_specs=[
                pl.BlockSpec((BLOCK, 4 * HD), lambda p, i, live: (i, p)),
                pl.BlockSpec((rows, 2 * HD), lambda p, i, live: (0, p)),
                pl.BlockSpec((rows, 2 * HD), lambda p, i, live: (0, p)),
                pl.BlockSpec((BLOCK, 1), lambda p, i, live: (i, 0)),
                pl.BlockSpec((1, rows), lambda p, i, live: (0, 0)),
            ],
            out_specs=pl.BlockSpec((BLOCK, 4 * HD), lambda p, i, live: (i, p)),
            scratch_shapes=[pltpu.VMEM((4, BLOCK, 2 * HD), jnp.float32)],
        ),
        cost_estimate=TINY,
        name="attend",
    )(live_blocks(segment), query, key, value, segment[:, None], segment[None, :])


def attend_back(query, grad_out, key, value, segment, query_lin, key_lin, turn, gain, start, panels):
    rows = query.shape[0]
    count = rows // BLOCK
    return pl.pallas_call(
        attend_back_kernel,
        out_shape=(
            jax.ShapeDtypeStruct((rows, panels * 4 * HD), jnp.bfloat16),
            jax.ShapeDtypeStruct((rows, panels * 2 * HD), jnp.bfloat16),
            jax.ShapeDtypeStruct((rows, panels * 2 * HD), jnp.bfloat16),
            jax.ShapeDtypeStruct((panels, HD, BLOCK), jnp.float32),
            jax.ShapeDtypeStruct((panels, HD, BLOCK), jnp.float32),
        ),
        grid_spec=pltpu.PrefetchScalarGridSpec(
            num_scalar_prefetch=1,
            grid=(panels, count),
            in_specs=[
                pl.BlockSpec((BLOCK, 4 * HD), lambda p, i, live: (i, start + p)),
                pl.BlockSpec((BLOCK, 4 * HD), lambda p, i, live: (i, start + p)),
                pl.BlockSpec((rows, 2 * HD), lambda p, i, live: (0, start + p)),
                pl.BlockSpec((rows, 2 * HD), lambda p, i, live: (0, start + p)),
                pl.BlockSpec((rows, 1), lambda p, i, live: (0, 0)),
                pl.BlockSpec((1, BLOCK), lambda p, i, live: (0, i)),
                pl.BlockSpec((BLOCK, 4 * HD), lambda p, i, live: (i, start + p)),
                pl.BlockSpec((rows, 2 * HD), lambda p, i, live: (0, start + p)),
                pl.BlockSpec((HD, BLOCK), lambda p, i, live: (0, i)),
                pl.BlockSpec((HD, rows), lambda p, i, live: (0, 0)),
                pl.BlockSpec((2 * HD, 1), lambda p, i, live: (0, 0)),
            ],
            out_specs=[
                pl.BlockSpec((BLOCK, 4 * HD), lambda p, i, live: (i, p)),
                pl.BlockSpec((rows, 2 * HD), lambda p, i, live: (0, p)),
                pl.BlockSpec((rows, 2 * HD), lambda p, i, live: (0, p)),
                pl.BlockSpec((1, HD, BLOCK), lambda p, i, live: (p, 0, 0)),
                pl.BlockSpec((1, HD, BLOCK), lambda p, i, live: (p, 0, 0)),
            ],
            scratch_shapes=[
                pltpu.VMEM((4, LOOK, BLOCK, BLOCK), jnp.float32),
                pltpu.VMEM((4, LOOK, BLOCK, BLOCK), jnp.float32),
                pltpu.VMEM((8, BLOCK), jnp.float32),
                pltpu.VMEM((8, BLOCK), jnp.float32),
                pltpu.VMEM((4 * HD, BLOCK), jnp.float32),
                pltpu.VMEM((rows, 2 * HD), jnp.float32),
                pltpu.VMEM((rows, 2 * HD), jnp.float32),
            ],
        ),
        cost_estimate=TINY,
        name="attend_back",
    )(live_blocks(segment), query, grad_out, key, value, segment[:, None], segment[None, :],
      query_lin, key_lin, turn, turn, gain)


def body(
    links,
    tokens,
    cotangent,
    segment,
    attn_gain,
    w_query,
    w_key,
    w_value,
    qk_gain,
    w_out,
    ffn_gain,
    w_gate,
    w_up,
    w_down,
):
    row_count = tokens.shape[0]
    rep_swap = links[3]
    core = lax.rem(lax.axis_index("rep"), 2)
    score_scale = 1.0 / math.sqrt(HD)
    spare = jnp.zeros((attn_gain.shape[0] - qk_gain.shape[0],), jnp.bfloat16)
    packed = jnp.stack([attn_gain, ffn_gain, jnp.concatenate([qk_gain, spare])], axis=1)
    packed = jnp.pad(packed, ((0, 0), (0, 125)))
    attn_weights = (w_query, w_key, w_value, packed)
    front_flow = Flow(
        gather_steps(
            links,
            jnp.concatenate([core_half(weight) for weight in attn_weights], axis=1),
            jnp.concatenate(attn_weights, axis=1),
            late="joined",
        )
    )
    w_out, w_gate, w_up, w_down = sync((w_out, w_gate, w_up, w_down), front_flow)
    out_flow = Flow(gather_steps(links, core_half(w_out), w_out, late="joined"))
    w_gate, w_up, w_down = sync((w_gate, w_up, w_down), front_flow)
    pair = jnp.concatenate([core_half(w_gate), core_half(w_up)], axis=1)
    pair_flow = Flow(gather_steps(links, pair, None, late=True))
    w_down = sync(w_down, front_flow)
    front = place_blocks(front_flow.finish())
    full_query = front[:, : HQ * HD]
    full_key = front[:, HQ * HD : (HQ + HK) * HD]
    full_value = front[:, (HQ + HK) * HD : (HQ + 2 * HK) * HD]
    gains = front[:, (HQ + 2 * HK) * HD :]
    full_attn_gain = gains[:, 0]
    full_ffn_gain = gains[:, 1]
    full_qk_gain = gains.reshape(links[0], -1, 128)[:, : qk_gain.shape[0], 2].reshape(-1)
    inputs = tokens.astype(jnp.float32)
    token_index = jnp.arange(row_count)
    same_seq = segment[:, None] == segment[None, :]
    allowed = same_seq & (token_index[None, :] <= token_index[:, None])
    positions = jnp.sum(
        (same_seq & (token_index[None, :] < token_index[:, None])).astype(jnp.float32), axis=1
    )
    live_rows = (segment >= 0).astype(jnp.float32)[:, None]
    cosine, sine_table = rope_tables(positions)
    scale_one = inv_rms(inputs)
    normed = (inputs * scale_one * full_attn_gain.astype(jnp.float32)).astype(jnp.bfloat16)
    query_lin = matmul_plain(normed, full_query).reshape(row_count, HQ, HD)
    key_lin = matmul_plain(normed, full_key).reshape(row_count, HK, HD)
    value_low = matmul_plain(normed, full_value).astype(jnp.bfloat16).reshape(row_count, HK, HD)
    qk_gains = full_qk_gain.astype(jnp.float32)
    query_scale = inv_rms(query_lin)
    key_scale = inv_rms(key_lin)
    query_rot = (
        rotate(query_lin * query_scale * qk_gains[:HD], cosine, sine_table)
        .astype(jnp.bfloat16)
    )
    key_rot = rotate(key_lin * key_scale * qk_gains[HD:], cosine, sine_table).astype(jnp.bfloat16)

    query_rot = (query_rot.astype(jnp.float32) * score_scale).astype(jnp.bfloat16)
    query_rot = query_rot.reshape(row_count, HQ * HD)
    key_rot = key_rot.reshape(row_count, HK * HD)
    value_low = value_low.reshape(row_count, HK * HD)
    query_rot, key_rot, value_low, w_down = sync(
        (query_rot, key_rot, value_low, w_down), out_flow
    )
    attn_low = attend(query_rot, key_rot, value_low, segment)
    attn_low, w_down = sync((attn_low, w_down), out_flow, pair_flow)
    down_flow = Flow(gather_steps(links, core_half(w_down), w_down))
    full_out = place_blocks(out_flow.finish())
    hidden = inputs + matmul_plain(attn_low, full_out)
    scale_two = inv_rms(hidden)
    normed_ffn = (hidden * scale_two * full_ffn_gain.astype(jnp.float32)).astype(jnp.bfloat16)
    normed_ffn, hidden = sync((normed_ffn, hidden), pair_flow)
    pair = pair_flow.finish()
    tiles = w_gate.shape[1] // FF_TILE
    first = ffn_forward(normed_ffn, w_gate, w_up, pair, 0, tiles // 2, None)
    normed_ffn, first = sync((normed_ffn, first), down_flow)
    mixed_act, act_low, slope = ffn_forward(
        normed_ffn, w_gate, w_up, pair, tiles // 2, tiles - tiles // 2, first
    )
    mixed_act, slope, act_low = sync((mixed_act, slope, act_low), down_flow)
    mixed_act, slope, act_low = sync((mixed_act, slope, act_low), down_flow)
    full_down = place_blocks(down_flow.finish())
    out_grad = live_rows * cotangent.astype(jnp.float32)
    out_low = out_grad.astype(jnp.bfloat16)
    grad_gate_low, grad_up_low = ffn_inner(out_low, full_down, act_low, slope)
    half = out_low.shape[1] // 2
    out_own = lax.dynamic_slice_in_dim(out_low, core * half, half, 1)
    out_other = lax.dynamic_slice_in_dim(out_low, (1 - core) * half, half, 1)
    normed_own, normed_other = pick_columns(links, normed_ffn)
    grad_up_low, grad_gate_low, out_own, out_other, mixed_act = pin(
        (grad_up_low, grad_gate_low, out_own, out_other, mixed_act)
    )

    def hand(product):
        return rep_swap(blocked(links, product).astype(jnp.bfloat16), 1)

    down_given = matmul_rows(mixed_act, out_other).astype(jnp.bfloat16)
    down_sent = hand(down_given)
    gate_given = matmul_rows(normed_other, pin(grad_gate_low, down_given)).astype(jnp.bfloat16)
    gate_sent = hand(gate_given)
    down_sent, mixed_act, grad_up_low, gate_given = pin(
        (down_sent, mixed_act, grad_up_low, gate_given)
    )
    down_given = blocked(links, matmul_rows(mixed_act, out_own).astype(jnp.bfloat16))
    down_back = Flow(scatter_steps(links, *pin((down_given, down_sent))))
    grad_up_low, grad_gate_low, normed_own, normed_other = pin(
        (grad_up_low, grad_gate_low, normed_own, normed_other), down_given
    )
    up_sent = hand(matmul_rows(normed_other, grad_up_low))
    gate_given = blocked(links, matmul_rows(normed_own, grad_gate_low).astype(jnp.bfloat16))
    up_given = blocked(links, matmul_rows(normed_own, grad_up_low).astype(jnp.bfloat16))
    gate_given, gate_sent, up_given, up_sent, grad_gate_low, grad_up_low = sync(
        (gate_given, gate_sent, up_given, up_sent, grad_gate_low, grad_up_low), down_back
    )
    gate_back = Flow(scatter_steps(links, gate_given, gate_sent))
    grad_normed_ffn = ffn_input(grad_gate_low, grad_up_low, w_gate, w_up, pair)
    grad_normed_ffn, up_given, up_sent = sync((grad_normed_ffn, up_given, up_sent), down_back)
    grad_hidden = out_grad + norm_back(
        grad_normed_ffn, hidden, scale_two, full_ffn_gain.astype(jnp.float32)
    )
    hidden_low = grad_hidden.astype(jnp.bfloat16)
    grad_attn_low = matmul_cols(hidden_low, full_out).astype(jnp.bfloat16)
    attn_own, attn_other = pick_columns(links, attn_low)
    out_sent = hand(matmul_rows(attn_other, hidden_low))
    out_given = blocked(links, matmul_rows(attn_own, hidden_low).astype(jnp.bfloat16))
    panels = HK // 4
    grad_attn_low, out_given, out_sent, up_given, up_sent = sync(
        (grad_attn_low, out_given, out_sent, up_given, up_sent), gate_back, down_back
    )
    up_back = Flow(scatter_steps(links, up_given, up_sent))
    turn = jnp.concatenate([cosine[:, 0].T, sine_table[:, 0].T], axis=0)
    flat = (query_lin.reshape(row_count, -1), key_lin.reshape(row_count, -1), turn, qk_gains[:, None])
    lower = attend_back(query_rot, grad_attn_low, key_rot, value_low, segment, *flat, 0, panels)
    grad_attn_low, lower = pin((grad_attn_low, lower))
    upper = attend_back(query_rot, grad_attn_low, key_rot, value_low, segment, *flat, panels, panels)
    lower, upper, out_given, out_sent = sync(
        (lower, upper, out_given, out_sent), gate_back, down_back, up_back
    )
    out_back = Flow(scatter_steps(links, out_given, out_sent))
    grad_qk_gain = jnp.concatenate(
        [jnp.sum(lower[at] + upper[at], axis=(0, 2)) for at in (3, 4)]
    )
    grad_front = jnp.concatenate([part for at in range(3) for part in (lower[at], upper[at])], axis=1)
    normed_own, normed_other = pick_columns(links, normed)
    front_other = blocked(links, matmul_rows(normed_other, grad_front))
    front_own = blocked(links, matmul_rows(normed_own, grad_front))
    front_other, front_own = (part.astype(jnp.bfloat16) for part in (front_other, front_own))
    grad_front = pin(grad_front, front_other, front_own)
    grad_query_low = grad_front[:, : HQ * HD]
    grad_key_low = grad_front[:, HQ * HD : (HQ + HK) * HD]
    grad_value_low = grad_front[:, (HQ + HK) * HD :]
    grad_normed = (
        matmul_cols(grad_query_low, full_query)
        + matmul_cols(grad_key_low, full_key)
        + matmul_cols(grad_value_low, full_value)
    )
    qk_part = jnp.pad(
        grad_qk_gain.reshape(links[0], -1),
        ((0, 0), (0, attn_gain.shape[0] - qk_gain.shape[0])),
    )
    small = jnp.pad(qk_part.reshape(-1, 1), ((0, 0), (0, 127)))
    small = small.astype(jnp.bfloat16).reshape(links[0], 2, -1, 128)
    own_front = jnp.concatenate([front_own, lax.dynamic_slice_in_dim(small, core, 1, 1)[:, 0]], axis=2)
    other_front = jnp.concatenate(
        [front_other, lax.dynamic_slice_in_dim(small, 1 - core, 1, 1)[:, 0]], axis=2
    )
    front_sent = rep_swap(other_front, 1)
    own_front, front_sent, mixed_act, grad_normed = sync(
        (own_front, front_sent, mixed_act, grad_normed), out_back, up_back, gate_back
    )
    front_back = Flow(scatter_steps(links, own_front, front_sent))
    grad_inputs = grad_hidden + norm_back(
        grad_normed, inputs, scale_one, full_attn_gain.astype(jnp.float32)
    )
    result = live_rows * (hidden + matmul_plain(mixed_act, full_down))
    grad_inputs, result = sync((grad_inputs, result), up_back, gate_back, out_back, front_back)
    front_share = join_rows(front_back.finish())
    share_query = front_share[:, : HQ * HD]
    share_key = front_share[:, HQ * HD : (HQ + HK) * HD]
    share_value = front_share[:, (HQ + HK) * HD : (HQ + 2 * HK) * HD]
    extras = front_share[:, (HQ + 2 * HK) * HD :]
    share_qk = extras[: qk_gain.shape[0], 0]
    share_out = join_rows(out_back.finish())
    share_gate = join_rows(gate_back.finish())
    share_up = join_rows(up_back.finish())
    share_down = join_columns(down_back.finish())
    def gain_share(gain, *pairs):
        inner = sum(
            jnp.sum(weight.astype(jnp.float32) * share, axis=1) for weight, share in pairs
        )
        return inner / gain.astype(jnp.float32)

    share_again = gain_share(
        attn_gain, (w_query, share_query), (w_key, share_key), (w_value, share_value)
    )
    share_fgain = gain_share(ffn_gain, (w_gate, share_gate), (w_up, share_up))
    return (
        result.astype(jnp.bfloat16),
        grad_inputs.astype(jnp.bfloat16),
        share_again,
        share_query,
        share_key,
        share_value,
        share_qk,
        share_out,
        share_fgain,
        share_gate,
        share_up,
        share_down,
    )


def solution(mesh):
    return jax.shard_map(
        functools.partial(body, make_links(mesh)),
        mesh=mesh,
        in_specs=(
            P(("shard", "rep"), None),
            P(("shard", "rep"), None),
            P(("shard", "rep")),
            P("shard"),
            P("shard", None),
            P("shard", None),
            P("shard", None),
            P("shard"),
            P("shard", None),
            P("shard"),
            P("shard", None),
            P("shard", None),
            P("shard", None),
        ),
        out_specs=(
            P(("shard", "rep"), None),
            P(("shard", "rep"), None),
            P("shard"),
            P("shard", None),
            P("shard", None),
            P("shard", None),
            P("shard"),
            P("shard", None),
            P("shard"),
            P("shard", None),
            P("shard", None),
            P("shard", None),
        ),
        check_vma=False,
    )
```

```python
import functools
import math

import jax
import jax.numpy as jnp
from jax import lax
from jax.experimental import pallas as pl
from jax.experimental.pallas import tpu as pltpu
from jax.sharding import PartitionSpec as P

HQ = 16
HK = 8
HD = 64


norm_eps = 1e-05
TINY = pl.CostEstimate(flops=1, bytes_accessed=1, transcendentals=0)
rope_base = 1000000.0


def inv_rms(values):
    return lax.rsqrt(jnp.mean(values * values, axis=-1, keepdims=True) + norm_eps)


def rope_tables(positions):
    half_dim = HD // 2
    freq_index = jnp.arange(half_dim).astype(jnp.float32)
    freq_vals = jnp.power(rope_base, -(2.0 * freq_index) / HD)
    angles = positions[:, None] * freq_vals[None, :]
    return (jnp.cos(angles)[:, None, :], jnp.sin(angles)[:, None, :])


def rotate(values, cosine, sine_table):
    half_dim = HD // 2
    first_half = values[..., :half_dim]
    second_half = values[..., half_dim:]
    return jnp.concatenate(
        [
            first_half * cosine - second_half * sine_table,
            second_half * cosine + first_half * sine_table,
        ],
        axis=-1,
    )


def norm_back(grad_out, inputs, scale_inv, gain_vec):
    weighted = grad_out * gain_vec
    row_inner = jnp.mean(weighted * inputs, axis=-1, keepdims=True)
    return scale_inv * weighted - inputs * (scale_inv * scale_inv * scale_inv) * row_inner


def matmul_plain(left_mat, right_mat):
    return jnp.dot(left_mat, right_mat, preferred_element_type=jnp.float32)


def matmul_rows(left_mat, right_mat):
    return lax.dot_general(
        left_mat, right_mat, (((0,), (0,)), ((), ())), preferred_element_type=jnp.float32
    )


def matmul_cols(left_mat, right_mat):
    return lax.dot_general(
        left_mat, right_mat, (((1,), (1,)), ((), ())), preferred_element_type=jnp.float32
    )


def make_links(mesh):
    shard_size, rep_size = mesh.shape["shard"], mesh.shape["rep"]
    axes = ("shard", "rep")

    def shard_swap(value, bit):
        pairs = [
            (s * rep_size + r, (s ^ bit) * rep_size + r)
            for s in range(shard_size)
            for r in range(rep_size)
        ]
        return lax.ppermute(value, axes, pairs)

    def rep_swap(value, bit):
        pairs = [
            (s * rep_size + r, s * rep_size + (r ^ bit))
            for s in range(shard_size)
            for r in range(rep_size)
        ]
        return lax.ppermute(value, axes, pairs)

    return shard_size, rep_size, shard_swap, rep_swap


def add_low(left, right):
    return (left.astype(jnp.float32) + right.astype(jnp.float32)).astype(jnp.bfloat16)


def pin(values, *waits):
    return lax.optimization_barrier((values, waits))[0]


class Flow:
    def __init__(self, steps):
        self.steps = steps
        self.result = None
        self.pending = next(steps)

    def resume(self, arrived):
        try:
            self.pending = self.steps.send(arrived)
        except StopIteration as stop:
            self.pending = ()
            self.steps = None
            self.result = stop.value

    def finish(self):
        while self.steps is not None:
            self.resume(self.pending)
        return self.result


def sync(values, *flows):
    flows = [flow for flow in flows if flow.steps is not None]
    values, arrived = lax.optimization_barrier((values, [flow.pending for flow in flows]))
    for flow, got in zip(flows, arrived):
        flow.resume(got)
    return values


def place_kernel(spots_ref, *refs):
    del spots_ref
    out_ref = refs[-1]
    for at in range(len(refs) - 1):

        @pl.when(pl.program_id(0) == at)
        def _():
            out_ref[...] = refs[at][...]


def place_blocks(gathered):
    blocks, spots = gathered
    rows, width = blocks[1].shape
    count = len(blocks) + 1
    return pl.pallas_call(
        place_kernel,
        out_shape=jax.ShapeDtypeStruct((count * rows, width), blocks[0].dtype),
        grid_spec=pltpu.PrefetchScalarGridSpec(
            num_scalar_prefetch=1,
            grid=(count,),
            in_specs=[
                pl.BlockSpec((rows, width), lambda i, spot, at=at: (at, 0))
                for at in (0, 1) + (0,) * (count - 2)
            ],
            out_specs=pl.BlockSpec((rows, width), lambda i, spot: (spot[i], 0)),
        ),
        cost_estimate=TINY,
        compiler_params=pltpu.CompilerParams(vmem_limit_bytes=60 << 20),
        name="place_blocks",
    )(spots, blocks[0], *blocks)


FF_TILE = 512


def block_specs(count, rows, tiles, start=0):
    own = [
        pl.BlockSpec((rows, FF_TILE), lambda i, spot, at=at: (at, i + start)) for at in (0, 1)
    ]
    gate = [pl.BlockSpec((rows, FF_TILE), lambda i, spot: (0, i + start))] * (count - 2)
    up = [pl.BlockSpec((rows, FF_TILE), lambda i, spot: (0, i + start + tiles))] * (count - 2)
    return own + gate + own + up


def settle(spots_ref, refs, whole_ref):
    rows = refs[0].shape[0]
    for at, ref in enumerate(refs):
        begin = pl.multiple_of(spots_ref[at] * rows, rows)
        whole_ref[pl.ds(begin, rows), :] = ref[...]


def ffn_forward_kernel(count, spare, spots_ref, a_ref, *refs):
    refs = refs[: 2 * count] + refs[2 * count + spare :]
    gate_refs, up_refs = refs[:count], refs[count : 2 * count]
    z_ref, act_ref, slope_ref, gate_whole, up_whole = refs[2 * count :]
    settle(spots_ref, gate_refs, gate_whole)
    settle(spots_ref, up_refs, up_whole)
    step = min(256, a_ref.shape[0])
    for begin in range(0, a_ref.shape[0], step):
        rows = slice(begin, begin + step)
        gate = jnp.dot(a_ref[rows], gate_whole[...], preferred_element_type=jnp.float32)
        up = jnp.dot(a_ref[rows], up_whole[...], preferred_element_type=jnp.float32)
        sig = jax.nn.sigmoid(gate)
        act = gate * sig
        z_ref[rows] = (act * up).astype(jnp.bfloat16)
        act_ref[rows] = act.astype(jnp.bfloat16)
        slope_ref[rows] = (up * (sig + act * (1.0 - sig))).astype(jnp.bfloat16)


def ffn_forward(normed, gate, up, gathered, start, steps, into):
    rows, depth = normed.shape
    blocks, spots = gathered
    count = len(blocks) + 2
    hidden = gate.shape[1]
    part = gate.shape[0] // 2
    out = jax.ShapeDtypeStruct((rows, hidden), jnp.bfloat16)
    into = [] if into is None else list(into)
    first = 2 + 2 * count
    return pl.pallas_call(
        functools.partial(ffn_forward_kernel, count, len(into)),
        out_shape=(out, out, out),
        grid_spec=pltpu.PrefetchScalarGridSpec(
            num_scalar_prefetch=1,
            grid=(steps,),
            in_specs=[pl.BlockSpec((rows, depth), lambda i, spot: (0, 0))]
            + block_specs(count, part, hidden // FF_TILE, start)
            + [pl.BlockSpec(memory_space=pl.ANY)] * len(into),
            out_specs=[pl.BlockSpec((rows, FF_TILE), lambda i, spot: (0, i + start))] * 3,
            scratch_shapes=[pltpu.VMEM((depth, FF_TILE), jnp.bfloat16)] * 2,
        ),
        input_output_aliases={first + at: at for at in range(len(into))},
        cost_estimate=TINY,
        compiler_params=pltpu.CompilerParams(vmem_limit_bytes=60 << 20),
        name="ffn_forward",
    )(spots, normed, gate, gate, *blocks, up, up, *blocks, *into)


def ffn_inner_kernel(g_ref, down_ref, act_ref, slope_ref, dgate_ref, dup_ref):
    step = min(256, g_ref.shape[0])
    for begin in range(0, g_ref.shape[0], step):
        rows = slice(begin, begin + step)
        mixed = nt_dot(g_ref[rows], down_ref[...])
        dgate_ref[rows] = (mixed * slope_ref[rows].astype(jnp.float32)).astype(jnp.bfloat16)
        dup_ref[rows] = (mixed * act_ref[rows].astype(jnp.float32)).astype(jnp.bfloat16)


def ffn_inner(grad_low, down, act, slope):
    rows, depth = grad_low.shape
    hidden = down.shape[0]
    out = jax.ShapeDtypeStruct((rows, hidden), jnp.bfloat16)
    tile = pl.BlockSpec((rows, FF_TILE), lambda i: (0, i))
    return pl.pallas_call(
        ffn_inner_kernel,
        out_shape=(out, out),
        grid=(hidden // FF_TILE,),
        in_specs=[
            pl.BlockSpec((rows, depth), lambda i: (0, 0)),
            pl.BlockSpec((FF_TILE, depth), lambda i: (i, 0)),
            tile,
            tile,
        ],
        out_specs=[tile, tile],
        cost_estimate=TINY,
        compiler_params=pltpu.CompilerParams(vmem_limit_bytes=60 << 20),
        name="ffn_inner",
    )(grad_low, down, act, slope)


def ffn_input_kernel(count, spots_ref, dgate_ref, dup_ref, *refs):
    gate_refs, up_refs = refs[:count], refs[count : 2 * count]
    out_ref, gate_whole, up_whole = refs[2 * count :]
    settle(spots_ref, gate_refs, gate_whole)
    settle(spots_ref, up_refs, up_whole)

    @pl.when(pl.program_id(0) == 0)
    def _():
        out_ref[...] = jnp.zeros_like(out_ref)

    step = min(256, dgate_ref.shape[0])
    for begin in range(0, dgate_ref.shape[0], step):
        rows = slice(begin, begin + step)
        out_ref[rows] += nt_dot(dgate_ref[rows], gate_whole[...]) + nt_dot(
            dup_ref[rows], up_whole[...]
        )


def ffn_input(grad_gate, grad_up, gate, up, gathered):
    rows, hidden = grad_gate.shape
    blocks, spots = gathered
    count = len(blocks) + 2
    part = gate.shape[0] // 2
    depth = count * part
    tile = pl.BlockSpec((rows, FF_TILE), lambda i, spot: (0, i))
    return pl.pallas_call(
        functools.partial(ffn_input_kernel, count),
        out_shape=jax.ShapeDtypeStruct((rows, depth), jnp.float32),
        grid_spec=pltpu.PrefetchScalarGridSpec(
            num_scalar_prefetch=1,
            grid=(hidden // FF_TILE,),
            in_specs=[tile, tile] + block_specs(count, part, hidden // FF_TILE),
            out_specs=pl.BlockSpec((rows, depth), lambda i, spot: (0, 0)),
            scratch_shapes=[pltpu.VMEM((depth, FF_TILE), jnp.bfloat16)] * 2,
        ),
        cost_estimate=TINY,
        compiler_params=pltpu.CompilerParams(vmem_limit_bytes=60 << 20),
        name="ffn_input",
    )(spots, grad_gate, grad_up, gate, gate, *blocks, up, up, *blocks)


def gather_steps(links, mine, whole, late=False):
    shard_size, rep_size, shard_swap, rep_swap = links
    me = lax.axis_index("shard")
    core = lax.rem(lax.axis_index("rep"), 2)
    half, width = mine.shape
    quarter = half // 2
    pieces, others = {}, {}
    if shard_size == 4:
        pieces[1] = shard_swap(mine, 1)
        pieces[2] = shard_swap(mine, 2)
        pieces[1], pieces[2] = yield (pieces[1], pieces[2])
        corner_a = shard_swap(pieces[1][:quarter], 2)
        corner_b = shard_swap(pieces[2][quarter:], 1)
        if late:
            early, waiting = (), (1, 2, 3)
            corner_a, corner_b, pieces[1], pieces[2] = yield (
                corner_a, corner_b, pieces[1], pieces[2]
            )
        else:
            early, waiting = (rep_swap(pieces[1], 1), rep_swap(pieces[2], 1)), (3,)
            corner_a, corner_b, *early = yield (corner_a, corner_b, *early)
        pieces[3] = jnp.concatenate([corner_a, corner_b], axis=0)
        if late == "joined":
            joined = jnp.stack([pieces[1], pieces[2], pieces[3]])
            (got,) = yield (rep_swap(joined, 1),)
            others = {d: got[d - 1] for d in (1, 2, 3)}
        else:
            rest = yield tuple(rep_swap(pieces[d], 1) for d in waiting)
            others = dict(zip((1, 2, 3), (*early, *rest)))
    else:
        pieces[0] = mine
        bit = 1
        while bit < shard_size:
            order = sorted(pieces)
            got = shard_swap(jnp.stack([pieces[d] for d in order]), bit)
            (got,) = yield (got,)
            for at, d in enumerate(order):
                pieces[d ^ bit] = got[at]
            bit *= 2
        del pieces[0]
        others = {d: rep_swap(piece, 1) for d, piece in pieces.items()}
    blocks, spots = [whole] if whole is not None else [], [2 * me, 2 * me + 1]
    for d in pieces:
        blocks += [pieces[d], others[d]]
        spots += [2 * (me ^ d) + core, 2 * (me ^ d) + 1 - core]
    return blocks, jnp.stack(spots).astype(jnp.int32)


def core_half(weight):
    core = lax.rem(lax.axis_index("rep"), 2)
    half = weight.shape[0] // 2
    return lax.dynamic_slice_in_dim(weight, core * half, half, 0)


def pick_columns(links, value):
    core = lax.rem(lax.axis_index("rep"), 2)
    width = value.shape[1] // links[0] // 2

    def half(which):
        return jnp.concatenate(
            [
                lax.dynamic_slice_in_dim(value, (2 * d + which) * width, width, 1)
                for d in range(links[0])
            ],
            axis=1,
        )

    return half(core), half(1 - core)


def blocked(links, product):
    return product.reshape(links[0], -1, product.shape[1])


def scatter_steps(links, own, received):
    shard_size, rep_size, shard_swap, rep_swap = links
    me = lax.axis_index("shard")
    rep = lax.axis_index("rep")
    rows = own.shape[1] // 2

    def piece(d, at):
        begin, extent = (me ^ d, at * rows, 0), (1, rows, own.shape[2])
        return add_low(
            lax.dynamic_slice(own, begin, extent)[0],
            lax.dynamic_slice(received, begin, extent)[0],
        )

    if shard_size == 4:
        got_a = shard_swap(jnp.stack([piece(1, 0), piece(3, 0)]), 1)
        got_b = shard_swap(jnp.stack([piece(2, 1), piece(3, 1)]), 2)
        got_a, got_b = yield (got_a, got_b)
        pass_a = shard_swap(add_low(piece(2, 0), got_a[1]), 2)
        pass_b = shard_swap(add_low(piece(1, 1), got_b[1]), 1)
        pass_a, pass_b = yield (pass_a, pass_b)
        sum_a = add_low(piece(0, 0).astype(jnp.float32) + got_a[0].astype(jnp.float32), pass_a)
        sum_b = add_low(piece(0, 1).astype(jnp.float32) + got_b[0].astype(jnp.float32), pass_b)
        halves = [sum_a, sum_b]
    else:
        held = {d: jnp.stack([piece(d, 0), piece(d, 1)]) for d in range(shard_size)}
        bit = shard_size // 2
        while bit:
            sent = [d for d in sorted(held) if d & bit]
            got = shard_swap(jnp.stack([held[d] for d in sent]), bit)
            (got,) = yield (got,)
            held = {d ^ bit: add_low(held[d ^ bit], got[at]) for at, d in enumerate(sent)}
            bit //= 2
        halves = [held[0][0], held[0][1]]
    upper = lax.rem(rep // 2, 2) == 1
    if rep_size >= 8:
        keep = jnp.where(upper, halves[1], halves[0])
        send = jnp.where(upper, halves[0], halves[1])
        got = rep_swap(send, 2)
        (got,) = yield (got,)
        keep = add_low(keep, got)
        bit = 4
        while bit < rep_size:
            got = rep_swap(keep, bit)
            (got,) = yield (got,)
            keep = add_low(keep, got)
            bit *= 2
        back = rep_swap(keep, 2)
        (back,) = yield (back,)
        halves = [jnp.where(upper, back, keep), jnp.where(upper, keep, back)]
        half = jnp.concatenate(halves, axis=0)
    else:
        half = jnp.concatenate(halves, axis=0)
        bit = 2
        while bit < rep_size:
            half = add_low(half, rep_swap(half, bit))
            bit *= 2
    other = rep_swap(half, 1)
    (other,) = yield (other,)
    return half, other


def join_rows(pair):
    core = lax.rem(lax.axis_index("rep"), 2)
    half, other = pair
    return jnp.where(
        core == 0,
        jnp.concatenate([half, other], axis=0),
        jnp.concatenate([other, half], axis=0),
    ).astype(jnp.float32)


def join_columns(pair):
    core = lax.rem(lax.axis_index("rep"), 2)
    half, other = pair
    return jnp.where(
        core == 0,
        jnp.concatenate([half, other], axis=1),
        jnp.concatenate([other, half], axis=1),
    ).astype(jnp.float32)


BLOCK = 256
LOOK = 3


def nt_dot(left_mat, right_mat):
    return lax.dot_general(
        left_mat, right_mat, (((1,), (1,)), ((), ())), preferred_element_type=jnp.float32
    )


def attend_kernel(live_ref, q_ref, k_ref, v_ref, seg_col_ref, seg_row_ref, o_ref, acc_ref):
    at = pl.program_id(1)
    acc_ref[...] = jnp.zeros_like(acc_ref)
    lane = lax.broadcasted_iota(jnp.int32, (BLOCK, 2 * HD), 1)
    low_lane = lane < HD
    for back in range(LOOK):
        key_block = jnp.maximum(at - back, 0)

        @pl.when((at >= back) & (live_ref[at, key_block] > 0))
        def _():
            begin = pl.multiple_of(key_block * BLOCK, BLOCK)
            same = seg_col_ref[...] == seg_row_ref[:, pl.ds(begin, BLOCK)]
            if back == 0:
                row = lax.broadcasted_iota(jnp.int32, (BLOCK, BLOCK), 0)
                col = lax.broadcasted_iota(jnp.int32, (BLOCK, BLOCK), 1)
                same = same & (col <= row)
            mask = same.astype(jnp.float32)
            keys = k_ref[pl.ds(begin, BLOCK), :]
            values = v_ref[pl.ds(begin, BLOCK), :]
            swapped = pltpu.roll(values.astype(jnp.float32), HD, 1).astype(jnp.bfloat16)
            one = jnp.ones_like(values)
            for head in range(4):
                group, odd = head // 2, head % 2
                scores = nt_dot(
                    q_ref[:, head * HD : (head + 1) * HD], keys[:, group * HD : (group + 1) * HD]
                )
                weights = (jnp.exp(scores) * mask).astype(jnp.bfloat16)
                held = values if group == odd else swapped
                padded = jnp.where(low_lane, held, one) if odd == 0 else jnp.where(low_lane, one, held)
                acc_ref[head] += jnp.dot(weights, padded, preferred_element_type=jnp.float32)

    for group in range(2):
        even, odd = acc_ref[2 * group], acc_ref[2 * group + 1]
        top = jnp.where(low_lane, even, odd)
        total = pltpu.roll(jnp.where(low_lane, odd, even), HD, 1)
        o_ref[:, group * 2 * HD : (group + 1) * 2 * HD] = (top / total).astype(o_ref.dtype)


def head_norm_back(grad, linear, turn, gain):
    half = HD // 2
    cosine, sine = turn[:half], turn[half:]
    gain_1, gain_2 = gain[:half], gain[half:]
    parts, sums = [], None
    for begin in range(0, grad.shape[0], HD):
        grad_1, grad_2 = grad[begin : begin + half], grad[begin + half : begin + HD]
        lin_1, lin_2 = linear[begin : begin + half], linear[begin + half : begin + HD]
        back_1 = grad_1 * cosine + grad_2 * sine
        back_2 = grad_2 * cosine - grad_1 * sine
        square = jnp.sum(lin_1 * lin_1 + lin_2 * lin_2, axis=0, keepdims=True)
        scale = lax.rsqrt(square * (1.0 / HD) + norm_eps)
        unit_1, unit_2 = lin_1 * scale, lin_2 * scale
        both = jnp.concatenate([back_1 * unit_1, back_2 * unit_2], axis=0)
        sums = both if sums is None else sums + both
        back_1, back_2 = back_1 * gain_1, back_2 * gain_2
        inner = jnp.sum(back_1 * unit_1 + back_2 * unit_2, axis=0, keepdims=True) * (1.0 / HD)
        parts += [scale * (back_1 - unit_1 * inner), scale * (back_2 - unit_2 * inner)]
    return jnp.concatenate(parts, axis=0), sums


def attend_back_kernel(
    live_ref, q_ref, do_ref, k_ref, v_ref, seg_col_ref, seg_row_ref,
    q_lin_ref, k_lin_ref, q_turn_ref, k_turn_ref, gain_ref,
    dq_out_ref, dk_out_ref, dv_out_ref, q_gain_ref, k_gain_ref,
    exp_ref, dp_ref, total_ref, inner_ref, dqt_ref, dk_ref, dv_ref,
):
    at = pl.program_id(1)

    @pl.when(at == 0)
    def _():
        dk_ref[...] = jnp.zeros_like(dk_ref)
        dv_ref[...] = jnp.zeros_like(dv_ref)
        q_gain_ref[...] = jnp.zeros_like(q_gain_ref)

    total_ref[...] = jnp.zeros_like(total_ref)
    inner_ref[...] = jnp.zeros_like(inner_ref)
    dqt_ref[...] = jnp.zeros_like(dqt_ref)

    def each_block(run):
        for back in range(LOOK):
            key_block = jnp.maximum(at - back, 0)

            @pl.when((at >= back) & (live_ref[at, key_block] > 0))
            def _():
                run(back, pl.multiple_of(key_block * BLOCK, BLOCK))

    def first(back, begin):
        same = seg_col_ref[pl.ds(begin, BLOCK), :] == seg_row_ref[...]
        if back == 0:
            row = lax.broadcasted_iota(jnp.int32, (BLOCK, BLOCK), 0)
            col = lax.broadcasted_iota(jnp.int32, (BLOCK, BLOCK), 1)
            same = same & (row <= col)
        mask = same.astype(jnp.float32)
        keys = k_ref[pl.ds(begin, BLOCK), :]
        values = v_ref[pl.ds(begin, BLOCK), :]
        for head in range(4):
            group = head // 2
            cols = slice(head * HD, (head + 1) * HD)
            kept = slice(group * HD, (group + 1) * HD)
            weights = jnp.exp(nt_dot(keys[:, kept], q_ref[:, cols])) * mask
            grads = nt_dot(values[:, kept], do_ref[:, cols])
            exp_ref[head, back] = weights
            dp_ref[head, back] = grads
            total_ref[head : head + 1] += jnp.sum(weights, axis=0, keepdims=True)
            inner_ref[head : head + 1] += jnp.sum(weights * grads, axis=0, keepdims=True)

    def second(back, begin):
        keys = k_ref[pl.ds(begin, BLOCK), :]
        dk_parts, dv_parts = [], []
        for group in range(2):
            dk_sum, dv_sum = None, None
            for head in (2 * group, 2 * group + 1):
                cols = slice(head * HD, (head + 1) * HD)
                scale = 1.0 / total_ref[head : head + 1]
                probs = exp_ref[head, back] * scale
                inner = inner_ref[head : head + 1] * scale
                low_scores = (probs * (dp_ref[head, back] - inner)).astype(jnp.bfloat16)
                dv_part = jnp.dot(
                    probs.astype(jnp.bfloat16), do_ref[:, cols], preferred_element_type=jnp.float32
                )
                dk_part = jnp.dot(low_scores, q_ref[:, cols], preferred_element_type=jnp.float32)
                dqt_ref[cols] += lax.dot_general(
                    keys[:, group * HD : (group + 1) * HD],
                    low_scores,
                    (((0,), (0,)), ((), ())),
                    preferred_element_type=jnp.float32,
                )
                dk_sum = dk_part if dk_sum is None else dk_sum + dk_part
                dv_sum = dv_part if dv_sum is None else dv_sum + dv_part
            dk_parts.append(dk_sum)
            dv_parts.append(dv_sum)
        dk_ref[pl.ds(begin, BLOCK), :] += jnp.concatenate(dk_parts, axis=1)
        dv_ref[pl.ds(begin, BLOCK), :] += jnp.concatenate(dv_parts, axis=1)

    each_block(first)
    each_block(second)
    grad, gain_sum = head_norm_back(
        dqt_ref[...] * (1.0 / math.sqrt(HD)), q_lin_ref[...].T, q_turn_ref[...], gain_ref[:HD]
    )
    q_gain_ref[0] += gain_sum
    dq_out_ref[...] = grad.T.astype(jnp.bfloat16)

    @pl.when(at == pl.num_programs(1) - 1)
    def _():
        dv_out_ref[...] = dv_ref[...].astype(jnp.bfloat16)
        key_sum = None
        for begin in range(0, dk_ref.shape[0], BLOCK):
            rows = slice(begin, begin + BLOCK)
            grad, gain_sum = head_norm_back(
                dk_ref[rows].T, k_lin_ref[rows].T, k_turn_ref[:, rows], gain_ref[HD:]
            )
            dk_out_ref[rows] = grad.T.astype(jnp.bfloat16)
            key_sum = gain_sum if key_sum is None else key_sum + gain_sum
        k_gain_ref[0] = key_sum


def live_blocks(segment):
    count = segment.shape[0] // BLOCK
    blocks = segment.reshape(count, BLOCK)
    index = jnp.arange(count)
    return (
        (blocks[:, :1] == blocks[:, -1][None, :]) | (index[:, None] == index[None, :])
    ).astype(jnp.int32)


def attend(query, key, value, segment):
    rows = query.shape[0]
    panels, count = HK // 2, rows // BLOCK
    return pl.pallas_call(
        attend_kernel,
        out_shape=jax.ShapeDtypeStruct((rows, HQ * HD), jnp.bfloat16),
        grid_spec=pltpu.PrefetchScalarGridSpec(
            num_scalar_prefetch=1,
            grid=(panels, count),
            in_specs=[
                pl.BlockSpec((BLOCK, 4 * HD), lambda p, i, live: (i, p)),
                pl.BlockSpec((rows, 2 * HD), lambda p, i, live: (0, p)),
                pl.BlockSpec((rows, 2 * HD), lambda p, i, live: (0, p)),
                pl.BlockSpec((BLOCK, 1), lambda p, i, live: (i, 0)),
                pl.BlockSpec((1, rows), lambda p, i, live: (0, 0)),
            ],
            out_specs=pl.BlockSpec((BLOCK, 4 * HD), lambda p, i, live: (i, p)),
            scratch_shapes=[pltpu.VMEM((4, BLOCK, 2 * HD), jnp.float32)],
        ),
        cost_estimate=TINY,
        name="attend",
    )(live_blocks(segment), query, key, value, segment[:, None], segment[None, :])


def attend_back(query, grad_out, key, value, segment, query_lin, key_lin, turn, gain, start, panels):
    rows = query.shape[0]
    count = rows // BLOCK
    return pl.pallas_call(
        attend_back_kernel,
        out_shape=(
            jax.ShapeDtypeStruct((rows, panels * 4 * HD), jnp.bfloat16),
            jax.ShapeDtypeStruct((rows, panels * 2 * HD), jnp.bfloat16),
            jax.ShapeDtypeStruct((rows, panels * 2 * HD), jnp.bfloat16),
            jax.ShapeDtypeStruct((panels, HD, BLOCK), jnp.float32),
            jax.ShapeDtypeStruct((panels, HD, BLOCK), jnp.float32),
        ),
        grid_spec=pltpu.PrefetchScalarGridSpec(
            num_scalar_prefetch=1,
            grid=(panels, count),
            in_specs=[
                pl.BlockSpec((BLOCK, 4 * HD), lambda p, i, live: (i, start + p)),
                pl.BlockSpec((BLOCK, 4 * HD), lambda p, i, live: (i, start + p)),
                pl.BlockSpec((rows, 2 * HD), lambda p, i, live: (0, start + p)),
                pl.BlockSpec((rows, 2 * HD), lambda p, i, live: (0, start + p)),
                pl.BlockSpec((rows, 1), lambda p, i, live: (0, 0)),
                pl.BlockSpec((1, BLOCK), lambda p, i, live: (0, i)),
                pl.BlockSpec((BLOCK, 4 * HD), lambda p, i, live: (i, start + p)),
                pl.BlockSpec((rows, 2 * HD), lambda p, i, live: (0, start + p)),
                pl.BlockSpec((HD, BLOCK), lambda p, i, live: (0, i)),
                pl.BlockSpec((HD, rows), lambda p, i, live: (0, 0)),
                pl.BlockSpec((2 * HD, 1), lambda p, i, live: (0, 0)),
            ],
            out_specs=[
                pl.BlockSpec((BLOCK, 4 * HD), lambda p, i, live: (i, p)),
                pl.BlockSpec((rows, 2 * HD), lambda p, i, live: (0, p)),
                pl.BlockSpec((rows, 2 * HD), lambda p, i, live: (0, p)),
                pl.BlockSpec((1, HD, BLOCK), lambda p, i, live: (p, 0, 0)),
                pl.BlockSpec((1, HD, BLOCK), lambda p, i, live: (p, 0, 0)),
            ],
            scratch_shapes=[
                pltpu.VMEM((4, LOOK, BLOCK, BLOCK), jnp.float32),
                pltpu.VMEM((4, LOOK, BLOCK, BLOCK), jnp.float32),
                pltpu.VMEM((8, BLOCK), jnp.float32),
                pltpu.VMEM((8, BLOCK), jnp.float32),
                pltpu.VMEM((4 * HD, BLOCK), jnp.float32),
                pltpu.VMEM((rows, 2 * HD), jnp.float32),
                pltpu.VMEM((rows, 2 * HD), jnp.float32),
            ],
        ),
        cost_estimate=TINY,
        name="attend_back",
    )(live_blocks(segment), query, grad_out, key, value, segment[:, None], segment[None, :],
      query_lin, key_lin, turn, turn, gain)


def body(
    links,
    tokens,
    cotangent,
    segment,
    attn_gain,
    w_query,
    w_key,
    w_value,
    qk_gain,
    w_out,
    ffn_gain,
    w_gate,
    w_up,
    w_down,
):
    row_count = tokens.shape[0]
    rep_swap = links[3]
    core = lax.rem(lax.axis_index("rep"), 2)
    score_scale = 1.0 / math.sqrt(HD)
    spare = jnp.zeros((attn_gain.shape[0] - qk_gain.shape[0],), jnp.bfloat16)
    packed = jnp.stack([attn_gain, ffn_gain, jnp.concatenate([qk_gain, spare])], axis=1)
    packed = jnp.pad(packed, ((0, 0), (0, 125)))
    attn_weights = (w_query, w_key, w_value, packed)
    front_flow = Flow(
        gather_steps(
            links,
            jnp.concatenate([core_half(weight) for weight in attn_weights], axis=1),
            jnp.concatenate(attn_weights, axis=1),
            late="joined",
        )
    )
    w_out, w_gate, w_up, w_down = sync((w_out, w_gate, w_up, w_down), front_flow)
    out_flow = Flow(gather_steps(links, core_half(w_out), w_out, late="joined"))
    w_gate, w_up, w_down = sync((w_gate, w_up, w_down), front_flow)
    pair = jnp.concatenate([core_half(w_gate), core_half(w_up)], axis=1)
    pair_flow = Flow(gather_steps(links, pair, None, late=True))
    w_down = sync(w_down, front_flow)
    front = place_blocks(front_flow.finish())
    full_query = front[:, : HQ * HD]
    full_key = front[:, HQ * HD : (HQ + HK) * HD]
    full_value = front[:, (HQ + HK) * HD : (HQ + 2 * HK) * HD]
    gains = front[:, (HQ + 2 * HK) * HD :]
    full_attn_gain = gains[:, 0]
    full_ffn_gain = gains[:, 1]
    full_qk_gain = gains.reshape(links[0], -1, 128)[:, : qk_gain.shape[0], 2].reshape(-1)
    inputs = tokens.astype(jnp.float32)
    token_index = jnp.arange(row_count)
    same_seq = segment[:, None] == segment[None, :]
    allowed = same_seq & (token_index[None, :] <= token_index[:, None])
    positions = jnp.sum(
        (same_seq & (token_index[None, :] < token_index[:, None])).astype(jnp.float32), axis=1
    )
    live_rows = (segment >= 0).astype(jnp.float32)[:, None]
    cosine, sine_table = rope_tables(positions)
    scale_one = inv_rms(inputs)
    normed = (inputs * scale_one * full_attn_gain.astype(jnp.float32)).astype(jnp.bfloat16)
    query_lin = matmul_plain(normed, full_query).reshape(row_count, HQ, HD)
    key_lin = matmul_plain(normed, full_key).reshape(row_count, HK, HD)
    value_low = matmul_plain(normed, full_value).astype(jnp.bfloat16).reshape(row_count, HK, HD)
    qk_gains = full_qk_gain.astype(jnp.float32)
    query_scale = inv_rms(query_lin)
    key_scale = inv_rms(key_lin)
    query_rot = (
        rotate(query_lin * query_scale * qk_gains[:HD], cosine, sine_table)
        .astype(jnp.bfloat16)
    )
    key_rot = rotate(key_lin * key_scale * qk_gains[HD:], cosine, sine_table).astype(jnp.bfloat16)

    query_rot = (query_rot.astype(jnp.float32) * score_scale).astype(jnp.bfloat16)
    query_rot = query_rot.reshape(row_count, HQ * HD)
    key_rot = key_rot.reshape(row_count, HK * HD)
    value_low = value_low.reshape(row_count, HK * HD)
    query_rot, key_rot, value_low, w_down = sync(
        (query_rot, key_rot, value_low, w_down), out_flow
    )
    attn_low = attend(query_rot, key_rot, value_low, segment)
    attn_low, w_down = sync((attn_low, w_down), out_flow, pair_flow)
    down_flow = Flow(gather_steps(links, core_half(w_down), w_down))
    full_out = place_blocks(out_flow.finish())
    hidden = inputs + matmul_plain(attn_low, full_out)
    scale_two = inv_rms(hidden)
    normed_ffn = (hidden * scale_two * full_ffn_gain.astype(jnp.float32)).astype(jnp.bfloat16)
    normed_ffn, hidden = sync((normed_ffn, hidden), pair_flow)
    pair = pair_flow.finish()
    tiles = w_gate.shape[1] // FF_TILE
    first = ffn_forward(normed_ffn, w_gate, w_up, pair, 0, tiles // 2, None)
    normed_ffn, first = sync((normed_ffn, first), down_flow)
    mixed_act, act_low, slope = ffn_forward(
        normed_ffn, w_gate, w_up, pair, tiles // 2, tiles - tiles // 2, first
    )
    mixed_act, slope, act_low = sync((mixed_act, slope, act_low), down_flow)
    mixed_act, slope, act_low = sync((mixed_act, slope, act_low), down_flow)
    full_down = place_blocks(down_flow.finish())
    out_grad = live_rows * cotangent.astype(jnp.float32)
    out_low = out_grad.astype(jnp.bfloat16)
    grad_gate_low, grad_up_low = ffn_inner(out_low, full_down, act_low, slope)
    half = out_low.shape[1] // 2
    out_own = lax.dynamic_slice_in_dim(out_low, core * half, half, 1)
    out_other = lax.dynamic_slice_in_dim(out_low, (1 - core) * half, half, 1)
    normed_own, normed_other = pick_columns(links, normed_ffn)
    grad_up_low, grad_gate_low, out_own, out_other, mixed_act = pin(
        (grad_up_low, grad_gate_low, out_own, out_other, mixed_act)
    )

    def hand(product):
        return rep_swap(blocked(links, product).astype(jnp.bfloat16), 1)

    down_given = matmul_rows(mixed_act, out_other).astype(jnp.bfloat16)
    down_sent = hand(down_given)
    gate_given = matmul_rows(normed_other, pin(grad_gate_low, down_given)).astype(jnp.bfloat16)
    gate_sent = hand(gate_given)
    down_sent, mixed_act, grad_up_low, gate_given = pin(
        (down_sent, mixed_act, grad_up_low, gate_given)
    )
    down_given = blocked(links, matmul_rows(mixed_act, out_own).astype(jnp.bfloat16))
    down_back = Flow(scatter_steps(links, *pin((down_given, down_sent))))
    grad_up_low, grad_gate_low, normed_own, normed_other = pin(
        (grad_up_low, grad_gate_low, normed_own, normed_other), down_given
    )
    up_sent = hand(matmul_rows(normed_other, grad_up_low))
    gate_given = blocked(links, matmul_rows(normed_own, grad_gate_low).astype(jnp.bfloat16))
    up_given = blocked(links, matmul_rows(normed_own, grad_up_low).astype(jnp.bfloat16))
    gate_given, gate_sent, up_given, up_sent, grad_gate_low, grad_up_low = sync(
        (gate_given, gate_sent, up_given, up_sent, grad_gate_low, grad_up_low), down_back
    )
    gate_back = Flow(scatter_steps(links, gate_given, gate_sent))
    grad_normed_ffn = ffn_input(grad_gate_low, grad_up_low, w_gate, w_up, pair)
    grad_normed_ffn, up_given, up_sent = sync((grad_normed_ffn, up_given, up_sent), down_back)
    grad_hidden = out_grad + norm_back(
        grad_normed_ffn, hidden, scale_two, full_ffn_gain.astype(jnp.float32)
    )
    hidden_low = grad_hidden.astype(jnp.bfloat16)
    grad_attn_low = matmul_cols(hidden_low, full_out).astype(jnp.bfloat16)
    attn_own, attn_other = pick_columns(links, attn_low)
    out_sent = hand(matmul_rows(attn_other, hidden_low))
    out_given = blocked(links, matmul_rows(attn_own, hidden_low).astype(jnp.bfloat16))
    panels = HK // 4
    grad_attn_low, out_given, out_sent, up_given, up_sent = sync(
        (grad_attn_low, out_given, out_sent, up_given, up_sent), gate_back, down_back
    )
    up_back = Flow(scatter_steps(links, up_given, up_sent))
    turn = jnp.concatenate([cosine[:, 0].T, sine_table[:, 0].T], axis=0)
    flat = (query_lin.reshape(row_count, -1), key_lin.reshape(row_count, -1), turn, qk_gains[:, None])
    lower = attend_back(query_rot, grad_attn_low, key_rot, value_low, segment, *flat, 0, panels)
    grad_attn_low, lower = sync((grad_attn_low, lower), up_back, gate_back, down_back)
    upper = attend_back(query_rot, grad_attn_low, key_rot, value_low, segment, *flat, panels, panels)
    lower, upper, out_given, out_sent = sync(
        (lower, upper, out_given, out_sent), up_back, gate_back, down_back
    )
    out_back = Flow(scatter_steps(links, out_given, out_sent))
    grad_qk_gain = jnp.concatenate(
        [jnp.sum(lower[at] + upper[at], axis=(0, 2)) for at in (3, 4)]
    )
    grad_front = jnp.concatenate([part for at in range(3) for part in (lower[at], upper[at])], axis=1)
    normed_own, normed_other = pick_columns(links, normed)
    front_other = blocked(links, matmul_rows(normed_other, grad_front))
    front_own = blocked(links, matmul_rows(normed_own, grad_front))
    front_other, front_own = (part.astype(jnp.bfloat16) for part in (front_other, front_own))
    grad_front = pin(grad_front, front_other, front_own)
    grad_query_low = grad_front[:, : HQ * HD]
    grad_key_low = grad_front[:, HQ * HD : (HQ + HK) * HD]
    grad_value_low = grad_front[:, (HQ + HK) * HD :]
    grad_normed = (
        matmul_cols(grad_query_low, full_query)
        + matmul_cols(grad_key_low, full_key)
        + matmul_cols(grad_value_low, full_value)
    )
    qk_part = jnp.pad(
        grad_qk_gain.reshape(links[0], -1),
        ((0, 0), (0, attn_gain.shape[0] - qk_gain.shape[0])),
    )
    small = jnp.pad(qk_part.reshape(-1, 1), ((0, 0), (0, 127)))
    small = small.astype(jnp.bfloat16).reshape(links[0], 2, -1, 128)
    own_front = jnp.concatenate([front_own, lax.dynamic_slice_in_dim(small, core, 1, 1)[:, 0]], axis=2)
    other_front = jnp.concatenate(
        [front_other, lax.dynamic_slice_in_dim(small, 1 - core, 1, 1)[:, 0]], axis=2
    )
    front_sent = rep_swap(other_front, 1)
    own_front, front_sent, mixed_act, grad_normed = sync(
        (own_front, front_sent, mixed_act, grad_normed), up_back, gate_back
    )
    front_back = Flow(scatter_steps(links, own_front, front_sent))
    grad_inputs = grad_hidden + norm_back(
        grad_normed, inputs, scale_one, full_attn_gain.astype(jnp.float32)
    )
    result = live_rows * (hidden + matmul_plain(mixed_act, full_down))
    grad_inputs, result = sync((grad_inputs, result), gate_back, front_back, out_back)
    sync((), up_back, front_back, out_back)
    sync((), up_back, front_back, out_back)
    sync((), front_back, out_back)
    front_share = join_rows(front_back.finish())
    share_query = front_share[:, : HQ * HD]
    share_key = front_share[:, HQ * HD : (HQ + HK) * HD]
    share_value = front_share[:, (HQ + HK) * HD : (HQ + 2 * HK) * HD]
    extras = front_share[:, (HQ + 2 * HK) * HD :]
    share_qk = extras[: qk_gain.shape[0], 0]
    share_out = join_rows(out_back.finish())
    share_gate = join_rows(gate_back.finish())
    share_up = join_rows(up_back.finish())
    share_down = join_columns(down_back.finish())
    def gain_share(gain, *pairs):
        inner = sum(
            jnp.sum(weight.astype(jnp.float32) * share, axis=1) for weight, share in pairs
        )
        return inner / gain.astype(jnp.float32)

    share_again = gain_share(
        attn_gain, (w_query, share_query), (w_key, share_key), (w_value, share_value)
    )
    share_fgain = gain_share(ffn_gain, (w_gate, share_gate), (w_up, share_up))
    return (
        result.astype(jnp.bfloat16),
        grad_inputs.astype(jnp.bfloat16),
        share_again,
        share_query,
        share_key,
        share_value,
        share_qk,
        share_out,
        share_fgain,
        share_gate,
        share_up,
        share_down,
    )


def solution(mesh):
    return jax.shard_map(
        functools.partial(body, make_links(mesh)),
        mesh=mesh,
        in_specs=(
            P(("shard", "rep"), None),
            P(("shard", "rep"), None),
            P(("shard", "rep")),
            P("shard"),
            P("shard", None),
            P("shard", None),
            P("shard", None),
            P("shard"),
            P("shard", None),
            P("shard"),
            P("shard", None),
            P("shard", None),
            P("shard", None),
        ),
        out_specs=(
            P(("shard", "rep"), None),
            P(("shard", "rep"), None),
            P("shard"),
            P("shard", None),
            P("shard", None),
            P("shard", None),
            P("shard"),
            P("shard", None),
            P("shard"),
            P("shard", None),
            P("shard", None),
            P("shard", None),
        ),
        check_vma=False,
    )
```

```python
import functools
import math

import jax
import jax.numpy as jnp
from jax import lax
from jax.experimental import pallas as pl
from jax.experimental.pallas import tpu as pltpu
from jax.sharding import PartitionSpec as P

HQ = 16
HK = 8
HD = 64


norm_eps = 1e-05
TINY = pl.CostEstimate(flops=1, bytes_accessed=1, transcendentals=0)
rope_base = 1000000.0


def inv_rms(values):
    return lax.rsqrt(jnp.mean(values * values, axis=-1, keepdims=True) + norm_eps)


def rope_tables(positions):
    half_dim = HD // 2
    freq_index = jnp.arange(half_dim).astype(jnp.float32)
    freq_vals = jnp.power(rope_base, -(2.0 * freq_index) / HD)
    angles = positions[:, None] * freq_vals[None, :]
    return (jnp.cos(angles)[:, None, :], jnp.sin(angles)[:, None, :])


def rotate(values, cosine, sine_table):
    half_dim = HD // 2
    first_half = values[..., :half_dim]
    second_half = values[..., half_dim:]
    return jnp.concatenate(
        [
            first_half * cosine - second_half * sine_table,
            second_half * cosine + first_half * sine_table,
        ],
        axis=-1,
    )


def norm_back(grad_out, inputs, scale_inv, gain_vec):
    weighted = grad_out * gain_vec
    row_inner = jnp.mean(weighted * inputs, axis=-1, keepdims=True)
    return scale_inv * weighted - inputs * (scale_inv * scale_inv * scale_inv) * row_inner


def matmul_plain(left_mat, right_mat):
    return jnp.dot(left_mat, right_mat, preferred_element_type=jnp.float32)


def matmul_rows(left_mat, right_mat):
    return lax.dot_general(
        left_mat, right_mat, (((0,), (0,)), ((), ())), preferred_element_type=jnp.float32
    )


def matmul_cols(left_mat, right_mat):
    return lax.dot_general(
        left_mat, right_mat, (((1,), (1,)), ((), ())), preferred_element_type=jnp.float32
    )


def make_links(mesh):
    shard_size, rep_size = mesh.shape["shard"], mesh.shape["rep"]
    axes = ("shard", "rep")

    def shard_swap(value, bit):
        pairs = [
            (s * rep_size + r, (s ^ bit) * rep_size + r)
            for s in range(shard_size)
            for r in range(rep_size)
        ]
        return lax.ppermute(value, axes, pairs)

    def rep_swap(value, bit):
        pairs = [
            (s * rep_size + r, s * rep_size + (r ^ bit))
            for s in range(shard_size)
            for r in range(rep_size)
        ]
        return lax.ppermute(value, axes, pairs)

    return shard_size, rep_size, shard_swap, rep_swap


def add_low(left, right):
    return (left.astype(jnp.float32) + right.astype(jnp.float32)).astype(jnp.bfloat16)


def pin(values, *waits):
    return lax.optimization_barrier((values, waits))[0]


class Flow:
    def __init__(self, steps):
        self.steps = steps
        self.result = None
        self.pending = next(steps)

    def resume(self, arrived):
        try:
            self.pending = self.steps.send(arrived)
        except StopIteration as stop:
            self.pending = ()
            self.steps = None
            self.result = stop.value

    def finish(self):
        while self.steps is not None:
            self.resume(self.pending)
        return self.result


def sync(values, *flows):
    flows = [flow for flow in flows if flow.steps is not None]
    values, arrived = lax.optimization_barrier((values, [flow.pending for flow in flows]))
    for flow, got in zip(flows, arrived):
        flow.resume(got)
    return values


def place_kernel(spots_ref, *refs):
    del spots_ref
    out_ref = refs[-1]
    for at in range(len(refs) - 1):

        @pl.when(pl.program_id(0) == at)
        def _():
            out_ref[...] = refs[at][...]


def place_blocks(gathered):
    blocks, spots = gathered
    rows, width = blocks[1].shape
    count = len(blocks) + 1
    return pl.pallas_call(
        place_kernel,
        out_shape=jax.ShapeDtypeStruct((count * rows, width), blocks[0].dtype),
        grid_spec=pltpu.PrefetchScalarGridSpec(
            num_scalar_prefetch=1,
            grid=(count,),
            in_specs=[
                pl.BlockSpec((rows, width), lambda i, spot, at=at: (at, 0))
                for at in (0, 1) + (0,) * (count - 2)
            ],
            out_specs=pl.BlockSpec((rows, width), lambda i, spot: (spot[i], 0)),
        ),
        cost_estimate=TINY,
        compiler_params=pltpu.CompilerParams(vmem_limit_bytes=60 << 20),
        name="place_blocks",
    )(spots, blocks[0], *blocks)


FF_TILE = 512


def block_specs(count, rows, tiles, start=0):
    own = [
        pl.BlockSpec((rows, FF_TILE), lambda i, spot, at=at: (at, i + start)) for at in (0, 1)
    ]
    gate = [pl.BlockSpec((rows, FF_TILE), lambda i, spot: (0, i + start))] * (count - 2)
    up = [pl.BlockSpec((rows, FF_TILE), lambda i, spot: (0, i + start + tiles))] * (count - 2)
    return own + gate + own + up


def settle(spots_ref, refs, whole_ref):
    rows = refs[0].shape[0]
    for at, ref in enumerate(refs):
        begin = pl.multiple_of(spots_ref[at] * rows, rows)
        whole_ref[pl.ds(begin, rows), :] = ref[...]


def ffn_forward_kernel(count, spare, spots_ref, a_ref, *refs):
    refs = refs[: 2 * count] + refs[2 * count + spare :]
    gate_refs, up_refs = refs[:count], refs[count : 2 * count]
    z_ref, act_ref, slope_ref, gate_whole, up_whole = refs[2 * count :]
    settle(spots_ref, gate_refs, gate_whole)
    settle(spots_ref, up_refs, up_whole)
    step = min(256, a_ref.shape[0])
    for begin in range(0, a_ref.shape[0], step):
        rows = slice(begin, begin + step)
        gate = jnp.dot(a_ref[rows], gate_whole[...], preferred_element_type=jnp.float32)
        up = jnp.dot(a_ref[rows], up_whole[...], preferred_element_type=jnp.float32)
        sig = jax.nn.sigmoid(gate)
        act = gate * sig
        z_ref[rows] = (act * up).astype(jnp.bfloat16)
        act_ref[rows] = act.astype(jnp.bfloat16)
        slope_ref[rows] = (up * (sig + act * (1.0 - sig))).astype(jnp.bfloat16)


def ffn_forward(normed, gate, up, gathered, start, steps, into):
    rows, depth = normed.shape
    blocks, spots = gathered
    count = len(blocks) + 2
    hidden = gate.shape[1]
    part = gate.shape[0] // 2
    out = jax.ShapeDtypeStruct((rows, hidden), jnp.bfloat16)
    into = [] if into is None else list(into)
    first = 2 + 2 * count
    return pl.pallas_call(
        functools.partial(ffn_forward_kernel, count, len(into)),
        out_shape=(out, out, out),
        grid_spec=pltpu.PrefetchScalarGridSpec(
            num_scalar_prefetch=1,
            grid=(steps,),
            in_specs=[pl.BlockSpec((rows, depth), lambda i, spot: (0, 0))]
            + block_specs(count, part, hidden // FF_TILE, start)
            + [pl.BlockSpec(memory_space=pl.ANY)] * len(into),
            out_specs=[pl.BlockSpec((rows, FF_TILE), lambda i, spot: (0, i + start))] * 3,
            scratch_shapes=[pltpu.VMEM((depth, FF_TILE), jnp.bfloat16)] * 2,
        ),
        input_output_aliases={first + at: at for at in range(len(into))},
        cost_estimate=TINY,
        compiler_params=pltpu.CompilerParams(vmem_limit_bytes=60 << 20),
        name="ffn_forward",
    )(spots, normed, gate, gate, *blocks, up, up, *blocks, *into)


def ffn_inner_kernel(g_ref, down_ref, act_ref, slope_ref, dgate_ref, dup_ref):
    step = min(256, g_ref.shape[0])
    for begin in range(0, g_ref.shape[0], step):
        rows = slice(begin, begin + step)
        mixed = nt_dot(g_ref[rows], down_ref[...])
        dgate_ref[rows] = (mixed * slope_ref[rows].astype(jnp.float32)).astype(jnp.bfloat16)
        dup_ref[rows] = (mixed * act_ref[rows].astype(jnp.float32)).astype(jnp.bfloat16)


def ffn_inner(grad_low, down, act, slope):
    rows, depth = grad_low.shape
    hidden = down.shape[0]
    out = jax.ShapeDtypeStruct((rows, hidden), jnp.bfloat16)
    tile = pl.BlockSpec((rows, FF_TILE), lambda i: (0, i))
    return pl.pallas_call(
        ffn_inner_kernel,
        out_shape=(out, out),
        grid=(hidden // FF_TILE,),
        in_specs=[
            pl.BlockSpec((rows, depth), lambda i: (0, 0)),
            pl.BlockSpec((FF_TILE, depth), lambda i: (i, 0)),
            tile,
            tile,
        ],
        out_specs=[tile, tile],
        cost_estimate=TINY,
        compiler_params=pltpu.CompilerParams(vmem_limit_bytes=60 << 20),
        name="ffn_inner",
    )(grad_low, down, act, slope)


def ffn_input_kernel(count, spots_ref, dgate_ref, dup_ref, *refs):
    gate_refs, up_refs = refs[:count], refs[count : 2 * count]
    out_ref, gate_whole, up_whole = refs[2 * count :]
    settle(spots_ref, gate_refs, gate_whole)
    settle(spots_ref, up_refs, up_whole)

    @pl.when(pl.program_id(0) == 0)
    def _():
        out_ref[...] = jnp.zeros_like(out_ref)

    step = min(256, dgate_ref.shape[0])
    for begin in range(0, dgate_ref.shape[0], step):
        rows = slice(begin, begin + step)
        out_ref[rows] += nt_dot(dgate_ref[rows], gate_whole[...]) + nt_dot(
            dup_ref[rows], up_whole[...]
        )


def ffn_input(grad_gate, grad_up, gate, up, gathered):
    rows, hidden = grad_gate.shape
    blocks, spots = gathered
    count = len(blocks) + 2
    part = gate.shape[0] // 2
    depth = count * part
    tile = pl.BlockSpec((rows, FF_TILE), lambda i, spot: (0, i))
    return pl.pallas_call(
        functools.partial(ffn_input_kernel, count),
        out_shape=jax.ShapeDtypeStruct((rows, depth), jnp.float32),
        grid_spec=pltpu.PrefetchScalarGridSpec(
            num_scalar_prefetch=1,
            grid=(hidden // FF_TILE,),
            in_specs=[tile, tile] + block_specs(count, part, hidden // FF_TILE),
            out_specs=pl.BlockSpec((rows, depth), lambda i, spot: (0, 0)),
            scratch_shapes=[pltpu.VMEM((depth, FF_TILE), jnp.bfloat16)] * 2,
        ),
        cost_estimate=TINY,
        compiler_params=pltpu.CompilerParams(vmem_limit_bytes=60 << 20),
        name="ffn_input",
    )(spots, grad_gate, grad_up, gate, gate, *blocks, up, up, *blocks)


def gather_steps(links, mine, whole, late=False):
    shard_size, rep_size, shard_swap, rep_swap = links
    me = lax.axis_index("shard")
    core = lax.rem(lax.axis_index("rep"), 2)
    half, width = mine.shape
    quarter = half // 2
    pieces, others = {}, {}
    if shard_size == 4:
        pieces[1] = shard_swap(mine, 1)
        pieces[2] = shard_swap(mine, 2)
        pieces[1], pieces[2] = yield (pieces[1], pieces[2])
        corner_a = shard_swap(pieces[1][:quarter], 2)
        corner_b = shard_swap(pieces[2][quarter:], 1)
        if late:
            early, waiting = (), (1, 2, 3)
            corner_a, corner_b, pieces[1], pieces[2] = yield (
                corner_a, corner_b, pieces[1], pieces[2]
            )
        else:
            early, waiting = (rep_swap(pieces[1], 1), rep_swap(pieces[2], 1)), (3,)
            corner_a, corner_b, *early = yield (corner_a, corner_b, *early)
        pieces[3] = jnp.concatenate([corner_a, corner_b], axis=0)
        if late == "joined":
            joined = jnp.stack([pieces[1], pieces[2], pieces[3]])
            (got,) = yield (rep_swap(joined, 1),)
            others = {d: got[d - 1] for d in (1, 2, 3)}
        else:
            rest = yield tuple(rep_swap(pieces[d], 1) for d in waiting)
            others = dict(zip((1, 2, 3), (*early, *rest)))
    else:
        pieces[0] = mine
        bit = 1
        while bit < shard_size:
            order = sorted(pieces)
            got = shard_swap(jnp.stack([pieces[d] for d in order]), bit)
            (got,) = yield (got,)
            for at, d in enumerate(order):
                pieces[d ^ bit] = got[at]
            bit *= 2
        del pieces[0]
        others = {d: rep_swap(piece, 1) for d, piece in pieces.items()}
    blocks, spots = [whole] if whole is not None else [], [2 * me, 2 * me + 1]
    for d in pieces:
        blocks += [pieces[d], others[d]]
        spots += [2 * (me ^ d) + core, 2 * (me ^ d) + 1 - core]
    return blocks, jnp.stack(spots).astype(jnp.int32)


def core_half(weight):
    core = lax.rem(lax.axis_index("rep"), 2)
    half = weight.shape[0] // 2
    return lax.dynamic_slice_in_dim(weight, core * half, half, 0)


def pick_columns(links, value):
    core = lax.rem(lax.axis_index("rep"), 2)
    width = value.shape[1] // links[0] // 2

    def half(which):
        return jnp.concatenate(
            [
                lax.dynamic_slice_in_dim(value, (2 * d + which) * width, width, 1)
                for d in range(links[0])
            ],
            axis=1,
        )

    return half(core), half(1 - core)


def blocked(links, product):
    return product.reshape(links[0], -1, product.shape[1])


def scatter_steps(links, own, received):
    shard_size, rep_size, shard_swap, rep_swap = links
    me = lax.axis_index("shard")
    rep = lax.axis_index("rep")
    rows = own.shape[1] // 2

    def piece(d, at):
        begin, extent = (me ^ d, at * rows, 0), (1, rows, own.shape[2])
        return add_low(
            lax.dynamic_slice(own, begin, extent)[0],
            lax.dynamic_slice(received, begin, extent)[0],
        )

    if shard_size == 4:
        got_a = shard_swap(jnp.stack([piece(1, 0), piece(3, 0)]), 1)
        got_b = shard_swap(jnp.stack([piece(2, 1), piece(3, 1)]), 2)
        got_a, got_b = yield (got_a, got_b)
        pass_a = shard_swap(add_low(piece(2, 0), got_a[1]), 2)
        pass_b = shard_swap(add_low(piece(1, 1), got_b[1]), 1)
        pass_a, pass_b = yield (pass_a, pass_b)
        sum_a = add_low(piece(0, 0).astype(jnp.float32) + got_a[0].astype(jnp.float32), pass_a)
        sum_b = add_low(piece(0, 1).astype(jnp.float32) + got_b[0].astype(jnp.float32), pass_b)
        halves = [sum_a, sum_b]
    else:
        held = {d: jnp.stack([piece(d, 0), piece(d, 1)]) for d in range(shard_size)}
        bit = shard_size // 2
        while bit:
            sent = [d for d in sorted(held) if d & bit]
            got = shard_swap(jnp.stack([held[d] for d in sent]), bit)
            (got,) = yield (got,)
            held = {d ^ bit: add_low(held[d ^ bit], got[at]) for at, d in enumerate(sent)}
            bit //= 2
        halves = [held[0][0], held[0][1]]
    upper = lax.rem(rep // 2, 2) == 1
    if rep_size >= 8:
        keep = jnp.where(upper, halves[1], halves[0])
        send = jnp.where(upper, halves[0], halves[1])
        got = rep_swap(send, 2)
        (got,) = yield (got,)
        keep = add_low(keep, got)
        bit = 4
        while bit < rep_size:
            got = rep_swap(keep, bit)
            (got,) = yield (got,)
            keep = add_low(keep, got)
            bit *= 2
        back = rep_swap(keep, 2)
        (back,) = yield (back,)
        halves = [jnp.where(upper, back, keep), jnp.where(upper, keep, back)]
        half = jnp.concatenate(halves, axis=0)
    else:
        half = jnp.concatenate(halves, axis=0)
        bit = 2
        while bit < rep_size:
            half = add_low(half, rep_swap(half, bit))
            bit *= 2
    other = rep_swap(half, 1)
    (other,) = yield (other,)
    return half, other


def join_rows(pair):
    core = lax.rem(lax.axis_index("rep"), 2)
    half, other = pair
    return jnp.where(
        core == 0,
        jnp.concatenate([half, other], axis=0),
        jnp.concatenate([other, half], axis=0),
    ).astype(jnp.float32)


def join_columns(pair):
    core = lax.rem(lax.axis_index("rep"), 2)
    half, other = pair
    return jnp.where(
        core == 0,
        jnp.concatenate([half, other], axis=1),
        jnp.concatenate([other, half], axis=1),
    ).astype(jnp.float32)


BLOCK = 256
LOOK = 3


def nt_dot(left_mat, right_mat):
    return lax.dot_general(
        left_mat, right_mat, (((1,), (1,)), ((), ())), preferred_element_type=jnp.float32
    )


def attend_kernel(live_ref, q_ref, k_ref, v_ref, seg_col_ref, seg_row_ref, o_ref, acc_ref):
    at = pl.program_id(1)
    acc_ref[...] = jnp.zeros_like(acc_ref)
    lane = lax.broadcasted_iota(jnp.int32, (BLOCK, 2 * HD), 1)
    low_lane = lane < HD
    for back in range(LOOK):
        key_block = jnp.maximum(at - back, 0)

        @pl.when((at >= back) & (live_ref[at, key_block] > 0))
        def _():
            begin = pl.multiple_of(key_block * BLOCK, BLOCK)
            same = seg_col_ref[...] == seg_row_ref[:, pl.ds(begin, BLOCK)]
            if back == 0:
                row = lax.broadcasted_iota(jnp.int32, (BLOCK, BLOCK), 0)
                col = lax.broadcasted_iota(jnp.int32, (BLOCK, BLOCK), 1)
                same = same & (col <= row)
            mask = same.astype(jnp.float32)
            keys = k_ref[pl.ds(begin, BLOCK), :]
            values = v_ref[pl.ds(begin, BLOCK), :]
            swapped = pltpu.roll(values.astype(jnp.float32), HD, 1).astype(jnp.bfloat16)
            one = jnp.ones_like(values)
            for head in range(4):
                group, odd = head // 2, head % 2
                scores = nt_dot(
                    q_ref[:, head * HD : (head + 1) * HD], keys[:, group * HD : (group + 1) * HD]
                )
                weights = (jnp.exp(scores) * mask).astype(jnp.bfloat16)
                held = values if group == odd else swapped
                padded = jnp.where(low_lane, held, one) if odd == 0 else jnp.where(low_lane, one, held)
                acc_ref[head] += jnp.dot(weights, padded, preferred_element_type=jnp.float32)

    for group in range(2):
        even, odd = acc_ref[2 * group], acc_ref[2 * group + 1]
        top = jnp.where(low_lane, even, odd)
        total = pltpu.roll(jnp.where(low_lane, odd, even), HD, 1)
        o_ref[:, group * 2 * HD : (group + 1) * 2 * HD] = (top / total).astype(o_ref.dtype)


def head_norm_back(grad, linear, turn, gain):
    half = HD // 2
    cosine, sine = turn[:half], turn[half:]
    gain_1, gain_2 = gain[:half], gain[half:]
    parts, sums = [], None
    for begin in range(0, grad.shape[0], HD):
        grad_1, grad_2 = grad[begin : begin + half], grad[begin + half : begin + HD]
        lin_1, lin_2 = linear[begin : begin + half], linear[begin + half : begin + HD]
        back_1 = grad_1 * cosine + grad_2 * sine
        back_2 = grad_2 * cosine - grad_1 * sine
        square = jnp.sum(lin_1 * lin_1 + lin_2 * lin_2, axis=0, keepdims=True)
        scale = lax.rsqrt(square * (1.0 / HD) + norm_eps)
        unit_1, unit_2 = lin_1 * scale, lin_2 * scale
        both = jnp.concatenate([back_1 * unit_1, back_2 * unit_2], axis=0)
        sums = both if sums is None else sums + both
        back_1, back_2 = back_1 * gain_1, back_2 * gain_2
        inner = jnp.sum(back_1 * unit_1 + back_2 * unit_2, axis=0, keepdims=True) * (1.0 / HD)
        parts += [scale * (back_1 - unit_1 * inner), scale * (back_2 - unit_2 * inner)]
    return jnp.concatenate(parts, axis=0), sums


def attend_back_kernel(
    live_ref, q_ref, do_ref, k_ref, v_ref, seg_col_ref, seg_row_ref,
    q_lin_ref, k_lin_ref, q_turn_ref, k_turn_ref, gain_ref,
    dq_out_ref, dk_out_ref, dv_out_ref, q_gain_ref, k_gain_ref,
    exp_ref, dp_ref, total_ref, inner_ref, dqt_ref, dk_ref, dv_ref,
):
    at = pl.program_id(1)

    @pl.when(at == 0)
    def _():
        dk_ref[...] = jnp.zeros_like(dk_ref)
        dv_ref[...] = jnp.zeros_like(dv_ref)
        q_gain_ref[...] = jnp.zeros_like(q_gain_ref)

    total_ref[...] = jnp.zeros_like(total_ref)
    inner_ref[...] = jnp.zeros_like(inner_ref)
    dqt_ref[...] = jnp.zeros_like(dqt_ref)

    def each_block(run):
        for back in range(LOOK):
            key_block = jnp.maximum(at - back, 0)

            @pl.when((at >= back) & (live_ref[at, key_block] > 0))
            def _():
                run(back, pl.multiple_of(key_block * BLOCK, BLOCK))

    def first(back, begin):
        same = seg_col_ref[pl.ds(begin, BLOCK), :] == seg_row_ref[...]
        if back == 0:
            row = lax.broadcasted_iota(jnp.int32, (BLOCK, BLOCK), 0)
            col = lax.broadcasted_iota(jnp.int32, (BLOCK, BLOCK), 1)
            same = same & (row <= col)
        mask = same.astype(jnp.float32)
        keys = k_ref[pl.ds(begin, BLOCK), :]
        values = v_ref[pl.ds(begin, BLOCK), :]
        for head in range(4):
            group = head // 2
            cols = slice(head * HD, (head + 1) * HD)
            kept = slice(group * HD, (group + 1) * HD)
            weights = jnp.exp(nt_dot(keys[:, kept], q_ref[:, cols])) * mask
            grads = nt_dot(values[:, kept], do_ref[:, cols])
            exp_ref[head, back] = weights
            dp_ref[head, back] = grads
            total_ref[head : head + 1] += jnp.sum(weights, axis=0, keepdims=True)
            inner_ref[head : head + 1] += jnp.sum(weights * grads, axis=0, keepdims=True)

    def second(back, begin):
        keys = k_ref[pl.ds(begin, BLOCK), :]
        dk_parts, dv_parts = [], []
        for group in range(2):
            dk_sum, dv_sum = None, None
            for head in (2 * group, 2 * group + 1):
                cols = slice(head * HD, (head + 1) * HD)
                scale = 1.0 / total_ref[head : head + 1]
                probs = exp_ref[head, back] * scale
                inner = inner_ref[head : head + 1] * scale
                low_scores = (probs * (dp_ref[head, back] - inner)).astype(jnp.bfloat16)
                dv_part = jnp.dot(
                    probs.astype(jnp.bfloat16), do_ref[:, cols], preferred_element_type=jnp.float32
                )
                dk_part = jnp.dot(low_scores, q_ref[:, cols], preferred_element_type=jnp.float32)
                dqt_ref[cols] += lax.dot_general(
                    keys[:, group * HD : (group + 1) * HD],
                    low_scores,
                    (((0,), (0,)), ((), ())),
                    preferred_element_type=jnp.float32,
                )
                dk_sum = dk_part if dk_sum is None else dk_sum + dk_part
                dv_sum = dv_part if dv_sum is None else dv_sum + dv_part
            dk_parts.append(dk_sum)
            dv_parts.append(dv_sum)
        dk_ref[pl.ds(begin, BLOCK), :] += jnp.concatenate(dk_parts, axis=1)
        dv_ref[pl.ds(begin, BLOCK), :] += jnp.concatenate(dv_parts, axis=1)

    each_block(first)
    each_block(second)
    grad, gain_sum = head_norm_back(
        dqt_ref[...] * (1.0 / math.sqrt(HD)), q_lin_ref[...].T, q_turn_ref[...], gain_ref[:HD]
    )
    q_gain_ref[0] += gain_sum
    dq_out_ref[...] = grad.T.astype(jnp.bfloat16)

    @pl.when(at == pl.num_programs(1) - 1)
    def _():
        dv_out_ref[...] = dv_ref[...].astype(jnp.bfloat16)
        key_sum = None
        for begin in range(0, dk_ref.shape[0], BLOCK):
            rows = slice(begin, begin + BLOCK)
            grad, gain_sum = head_norm_back(
                dk_ref[rows].T, k_lin_ref[rows].T, k_turn_ref[:, rows], gain_ref[HD:]
            )
            dk_out_ref[rows] = grad.T.astype(jnp.bfloat16)
            key_sum = gain_sum if key_sum is None else key_sum + gain_sum
        k_gain_ref[0] = key_sum


def live_blocks(segment):
    count = segment.shape[0] // BLOCK
    blocks = segment.reshape(count, BLOCK)
    index = jnp.arange(count)
    return (
        (blocks[:, :1] == blocks[:, -1][None, :]) | (index[:, None] == index[None, :])
    ).astype(jnp.int32)


def attend(query, key, value, segment):
    rows = query.shape[0]
    panels, count = HK // 2, rows // BLOCK
    return pl.pallas_call(
        attend_kernel,
        out_shape=jax.ShapeDtypeStruct((rows, HQ * HD), jnp.bfloat16),
        grid_spec=pltpu.PrefetchScalarGridSpec(
            num_scalar_prefetch=1,
            grid=(panels, count),
            in_specs=[
                pl.BlockSpec((BLOCK, 4 * HD), lambda p, i, live: (i, p)),
                pl.BlockSpec((rows, 2 * HD), lambda p, i, live: (0, p)),
                pl.BlockSpec((rows, 2 * HD), lambda p, i, live: (0, p)),
                pl.BlockSpec((BLOCK, 1), lambda p, i, live: (i, 0)),
                pl.BlockSpec((1, rows), lambda p, i, live: (0, 0)),
            ],
            out_specs=pl.BlockSpec((BLOCK, 4 * HD), lambda p, i, live: (i, p)),
            scratch_shapes=[pltpu.VMEM((4, BLOCK, 2 * HD), jnp.float32)],
        ),
        cost_estimate=TINY,
        name="attend",
    )(live_blocks(segment), query, key, value, segment[:, None], segment[None, :])


def attend_back(query, grad_out, key, value, segment, query_lin, key_lin, turn, gain, start, panels):
    rows = query.shape[0]
    count = rows // BLOCK
    return pl.pallas_call(
        attend_back_kernel,
        out_shape=(
            jax.ShapeDtypeStruct((rows, panels * 4 * HD), jnp.bfloat16),
            jax.ShapeDtypeStruct((rows, panels * 2 * HD), jnp.bfloat16),
            jax.ShapeDtypeStruct((rows, panels * 2 * HD), jnp.bfloat16),
            jax.ShapeDtypeStruct((panels, HD, BLOCK), jnp.float32),
            jax.ShapeDtypeStruct((panels, HD, BLOCK), jnp.float32),
        ),
        grid_spec=pltpu.PrefetchScalarGridSpec(
            num_scalar_prefetch=1,
            grid=(panels, count),
            in_specs=[
                pl.BlockSpec((BLOCK, 4 * HD), lambda p, i, live: (i, start + p)),
                pl.BlockSpec((BLOCK, 4 * HD), lambda p, i, live: (i, start + p)),
                pl.BlockSpec((rows, 2 * HD), lambda p, i, live: (0, start + p)),
                pl.BlockSpec((rows, 2 * HD), lambda p, i, live: (0, start + p)),
                pl.BlockSpec((rows, 1), lambda p, i, live: (0, 0)),
                pl.BlockSpec((1, BLOCK), lambda p, i, live: (0, i)),
                pl.BlockSpec((BLOCK, 4 * HD), lambda p, i, live: (i, start + p)),
                pl.BlockSpec((rows, 2 * HD), lambda p, i, live: (0, start + p)),
                pl.BlockSpec((HD, BLOCK), lambda p, i, live: (0, i)),
                pl.BlockSpec((HD, rows), lambda p, i, live: (0, 0)),
                pl.BlockSpec((2 * HD, 1), lambda p, i, live: (0, 0)),
            ],
            out_specs=[
                pl.BlockSpec((BLOCK, 4 * HD), lambda p, i, live: (i, p)),
                pl.BlockSpec((rows, 2 * HD), lambda p, i, live: (0, p)),
                pl.BlockSpec((rows, 2 * HD), lambda p, i, live: (0, p)),
                pl.BlockSpec((1, HD, BLOCK), lambda p, i, live: (p, 0, 0)),
                pl.BlockSpec((1, HD, BLOCK), lambda p, i, live: (p, 0, 0)),
            ],
            scratch_shapes=[
                pltpu.VMEM((4, LOOK, BLOCK, BLOCK), jnp.float32),
                pltpu.VMEM((4, LOOK, BLOCK, BLOCK), jnp.float32),
                pltpu.VMEM((8, BLOCK), jnp.float32),
                pltpu.VMEM((8, BLOCK), jnp.float32),
                pltpu.VMEM((4 * HD, BLOCK), jnp.float32),
                pltpu.VMEM((rows, 2 * HD), jnp.float32),
                pltpu.VMEM((rows, 2 * HD), jnp.float32),
            ],
        ),
        cost_estimate=TINY,
        name="attend_back",
    )(live_blocks(segment), query, grad_out, key, value, segment[:, None], segment[None, :],
      query_lin, key_lin, turn, turn, gain)


def body(
    links,
    tokens,
    cotangent,
    segment,
    attn_gain,
    w_query,
    w_key,
    w_value,
    qk_gain,
    w_out,
    ffn_gain,
    w_gate,
    w_up,
    w_down,
):
    row_count = tokens.shape[0]
    rep_swap = links[3]
    core = lax.rem(lax.axis_index("rep"), 2)
    score_scale = 1.0 / math.sqrt(HD)
    spare = jnp.zeros((attn_gain.shape[0] - qk_gain.shape[0],), jnp.bfloat16)
    packed = jnp.stack([attn_gain, ffn_gain, jnp.concatenate([qk_gain, spare])], axis=1)
    packed = jnp.pad(packed, ((0, 0), (0, 125)))
    attn_weights = (w_query, w_key, w_value, packed)
    front_flow = Flow(
        gather_steps(
            links,
            jnp.concatenate([core_half(weight) for weight in attn_weights], axis=1),
            jnp.concatenate(attn_weights, axis=1),
            late="joined",
        )
    )
    w_out, w_gate, w_up, w_down = sync((w_out, w_gate, w_up, w_down), front_flow)
    out_flow = Flow(gather_steps(links, core_half(w_out), w_out, late="joined"))
    w_gate, w_up, w_down = sync((w_gate, w_up, w_down), front_flow)
    pair = jnp.concatenate([core_half(w_gate), core_half(w_up)], axis=1)
    pair_flow = Flow(gather_steps(links, pair, None, late=True))
    w_down = sync(w_down, front_flow)
    front = place_blocks(front_flow.finish())
    full_query = front[:, : HQ * HD]
    full_key = front[:, HQ * HD : (HQ + HK) * HD]
    full_value = front[:, (HQ + HK) * HD : (HQ + 2 * HK) * HD]
    gains = front[:, (HQ + 2 * HK) * HD :]
    full_attn_gain = gains[:, 0]
    full_ffn_gain = gains[:, 1]
    full_qk_gain = gains.reshape(links[0], -1, 128)[:, : qk_gain.shape[0], 2].reshape(-1)
    inputs = tokens.astype(jnp.float32)
    token_index = jnp.arange(row_count)
    same_seq = segment[:, None] == segment[None, :]
    allowed = same_seq & (token_index[None, :] <= token_index[:, None])
    positions = jnp.sum(
        (same_seq & (token_index[None, :] < token_index[:, None])).astype(jnp.float32), axis=1
    )
    live_rows = (segment >= 0).astype(jnp.float32)[:, None]
    cosine, sine_table = rope_tables(positions)
    scale_one = inv_rms(inputs)
    normed = (inputs * scale_one * full_attn_gain.astype(jnp.float32)).astype(jnp.bfloat16)
    query_lin = matmul_plain(normed, full_query).reshape(row_count, HQ, HD)
    key_lin = matmul_plain(normed, full_key).reshape(row_count, HK, HD)
    value_low = matmul_plain(normed, full_value).astype(jnp.bfloat16).reshape(row_count, HK, HD)
    qk_gains = full_qk_gain.astype(jnp.float32)
    query_scale = inv_rms(query_lin)
    key_scale = inv_rms(key_lin)
    query_rot = (
        rotate(query_lin * query_scale * qk_gains[:HD], cosine, sine_table)
        .astype(jnp.bfloat16)
    )
    key_rot = rotate(key_lin * key_scale * qk_gains[HD:], cosine, sine_table).astype(jnp.bfloat16)

    query_rot = (query_rot.astype(jnp.float32) * score_scale).astype(jnp.bfloat16)
    query_rot = query_rot.reshape(row_count, HQ * HD)
    key_rot = key_rot.reshape(row_count, HK * HD)
    value_low = value_low.reshape(row_count, HK * HD)
    query_rot, key_rot, value_low, w_down = sync(
        (query_rot, key_rot, value_low, w_down), out_flow
    )
    attn_low = attend(query_rot, key_rot, value_low, segment)
    attn_low, w_down = sync((attn_low, w_down), out_flow, pair_flow)
    down_flow = Flow(gather_steps(links, core_half(w_down), w_down))
    full_out = place_blocks(out_flow.finish())
    hidden = inputs + matmul_plain(attn_low, full_out)
    scale_two = inv_rms(hidden)
    normed_ffn = (hidden * scale_two * full_ffn_gain.astype(jnp.float32)).astype(jnp.bfloat16)
    normed_ffn, hidden = sync((normed_ffn, hidden), pair_flow)
    pair = pair_flow.finish()
    tiles = w_gate.shape[1] // FF_TILE
    first = ffn_forward(normed_ffn, w_gate, w_up, pair, 0, tiles // 2, None)
    normed_ffn, first = sync((normed_ffn, first), down_flow)
    mixed_act, act_low, slope = ffn_forward(
        normed_ffn, w_gate, w_up, pair, tiles // 2, tiles - tiles // 2, first
    )
    mixed_act, slope, act_low = sync((mixed_act, slope, act_low), down_flow)
    mixed_act, slope, act_low = sync((mixed_act, slope, act_low), down_flow)
    full_down = place_blocks(down_flow.finish())
    out_grad = live_rows * cotangent.astype(jnp.float32)
    out_low = out_grad.astype(jnp.bfloat16)
    grad_gate_low, grad_up_low = ffn_inner(out_low, full_down, act_low, slope)
    half = out_low.shape[1] // 2
    out_own = lax.dynamic_slice_in_dim(out_low, core * half, half, 1)
    out_other = lax.dynamic_slice_in_dim(out_low, (1 - core) * half, half, 1)
    normed_own, normed_other = pick_columns(links, normed_ffn)
    grad_up_low, grad_gate_low, out_own, out_other, mixed_act = pin(
        (grad_up_low, grad_gate_low, out_own, out_other, mixed_act)
    )

    def hand(product):
        return rep_swap(blocked(links, product).astype(jnp.bfloat16), 1)

    down_given = matmul_rows(mixed_act, out_other).astype(jnp.bfloat16)
    down_sent = hand(down_given)
    gate_given = matmul_rows(normed_other, pin(grad_gate_low, down_given)).astype(jnp.bfloat16)
    gate_sent = hand(gate_given)
    down_sent, mixed_act, grad_up_low, gate_given = pin(
        (down_sent, mixed_act, grad_up_low, gate_given)
    )
    down_given = blocked(links, matmul_rows(mixed_act, out_own).astype(jnp.bfloat16))
    down_back = Flow(scatter_steps(links, *pin((down_given, down_sent))))
    grad_up_low, grad_gate_low, normed_own, normed_other = pin(
        (grad_up_low, grad_gate_low, normed_own, normed_other), down_given
    )
    up_sent = hand(matmul_rows(normed_other, grad_up_low))
    gate_given = blocked(links, matmul_rows(normed_own, grad_gate_low).astype(jnp.bfloat16))
    up_given = blocked(links, matmul_rows(normed_own, grad_up_low).astype(jnp.bfloat16))
    gate_given, gate_sent, up_given, up_sent, grad_gate_low, grad_up_low = sync(
        (gate_given, gate_sent, up_given, up_sent, grad_gate_low, grad_up_low), down_back
    )
    gate_back = Flow(scatter_steps(links, gate_given, gate_sent))
    grad_normed_ffn = ffn_input(grad_gate_low, grad_up_low, w_gate, w_up, pair)
    grad_normed_ffn, up_given, up_sent = sync((grad_normed_ffn, up_given, up_sent), down_back)
    grad_hidden = out_grad + norm_back(
        grad_normed_ffn, hidden, scale_two, full_ffn_gain.astype(jnp.float32)
    )
    hidden_low = grad_hidden.astype(jnp.bfloat16)
    grad_attn_low = matmul_cols(hidden_low, full_out).astype(jnp.bfloat16)
    attn_own, attn_other = pick_columns(links, attn_low)
    out_sent = hand(matmul_rows(attn_other, hidden_low))
    out_given = blocked(links, matmul_rows(attn_own, hidden_low).astype(jnp.bfloat16))
    panels = HK // 4
    grad_attn_low, out_given, out_sent, up_given, up_sent = sync(
        (grad_attn_low, out_given, out_sent, up_given, up_sent), gate_back, down_back
    )
    up_back = Flow(scatter_steps(links, up_given, up_sent))
    turn = jnp.concatenate([cosine[:, 0].T, sine_table[:, 0].T], axis=0)
    flat = (query_lin.reshape(row_count, -1), key_lin.reshape(row_count, -1), turn, qk_gains[:, None])
    lower = attend_back(query_rot, grad_attn_low, key_rot, value_low, segment, *flat, 0, panels)
    grad_attn_low, lower, out_given, out_sent = sync(
        (grad_attn_low, lower, out_given, out_sent), up_back, gate_back
    )
    out_back = Flow(scatter_steps(links, out_given, out_sent))
    upper = attend_back(query_rot, grad_attn_low, key_rot, value_low, segment, *flat, panels, panels)
    lower, upper = sync((lower, upper), up_back, gate_back, out_back, down_back)
    grad_qk_gain = jnp.concatenate(
        [jnp.sum(lower[at] + upper[at], axis=(0, 2)) for at in (3, 4)]
    )
    grad_front = jnp.concatenate([part for at in range(3) for part in (lower[at], upper[at])], axis=1)
    normed_own, normed_other = pick_columns(links, normed)
    front_other = blocked(links, matmul_rows(normed_other, grad_front))
    front_own = blocked(links, matmul_rows(normed_own, grad_front))
    front_other, front_own = (part.astype(jnp.bfloat16) for part in (front_other, front_own))
    grad_front = pin(grad_front, front_other, front_own)
    grad_query_low = grad_front[:, : HQ * HD]
    grad_key_low = grad_front[:, HQ * HD : (HQ + HK) * HD]
    grad_value_low = grad_front[:, (HQ + HK) * HD :]
    grad_normed = (
        matmul_cols(grad_query_low, full_query)
        + matmul_cols(grad_key_low, full_key)
        + matmul_cols(grad_value_low, full_value)
    )
    qk_part = jnp.pad(
        grad_qk_gain.reshape(links[0], -1),
        ((0, 0), (0, attn_gain.shape[0] - qk_gain.shape[0])),
    )
    small = jnp.pad(qk_part.reshape(-1, 1), ((0, 0), (0, 127)))
    small = small.astype(jnp.bfloat16).reshape(links[0], 2, -1, 128)
    own_front = jnp.concatenate([front_own, lax.dynamic_slice_in_dim(small, core, 1, 1)[:, 0]], axis=2)
    other_front = jnp.concatenate(
        [front_other, lax.dynamic_slice_in_dim(small, 1 - core, 1, 1)[:, 0]], axis=2
    )
    front_sent = rep_swap(other_front, 1)
    own_front, front_sent, mixed_act, grad_normed = sync(
        (own_front, front_sent, mixed_act, grad_normed), out_back
    )
    front_back = Flow(scatter_steps(links, own_front, front_sent))
    grad_inputs = grad_hidden + norm_back(
        grad_normed, inputs, scale_one, full_attn_gain.astype(jnp.float32)
    )
    result = live_rows * (hidden + matmul_plain(mixed_act, full_down))
    grad_inputs, result = sync((grad_inputs, result), up_back, gate_back, front_back, out_back)
    sync((), front_back, out_back, gate_back)
    sync((), front_back, up_back, out_back)
    sync((), front_back, up_back)
    front_share = join_rows(front_back.finish())
    share_query = front_share[:, : HQ * HD]
    share_key = front_share[:, HQ * HD : (HQ + HK) * HD]
    share_value = front_share[:, (HQ + HK) * HD : (HQ + 2 * HK) * HD]
    extras = front_share[:, (HQ + 2 * HK) * HD :]
    share_qk = extras[: qk_gain.shape[0], 0]
    share_out = join_rows(out_back.finish())
    share_gate = join_rows(gate_back.finish())
    share_up = join_rows(up_back.finish())
    share_down = join_columns(down_back.finish())
    def gain_share(gain, *pairs):
        inner = sum(
            jnp.sum(weight.astype(jnp.float32) * share, axis=1) for weight, share in pairs
        )
        return inner / gain.astype(jnp.float32)

    share_again = gain_share(
        attn_gain, (w_query, share_query), (w_key, share_key), (w_value, share_value)
    )
    share_fgain = gain_share(ffn_gain, (w_gate, share_gate), (w_up, share_up))
    return (
        result.astype(jnp.bfloat16),
        grad_inputs.astype(jnp.bfloat16),
        share_again,
        share_query,
        share_key,
        share_value,
        share_qk,
        share_out,
        share_fgain,
        share_gate,
        share_up,
        share_down,
    )


def solution(mesh):
    return jax.shard_map(
        functools.partial(body, make_links(mesh)),
        mesh=mesh,
        in_specs=(
            P(("shard", "rep"), None),
            P(("shard", "rep"), None),
            P(("shard", "rep")),
            P("shard"),
            P("shard", None),
            P("shard", None),
            P("shard", None),
            P("shard"),
            P("shard", None),
            P("shard"),
            P("shard", None),
            P("shard", None),
            P("shard", None),
        ),
        out_specs=(
            P(("shard", "rep"), None),
            P(("shard", "rep"), None),
            P("shard"),
            P("shard", None),
            P("shard", None),
            P("shard", None),
            P("shard"),
            P("shard", None),
            P("shard"),
            P("shard", None),
            P("shard", None),
            P("shard", None),
        ),
        check_vma=False,
    )
```

```python
import functools
import math

import jax
import jax.numpy as jnp
from jax import lax
from jax.experimental import pallas as pl
from jax.experimental.pallas import tpu as pltpu
from jax.sharding import PartitionSpec as P

HQ = 16
HK = 8
HD = 64


norm_eps = 1e-05
TINY = pl.CostEstimate(flops=1, bytes_accessed=1, transcendentals=0)
rope_base = 1000000.0


def inv_rms(values):
    return lax.rsqrt(jnp.mean(values * values, axis=-1, keepdims=True) + norm_eps)


def rope_tables(positions):
    half_dim = HD // 2
    freq_index = jnp.arange(half_dim).astype(jnp.float32)
    freq_vals = jnp.power(rope_base, -(2.0 * freq_index) / HD)
    angles = positions[:, None] * freq_vals[None, :]
    return (jnp.cos(angles)[:, None, :], jnp.sin(angles)[:, None, :])


def rotate(values, cosine, sine_table):
    half_dim = HD // 2
    first_half = values[..., :half_dim]
    second_half = values[..., half_dim:]
    return jnp.concatenate(
        [
            first_half * cosine - second_half * sine_table,
            second_half * cosine + first_half * sine_table,
        ],
        axis=-1,
    )


def norm_back(grad_out, inputs, scale_inv, gain_vec):
    weighted = grad_out * gain_vec
    row_inner = jnp.mean(weighted * inputs, axis=-1, keepdims=True)
    return scale_inv * weighted - inputs * (scale_inv * scale_inv * scale_inv) * row_inner


def matmul_plain(left_mat, right_mat):
    return jnp.dot(left_mat, right_mat, preferred_element_type=jnp.float32)


def matmul_rows(left_mat, right_mat):
    return lax.dot_general(
        left_mat, right_mat, (((0,), (0,)), ((), ())), preferred_element_type=jnp.float32
    )


def matmul_cols(left_mat, right_mat):
    return lax.dot_general(
        left_mat, right_mat, (((1,), (1,)), ((), ())), preferred_element_type=jnp.float32
    )


def make_links(mesh):
    shard_size, rep_size = mesh.shape["shard"], mesh.shape["rep"]
    axes = ("shard", "rep")

    def shard_swap(value, bit):
        pairs = [
            (s * rep_size + r, (s ^ bit) * rep_size + r)
            for s in range(shard_size)
            for r in range(rep_size)
        ]
        return lax.ppermute(value, axes, pairs)

    def rep_swap(value, bit):
        pairs = [
            (s * rep_size + r, s * rep_size + (r ^ bit))
            for s in range(shard_size)
            for r in range(rep_size)
        ]
        return lax.ppermute(value, axes, pairs)

    return shard_size, rep_size, shard_swap, rep_swap


def add_low(left, right):
    return (left.astype(jnp.float32) + right.astype(jnp.float32)).astype(jnp.bfloat16)


def pin(values, *waits):
    return lax.optimization_barrier((values, waits))[0]


class Flow:
    def __init__(self, steps):
        self.steps = steps
        self.result = None
        self.pending = next(steps)

    def resume(self, arrived):
        try:
            self.pending = self.steps.send(arrived)
        except StopIteration as stop:
            self.pending = ()
            self.steps = None
            self.result = stop.value

    def finish(self):
        while self.steps is not None:
            self.resume(self.pending)
        return self.result


def sync(values, *flows):
    flows = [flow for flow in flows if flow.steps is not None]
    values, arrived = lax.optimization_barrier((values, [flow.pending for flow in flows]))
    for flow, got in zip(flows, arrived):
        flow.resume(got)
    return values


def place_kernel(spots_ref, *refs):
    del spots_ref
    out_ref = refs[-1]
    for at in range(len(refs) - 1):

        @pl.when(pl.program_id(0) == at)
        def _():
            out_ref[...] = refs[at][...]


def place_blocks(gathered):
    blocks, spots = gathered
    rows, width = blocks[1].shape
    count = len(blocks) + 1
    return pl.pallas_call(
        place_kernel,
        out_shape=jax.ShapeDtypeStruct((count * rows, width), blocks[0].dtype),
        grid_spec=pltpu.PrefetchScalarGridSpec(
            num_scalar_prefetch=1,
            grid=(count,),
            in_specs=[
                pl.BlockSpec((rows, width), lambda i, spot, at=at: (at, 0))
                for at in (0, 1) + (0,) * (count - 2)
            ],
            out_specs=pl.BlockSpec((rows, width), lambda i, spot: (spot[i], 0)),
        ),
        cost_estimate=TINY,
        compiler_params=pltpu.CompilerParams(vmem_limit_bytes=60 << 20),
        name="place_blocks",
    )(spots, blocks[0], *blocks)


FF_TILE = 512


def block_specs(count, rows, tiles, start=0):
    own = [
        pl.BlockSpec((rows, FF_TILE), lambda i, spot, at=at: (at, i + start)) for at in (0, 1)
    ]
    gate = [pl.BlockSpec((rows, FF_TILE), lambda i, spot: (0, i + start))] * (count - 2)
    up = [pl.BlockSpec((rows, FF_TILE), lambda i, spot: (0, i + start + tiles))] * (count - 2)
    return own + gate + own + up


def settle(spots_ref, refs, whole_ref):
    rows = refs[0].shape[0]
    for at, ref in enumerate(refs):
        begin = pl.multiple_of(spots_ref[at] * rows, rows)
        whole_ref[pl.ds(begin, rows), :] = ref[...]


def ffn_forward_kernel(count, spare, spots_ref, a_ref, *refs):
    refs = refs[: 2 * count] + refs[2 * count + spare :]
    gate_refs, up_refs = refs[:count], refs[count : 2 * count]
    z_ref, act_ref, slope_ref, gate_whole, up_whole = refs[2 * count :]
    settle(spots_ref, gate_refs, gate_whole)
    settle(spots_ref, up_refs, up_whole)
    step = min(256, a_ref.shape[0])
    for begin in range(0, a_ref.shape[0], step):
        rows = slice(begin, begin + step)
        gate = jnp.dot(a_ref[rows], gate_whole[...], preferred_element_type=jnp.float32)
        up = jnp.dot(a_ref[rows], up_whole[...], preferred_element_type=jnp.float32)
        sig = jax.nn.sigmoid(gate)
        act = gate * sig
        z_ref[rows] = (act * up).astype(jnp.bfloat16)
        act_ref[rows] = act.astype(jnp.bfloat16)
        slope_ref[rows] = (up * (sig + act * (1.0 - sig))).astype(jnp.bfloat16)


def ffn_forward(normed, gate, up, gathered, start, steps, into):
    rows, depth = normed.shape
    blocks, spots = gathered
    count = len(blocks) + 2
    hidden = gate.shape[1]
    part = gate.shape[0] // 2
    out = jax.ShapeDtypeStruct((rows, hidden), jnp.bfloat16)
    into = [] if into is None else list(into)
    first = 2 + 2 * count
    return pl.pallas_call(
        functools.partial(ffn_forward_kernel, count, len(into)),
        out_shape=(out, out, out),
        grid_spec=pltpu.PrefetchScalarGridSpec(
            num_scalar_prefetch=1,
            grid=(steps,),
            in_specs=[pl.BlockSpec((rows, depth), lambda i, spot: (0, 0))]
            + block_specs(count, part, hidden // FF_TILE, start)
            + [pl.BlockSpec(memory_space=pl.ANY)] * len(into),
            out_specs=[pl.BlockSpec((rows, FF_TILE), lambda i, spot: (0, i + start))] * 3,
            scratch_shapes=[pltpu.VMEM((depth, FF_TILE), jnp.bfloat16)] * 2,
        ),
        input_output_aliases={first + at: at for at in range(len(into))},
        cost_estimate=TINY,
        compiler_params=pltpu.CompilerParams(vmem_limit_bytes=60 << 20),
        name="ffn_forward",
    )(spots, normed, gate, gate, *blocks, up, up, *blocks, *into)


def ffn_inner_kernel(g_ref, down_ref, act_ref, slope_ref, dgate_ref, dup_ref):
    step = min(256, g_ref.shape[0])
    for begin in range(0, g_ref.shape[0], step):
        rows = slice(begin, begin + step)
        mixed = nt_dot(g_ref[rows], down_ref[...])
        dgate_ref[rows] = (mixed * slope_ref[rows].astype(jnp.float32)).astype(jnp.bfloat16)
        dup_ref[rows] = (mixed * act_ref[rows].astype(jnp.float32)).astype(jnp.bfloat16)


def ffn_inner(grad_low, down, act, slope):
    rows, depth = grad_low.shape
    hidden = down.shape[0]
    out = jax.ShapeDtypeStruct((rows, hidden), jnp.bfloat16)
    tile = pl.BlockSpec((rows, FF_TILE), lambda i: (0, i))
    return pl.pallas_call(
        ffn_inner_kernel,
        out_shape=(out, out),
        grid=(hidden // FF_TILE,),
        in_specs=[
            pl.BlockSpec((rows, depth), lambda i: (0, 0)),
            pl.BlockSpec((FF_TILE, depth), lambda i: (i, 0)),
            tile,
            tile,
        ],
        out_specs=[tile, tile],
        cost_estimate=TINY,
        compiler_params=pltpu.CompilerParams(vmem_limit_bytes=60 << 20),
        name="ffn_inner",
    )(grad_low, down, act, slope)


def ffn_input_kernel(count, spots_ref, dgate_ref, dup_ref, *refs):
    gate_refs, up_refs = refs[:count], refs[count : 2 * count]
    out_ref, gate_whole, up_whole = refs[2 * count :]
    settle(spots_ref, gate_refs, gate_whole)
    settle(spots_ref, up_refs, up_whole)

    @pl.when(pl.program_id(0) == 0)
    def _():
        out_ref[...] = jnp.zeros_like(out_ref)

    step = min(256, dgate_ref.shape[0])
    for begin in range(0, dgate_ref.shape[0], step):
        rows = slice(begin, begin + step)
        out_ref[rows] += nt_dot(dgate_ref[rows], gate_whole[...]) + nt_dot(
            dup_ref[rows], up_whole[...]
        )


def ffn_input(grad_gate, grad_up, gate, up, gathered):
    rows, hidden = grad_gate.shape
    blocks, spots = gathered
    count = len(blocks) + 2
    part = gate.shape[0] // 2
    depth = count * part
    tile = pl.BlockSpec((rows, FF_TILE), lambda i, spot: (0, i))
    return pl.pallas_call(
        functools.partial(ffn_input_kernel, count),
        out_shape=jax.ShapeDtypeStruct((rows, depth), jnp.float32),
        grid_spec=pltpu.PrefetchScalarGridSpec(
            num_scalar_prefetch=1,
            grid=(hidden // FF_TILE,),
            in_specs=[tile, tile] + block_specs(count, part, hidden // FF_TILE),
            out_specs=pl.BlockSpec((rows, depth), lambda i, spot: (0, 0)),
            scratch_shapes=[pltpu.VMEM((depth, FF_TILE), jnp.bfloat16)] * 2,
        ),
        cost_estimate=TINY,
        compiler_params=pltpu.CompilerParams(vmem_limit_bytes=60 << 20),
        name="ffn_input",
    )(spots, grad_gate, grad_up, gate, gate, *blocks, up, up, *blocks)


def gather_steps(links, mine, whole, late=False):
    shard_size, rep_size, shard_swap, rep_swap = links
    me = lax.axis_index("shard")
    core = lax.rem(lax.axis_index("rep"), 2)
    half, width = mine.shape
    quarter = half // 2
    pieces, others = {}, {}
    if shard_size == 4:
        pieces[1] = shard_swap(mine, 1)
        pieces[2] = shard_swap(mine, 2)
        pieces[1], pieces[2] = yield (pieces[1], pieces[2])
        corner_a = shard_swap(pieces[1][:quarter], 2)
        corner_b = shard_swap(pieces[2][quarter:], 1)
        if late:
            early, waiting = (), (1, 2, 3)
            corner_a, corner_b, pieces[1], pieces[2] = yield (
                corner_a, corner_b, pieces[1], pieces[2]
            )
        else:
            early, waiting = (rep_swap(pieces[1], 1), rep_swap(pieces[2], 1)), (3,)
            corner_a, corner_b, *early = yield (corner_a, corner_b, *early)
        pieces[3] = jnp.concatenate([corner_a, corner_b], axis=0)
        if late == "joined":
            joined = jnp.stack([pieces[1], pieces[2], pieces[3]])
            (got,) = yield (rep_swap(joined, 1),)
            others = {d: got[d - 1] for d in (1, 2, 3)}
        else:
            rest = yield tuple(rep_swap(pieces[d], 1) for d in waiting)
            others = dict(zip((1, 2, 3), (*early, *rest)))
    else:
        pieces[0] = mine
        bit = 1
        while bit < shard_size:
            order = sorted(pieces)
            got = shard_swap(jnp.stack([pieces[d] for d in order]), bit)
            (got,) = yield (got,)
            for at, d in enumerate(order):
                pieces[d ^ bit] = got[at]
            bit *= 2
        del pieces[0]
        others = {d: rep_swap(piece, 1) for d, piece in pieces.items()}
    blocks, spots = [whole] if whole is not None else [], [2 * me, 2 * me + 1]
    for d in pieces:
        blocks += [pieces[d], others[d]]
        spots += [2 * (me ^ d) + core, 2 * (me ^ d) + 1 - core]
    return blocks, jnp.stack(spots).astype(jnp.int32)


def core_half(weight):
    core = lax.rem(lax.axis_index("rep"), 2)
    half = weight.shape[0] // 2
    return lax.dynamic_slice_in_dim(weight, core * half, half, 0)


def pick_columns(links, value):
    core = lax.rem(lax.axis_index("rep"), 2)
    width = value.shape[1] // links[0] // 2

    def half(which):
        return jnp.concatenate(
            [
                lax.dynamic_slice_in_dim(value, (2 * d + which) * width, width, 1)
                for d in range(links[0])
            ],
            axis=1,
        )

    return half(core), half(1 - core)


def blocked(links, product):
    return product.reshape(links[0], -1, product.shape[1])


def scatter_steps(links, own, received):
    shard_size, rep_size, shard_swap, rep_swap = links
    me = lax.axis_index("shard")
    rep = lax.axis_index("rep")
    rows = own.shape[1] // 2

    def piece(d, at):
        begin, extent = (me ^ d, at * rows, 0), (1, rows, own.shape[2])
        return add_low(
            lax.dynamic_slice(own, begin, extent)[0],
            lax.dynamic_slice(received, begin, extent)[0],
        )

    if shard_size == 4:
        got_a = shard_swap(jnp.stack([piece(1, 0), piece(3, 0)]), 1)
        got_b = shard_swap(jnp.stack([piece(2, 1), piece(3, 1)]), 2)
        got_a, got_b = yield (got_a, got_b)
        pass_a = shard_swap(add_low(piece(2, 0), got_a[1]), 2)
        pass_b = shard_swap(add_low(piece(1, 1), got_b[1]), 1)
        pass_a, pass_b = yield (pass_a, pass_b)
        sum_a = add_low(piece(0, 0).astype(jnp.float32) + got_a[0].astype(jnp.float32), pass_a)
        sum_b = add_low(piece(0, 1).astype(jnp.float32) + got_b[0].astype(jnp.float32), pass_b)
        halves = [sum_a, sum_b]
    else:
        held = {d: jnp.stack([piece(d, 0), piece(d, 1)]) for d in range(shard_size)}
        bit = shard_size // 2
        while bit:
            sent = [d for d in sorted(held) if d & bit]
            got = shard_swap(jnp.stack([held[d] for d in sent]), bit)
            (got,) = yield (got,)
            held = {d ^ bit: add_low(held[d ^ bit], got[at]) for at, d in enumerate(sent)}
            bit //= 2
        halves = [held[0][0], held[0][1]]
    upper = lax.rem(rep // 2, 2) == 1
    if rep_size >= 8:
        keep = jnp.where(upper, halves[1], halves[0])
        send = jnp.where(upper, halves[0], halves[1])
        got = rep_swap(send, 2)
        (got,) = yield (got,)
        keep = add_low(keep, got)
        bit = 4
        while bit < rep_size:
            got = rep_swap(keep, bit)
            (got,) = yield (got,)
            keep = add_low(keep, got)
            bit *= 2
        back = rep_swap(keep, 2)
        (back,) = yield (back,)
        halves = [jnp.where(upper, back, keep), jnp.where(upper, keep, back)]
        half = jnp.concatenate(halves, axis=0)
    else:
        half = jnp.concatenate(halves, axis=0)
        bit = 2
        while bit < rep_size:
            half = add_low(half, rep_swap(half, bit))
            bit *= 2
    other = rep_swap(half, 1)
    (other,) = yield (other,)
    return half, other


def join_rows(pair):
    core = lax.rem(lax.axis_index("rep"), 2)
    half, other = pair
    return jnp.where(
        core == 0,
        jnp.concatenate([half, other], axis=0),
        jnp.concatenate([other, half], axis=0),
    ).astype(jnp.float32)


def join_columns(pair):
    core = lax.rem(lax.axis_index("rep"), 2)
    half, other = pair
    return jnp.where(
        core == 0,
        jnp.concatenate([half, other], axis=1),
        jnp.concatenate([other, half], axis=1),
    ).astype(jnp.float32)


BLOCK = 256
LOOK = 3


def nt_dot(left_mat, right_mat):
    return lax.dot_general(
        left_mat, right_mat, (((1,), (1,)), ((), ())), preferred_element_type=jnp.float32
    )


def attend_kernel(live_ref, q_ref, k_ref, v_ref, seg_col_ref, seg_row_ref, o_ref, acc_ref):
    at = pl.program_id(1)
    acc_ref[...] = jnp.zeros_like(acc_ref)
    lane = lax.broadcasted_iota(jnp.int32, (BLOCK, 2 * HD), 1)
    low_lane = lane < HD
    for back in range(LOOK):
        key_block = jnp.maximum(at - back, 0)

        @pl.when((at >= back) & (live_ref[at, key_block] > 0))
        def _():
            begin = pl.multiple_of(key_block * BLOCK, BLOCK)
            same = seg_col_ref[...] == seg_row_ref[:, pl.ds(begin, BLOCK)]
            if back == 0:
                row = lax.broadcasted_iota(jnp.int32, (BLOCK, BLOCK), 0)
                col = lax.broadcasted_iota(jnp.int32, (BLOCK, BLOCK), 1)
                same = same & (col <= row)
            mask = same.astype(jnp.float32)
            keys = k_ref[pl.ds(begin, BLOCK), :]
            values = v_ref[pl.ds(begin, BLOCK), :]
            swapped = pltpu.roll(values.astype(jnp.float32), HD, 1).astype(jnp.bfloat16)
            one = jnp.ones_like(values)
            for head in range(4):
                group, odd = head // 2, head % 2
                scores = nt_dot(
                    q_ref[:, head * HD : (head + 1) * HD], keys[:, group * HD : (group + 1) * HD]
                )
                weights = (jnp.exp(scores) * mask).astype(jnp.bfloat16)
                held = values if group == odd else swapped
                padded = jnp.where(low_lane, held, one) if odd == 0 else jnp.where(low_lane, one, held)
                acc_ref[head] += jnp.dot(weights, padded, preferred_element_type=jnp.float32)

    for group in range(2):
        even, odd = acc_ref[2 * group], acc_ref[2 * group + 1]
        top = jnp.where(low_lane, even, odd)
        total = pltpu.roll(jnp.where(low_lane, odd, even), HD, 1)
        o_ref[:, group * 2 * HD : (group + 1) * 2 * HD] = (top / total).astype(o_ref.dtype)


def head_norm_back(grad, linear, turn, gain):
    half = HD // 2
    cosine, sine = turn[:half], turn[half:]
    gain_1, gain_2 = gain[:half], gain[half:]
    parts, sums = [], None
    for begin in range(0, grad.shape[0], HD):
        grad_1, grad_2 = grad[begin : begin + half], grad[begin + half : begin + HD]
        lin_1, lin_2 = linear[begin : begin + half], linear[begin + half : begin + HD]
        back_1 = grad_1 * cosine + grad_2 * sine
        back_2 = grad_2 * cosine - grad_1 * sine
        square = jnp.sum(lin_1 * lin_1 + lin_2 * lin_2, axis=0, keepdims=True)
        scale = lax.rsqrt(square * (1.0 / HD) + norm_eps)
        unit_1, unit_2 = lin_1 * scale, lin_2 * scale
        both = jnp.concatenate([back_1 * unit_1, back_2 * unit_2], axis=0)
        sums = both if sums is None else sums + both
        back_1, back_2 = back_1 * gain_1, back_2 * gain_2
        inner = jnp.sum(back_1 * unit_1 + back_2 * unit_2, axis=0, keepdims=True) * (1.0 / HD)
        parts += [scale * (back_1 - unit_1 * inner), scale * (back_2 - unit_2 * inner)]
    return jnp.concatenate(parts, axis=0), sums


def attend_back_kernel(
    live_ref, q_ref, do_ref, k_ref, v_ref, seg_col_ref, seg_row_ref,
    q_lin_ref, k_lin_ref, q_turn_ref, k_turn_ref, gain_ref,
    dq_out_ref, dk_out_ref, dv_out_ref, q_gain_ref, k_gain_ref,
    exp_ref, dp_ref, total_ref, inner_ref, dqt_ref, dk_ref, dv_ref,
):
    at = pl.program_id(1)

    @pl.when(at == 0)
    def _():
        dk_ref[...] = jnp.zeros_like(dk_ref)
        dv_ref[...] = jnp.zeros_like(dv_ref)
        q_gain_ref[...] = jnp.zeros_like(q_gain_ref)

    total_ref[...] = jnp.zeros_like(total_ref)
    inner_ref[...] = jnp.zeros_like(inner_ref)
    dqt_ref[...] = jnp.zeros_like(dqt_ref)

    def each_block(run):
        for back in range(LOOK):
            key_block = jnp.maximum(at - back, 0)

            @pl.when((at >= back) & (live_ref[at, key_block] > 0))
            def _():
                run(back, pl.multiple_of(key_block * BLOCK, BLOCK))

    def first(back, begin):
        same = seg_col_ref[pl.ds(begin, BLOCK), :] == seg_row_ref[...]
        if back == 0:
            row = lax.broadcasted_iota(jnp.int32, (BLOCK, BLOCK), 0)
            col = lax.broadcasted_iota(jnp.int32, (BLOCK, BLOCK), 1)
            same = same & (row <= col)
        mask = same.astype(jnp.float32)
        keys = k_ref[pl.ds(begin, BLOCK), :]
        values = v_ref[pl.ds(begin, BLOCK), :]
        for head in range(4):
            group = head // 2
            cols = slice(head * HD, (head + 1) * HD)
            kept = slice(group * HD, (group + 1) * HD)
            weights = jnp.exp(nt_dot(keys[:, kept], q_ref[:, cols])) * mask
            grads = nt_dot(values[:, kept], do_ref[:, cols])
            exp_ref[head, back] = weights
            dp_ref[head, back] = grads
            total_ref[head : head + 1] += jnp.sum(weights, axis=0, keepdims=True)
            inner_ref[head : head + 1] += jnp.sum(weights * grads, axis=0, keepdims=True)

    def second(back, begin):
        keys = k_ref[pl.ds(begin, BLOCK), :]
        dk_parts, dv_parts = [], []
        for group in range(2):
            dk_sum, dv_sum = None, None
            for head in (2 * group, 2 * group + 1):
                cols = slice(head * HD, (head + 1) * HD)
                scale = 1.0 / total_ref[head : head + 1]
                probs = exp_ref[head, back] * scale
                inner = inner_ref[head : head + 1] * scale
                low_scores = (probs * (dp_ref[head, back] - inner)).astype(jnp.bfloat16)
                dv_part = jnp.dot(
                    probs.astype(jnp.bfloat16), do_ref[:, cols], preferred_element_type=jnp.float32
                )
                dk_part = jnp.dot(low_scores, q_ref[:, cols], preferred_element_type=jnp.float32)
                dqt_ref[cols] += lax.dot_general(
                    keys[:, group * HD : (group + 1) * HD],
                    low_scores,
                    (((0,), (0,)), ((), ())),
                    preferred_element_type=jnp.float32,
                )
                dk_sum = dk_part if dk_sum is None else dk_sum + dk_part
                dv_sum = dv_part if dv_sum is None else dv_sum + dv_part
            dk_parts.append(dk_sum)
            dv_parts.append(dv_sum)
        dk_ref[pl.ds(begin, BLOCK), :] += jnp.concatenate(dk_parts, axis=1)
        dv_ref[pl.ds(begin, BLOCK), :] += jnp.concatenate(dv_parts, axis=1)

    each_block(first)
    each_block(second)
    grad, gain_sum = head_norm_back(
        dqt_ref[...] * (1.0 / math.sqrt(HD)), q_lin_ref[...].T, q_turn_ref[...], gain_ref[:HD]
    )
    q_gain_ref[0] += gain_sum
    dq_out_ref[...] = grad.T.astype(jnp.bfloat16)

    @pl.when(at == pl.num_programs(1) - 1)
    def _():
        dv_out_ref[...] = dv_ref[...].astype(jnp.bfloat16)
        key_sum = None
        for begin in range(0, dk_ref.shape[0], BLOCK):
            rows = slice(begin, begin + BLOCK)
            grad, gain_sum = head_norm_back(
                dk_ref[rows].T, k_lin_ref[rows].T, k_turn_ref[:, rows], gain_ref[HD:]
            )
            dk_out_ref[rows] = grad.T.astype(jnp.bfloat16)
            key_sum = gain_sum if key_sum is None else key_sum + gain_sum
        k_gain_ref[0] = key_sum


def live_blocks(segment):
    count = segment.shape[0] // BLOCK
    blocks = segment.reshape(count, BLOCK)
    index = jnp.arange(count)
    return (
        (blocks[:, :1] == blocks[:, -1][None, :]) | (index[:, None] == index[None, :])
    ).astype(jnp.int32)


def attend(query, key, value, segment):
    rows = query.shape[0]
    panels, count = HK // 2, rows // BLOCK
    return pl.pallas_call(
        attend_kernel,
        out_shape=jax.ShapeDtypeStruct((rows, HQ * HD), jnp.bfloat16),
        grid_spec=pltpu.PrefetchScalarGridSpec(
            num_scalar_prefetch=1,
            grid=(panels, count),
            in_specs=[
                pl.BlockSpec((BLOCK, 4 * HD), lambda p, i, live: (i, p)),
                pl.BlockSpec((rows, 2 * HD), lambda p, i, live: (0, p)),
                pl.BlockSpec((rows, 2 * HD), lambda p, i, live: (0, p)),
                pl.BlockSpec((BLOCK, 1), lambda p, i, live: (i, 0)),
                pl.BlockSpec((1, rows), lambda p, i, live: (0, 0)),
            ],
            out_specs=pl.BlockSpec((BLOCK, 4 * HD), lambda p, i, live: (i, p)),
            scratch_shapes=[pltpu.VMEM((4, BLOCK, 2 * HD), jnp.float32)],
        ),
        cost_estimate=TINY,
        name="attend",
    )(live_blocks(segment), query, key, value, segment[:, None], segment[None, :])


def attend_back(query, grad_out, key, value, segment, query_lin, key_lin, turn, gain, start, panels):
    rows = query.shape[0]
    count = rows // BLOCK
    return pl.pallas_call(
        attend_back_kernel,
        out_shape=(
            jax.ShapeDtypeStruct((rows, panels * 4 * HD), jnp.bfloat16),
            jax.ShapeDtypeStruct((rows, panels * 2 * HD), jnp.bfloat16),
            jax.ShapeDtypeStruct((rows, panels * 2 * HD), jnp.bfloat16),
            jax.ShapeDtypeStruct((panels, HD, BLOCK), jnp.float32),
            jax.ShapeDtypeStruct((panels, HD, BLOCK), jnp.float32),
        ),
        grid_spec=pltpu.PrefetchScalarGridSpec(
            num_scalar_prefetch=1,
            grid=(panels, count),
            in_specs=[
                pl.BlockSpec((BLOCK, 4 * HD), lambda p, i, live: (i, start + p)),
                pl.BlockSpec((BLOCK, 4 * HD), lambda p, i, live: (i, start + p)),
                pl.BlockSpec((rows, 2 * HD), lambda p, i, live: (0, start + p)),
                pl.BlockSpec((rows, 2 * HD), lambda p, i, live: (0, start + p)),
                pl.BlockSpec((rows, 1), lambda p, i, live: (0, 0)),
                pl.BlockSpec((1, BLOCK), lambda p, i, live: (0, i)),
                pl.BlockSpec((BLOCK, 4 * HD), lambda p, i, live: (i, start + p)),
                pl.BlockSpec((rows, 2 * HD), lambda p, i, live: (0, start + p)),
                pl.BlockSpec((HD, BLOCK), lambda p, i, live: (0, i)),
                pl.BlockSpec((HD, rows), lambda p, i, live: (0, 0)),
                pl.BlockSpec((2 * HD, 1), lambda p, i, live: (0, 0)),
            ],
            out_specs=[
                pl.BlockSpec((BLOCK, 4 * HD), lambda p, i, live: (i, p)),
                pl.BlockSpec((rows, 2 * HD), lambda p, i, live: (0, p)),
                pl.BlockSpec((rows, 2 * HD), lambda p, i, live: (0, p)),
                pl.BlockSpec((1, HD, BLOCK), lambda p, i, live: (p, 0, 0)),
                pl.BlockSpec((1, HD, BLOCK), lambda p, i, live: (p, 0, 0)),
            ],
            scratch_shapes=[
                pltpu.VMEM((4, LOOK, BLOCK, BLOCK), jnp.float32),
                pltpu.VMEM((4, LOOK, BLOCK, BLOCK), jnp.float32),
                pltpu.VMEM((8, BLOCK), jnp.float32),
                pltpu.VMEM((8, BLOCK), jnp.float32),
                pltpu.VMEM((4 * HD, BLOCK), jnp.float32),
                pltpu.VMEM((rows, 2 * HD), jnp.float32),
                pltpu.VMEM((rows, 2 * HD), jnp.float32),
            ],
        ),
        cost_estimate=TINY,
        name="attend_back",
    )(live_blocks(segment), query, grad_out, key, value, segment[:, None], segment[None, :],
      query_lin, key_lin, turn, turn, gain)


def body(
    links,
    tokens,
    cotangent,
    segment,
    attn_gain,
    w_query,
    w_key,
    w_value,
    qk_gain,
    w_out,
    ffn_gain,
    w_gate,
    w_up,
    w_down,
):
    row_count = tokens.shape[0]
    rep_swap = links[3]
    core = lax.rem(lax.axis_index("rep"), 2)
    score_scale = 1.0 / math.sqrt(HD)
    spare = jnp.zeros((attn_gain.shape[0] - qk_gain.shape[0],), jnp.bfloat16)
    packed = jnp.stack([attn_gain, ffn_gain, jnp.concatenate([qk_gain, spare])], axis=1)
    packed = jnp.pad(packed, ((0, 0), (0, 125)))
    attn_weights = (w_query, w_key, w_value, packed)
    front_flow = Flow(
        gather_steps(
            links,
            jnp.concatenate([core_half(weight) for weight in attn_weights], axis=1),
            jnp.concatenate(attn_weights, axis=1),
            late="joined",
        )
    )
    w_out, w_gate, w_up, w_down = sync((w_out, w_gate, w_up, w_down), front_flow)
    out_flow = Flow(gather_steps(links, core_half(w_out), w_out, late="joined"))
    w_gate, w_up, w_down = sync((w_gate, w_up, w_down), front_flow)
    pair = jnp.concatenate([core_half(w_gate), core_half(w_up)], axis=1)
    pair_flow = Flow(gather_steps(links, pair, None, late=True))
    w_down = sync(w_down, front_flow)
    front = place_blocks(front_flow.finish())
    full_query = front[:, : HQ * HD]
    full_key = front[:, HQ * HD : (HQ + HK) * HD]
    full_value = front[:, (HQ + HK) * HD : (HQ + 2 * HK) * HD]
    gains = front[:, (HQ + 2 * HK) * HD :]
    full_attn_gain = gains[:, 0]
    full_ffn_gain = gains[:, 1]
    full_qk_gain = gains.reshape(links[0], -1, 128)[:, : qk_gain.shape[0], 2].reshape(-1)
    inputs = tokens.astype(jnp.float32)
    token_index = jnp.arange(row_count)
    same_seq = segment[:, None] == segment[None, :]
    allowed = same_seq & (token_index[None, :] <= token_index[:, None])
    positions = jnp.sum(
        (same_seq & (token_index[None, :] < token_index[:, None])).astype(jnp.float32), axis=1
    )
    live_rows = (segment >= 0).astype(jnp.float32)[:, None]
    cosine, sine_table = rope_tables(positions)
    scale_one = inv_rms(inputs)
    normed = (inputs * scale_one * full_attn_gain.astype(jnp.float32)).astype(jnp.bfloat16)
    query_lin = matmul_plain(normed, full_query).reshape(row_count, HQ, HD)
    key_lin = matmul_plain(normed, full_key).reshape(row_count, HK, HD)
    value_low = matmul_plain(normed, full_value).astype(jnp.bfloat16).reshape(row_count, HK, HD)
    qk_gains = full_qk_gain.astype(jnp.float32)
    query_scale = inv_rms(query_lin)
    key_scale = inv_rms(key_lin)
    query_rot = (
        rotate(query_lin * query_scale * qk_gains[:HD], cosine, sine_table)
        .astype(jnp.bfloat16)
    )
    key_rot = rotate(key_lin * key_scale * qk_gains[HD:], cosine, sine_table).astype(jnp.bfloat16)

    query_rot = (query_rot.astype(jnp.float32) * score_scale).astype(jnp.bfloat16)
    query_rot = query_rot.reshape(row_count, HQ * HD)
    key_rot = key_rot.reshape(row_count, HK * HD)
    value_low = value_low.reshape(row_count, HK * HD)
    query_rot, key_rot, value_low, w_down = sync(
        (query_rot, key_rot, value_low, w_down), out_flow
    )
    attn_low = attend(query_rot, key_rot, value_low, segment)
    attn_low, w_down = sync((attn_low, w_down), out_flow, pair_flow)
    down_flow = Flow(gather_steps(links, core_half(w_down), w_down))
    full_out = place_blocks(out_flow.finish())
    hidden = inputs + matmul_plain(attn_low, full_out)
    scale_two = inv_rms(hidden)
    normed_ffn = (hidden * scale_two * full_ffn_gain.astype(jnp.float32)).astype(jnp.bfloat16)
    normed_ffn, hidden = sync((normed_ffn, hidden), pair_flow)
    pair = pair_flow.finish()
    tiles = w_gate.shape[1] // FF_TILE
    first = ffn_forward(normed_ffn, w_gate, w_up, pair, 0, tiles // 2, None)
    normed_ffn, first = sync((normed_ffn, first), down_flow)
    mixed_act, act_low, slope = ffn_forward(
        normed_ffn, w_gate, w_up, pair, tiles // 2, tiles - tiles // 2, first
    )
    mixed_act, slope, act_low = sync((mixed_act, slope, act_low), down_flow)
    mixed_act, slope, act_low = sync((mixed_act, slope, act_low), down_flow)
    full_down = place_blocks(down_flow.finish())
    out_grad = live_rows * cotangent.astype(jnp.float32)
    out_low = out_grad.astype(jnp.bfloat16)
    grad_gate_low, grad_up_low = ffn_inner(out_low, full_down, act_low, slope)
    half = out_low.shape[1] // 2
    out_own = lax.dynamic_slice_in_dim(out_low, core * half, half, 1)
    out_other = lax.dynamic_slice_in_dim(out_low, (1 - core) * half, half, 1)
    normed_own, normed_other = pick_columns(links, normed_ffn)
    grad_up_low, grad_gate_low, out_own, out_other, mixed_act = pin(
        (grad_up_low, grad_gate_low, out_own, out_other, mixed_act)
    )

    def hand(product):
        return rep_swap(blocked(links, product).astype(jnp.bfloat16), 1)

    down_given = matmul_rows(mixed_act, out_other).astype(jnp.bfloat16)
    down_sent = hand(down_given)
    gate_given = matmul_rows(normed_other, pin(grad_gate_low, down_given)).astype(jnp.bfloat16)
    gate_sent = hand(gate_given)
    down_sent, mixed_act, grad_up_low, gate_given = pin(
        (down_sent, mixed_act, grad_up_low, gate_given)
    )
    down_given = blocked(links, matmul_rows(mixed_act, out_own).astype(jnp.bfloat16))
    down_back = Flow(scatter_steps(links, *pin((down_given, down_sent))))
    grad_up_low, grad_gate_low, normed_own, normed_other = pin(
        (grad_up_low, grad_gate_low, normed_own, normed_other), down_given
    )
    up_sent = hand(matmul_rows(normed_other, grad_up_low))
    gate_given = blocked(links, matmul_rows(normed_own, grad_gate_low).astype(jnp.bfloat16))
    up_given = blocked(links, matmul_rows(normed_own, grad_up_low).astype(jnp.bfloat16))
    gate_given, gate_sent, up_given, up_sent, grad_gate_low, grad_up_low = sync(
        (gate_given, gate_sent, up_given, up_sent, grad_gate_low, grad_up_low), down_back
    )
    gate_back = Flow(scatter_steps(links, gate_given, gate_sent))
    grad_normed_ffn = ffn_input(grad_gate_low, grad_up_low, w_gate, w_up, pair)
    grad_normed_ffn, up_given, up_sent = sync((grad_normed_ffn, up_given, up_sent), down_back)
    grad_hidden = out_grad + norm_back(
        grad_normed_ffn, hidden, scale_two, full_ffn_gain.astype(jnp.float32)
    )
    hidden_low = grad_hidden.astype(jnp.bfloat16)
    grad_attn_low = matmul_cols(hidden_low, full_out).astype(jnp.bfloat16)
    attn_own, attn_other = pick_columns(links, attn_low)
    out_sent = hand(matmul_rows(attn_other, hidden_low))
    out_given = blocked(links, matmul_rows(attn_own, hidden_low).astype(jnp.bfloat16))
    panels = HK // 4
    grad_attn_low, out_given, out_sent, up_given, up_sent = sync(
        (grad_attn_low, out_given, out_sent, up_given, up_sent), gate_back, down_back
    )
    up_back = Flow(scatter_steps(links, up_given, up_sent))
    turn = jnp.concatenate([cosine[:, 0].T, sine_table[:, 0].T], axis=0)
    flat = (query_lin.reshape(row_count, -1), key_lin.reshape(row_count, -1), turn, qk_gains[:, None])
    lower = attend_back(query_rot, grad_attn_low, key_rot, value_low, segment, *flat, 0, panels)
    grad_attn_low, lower = sync((grad_attn_low, lower), up_back, gate_back, down_back)
    upper = attend_back(query_rot, grad_attn_low, key_rot, value_low, segment, *flat, panels, panels)
    lower, upper, out_given, out_sent = sync(
        (lower, upper, out_given, out_sent), up_back, gate_back, down_back
    )
    out_back = Flow(scatter_steps(links, out_given, out_sent))
    grad_qk_gain = jnp.concatenate(
        [jnp.sum(lower[at] + upper[at], axis=(0, 2)) for at in (3, 4)]
    )
    grad_front = jnp.concatenate([part for at in range(3) for part in (lower[at], upper[at])], axis=1)
    normed_own, normed_other = pick_columns(links, normed)
    front_other = blocked(links, matmul_rows(normed_other, grad_front))
    front_own = blocked(links, matmul_rows(normed_own, grad_front))
    front_other, front_own = (part.astype(jnp.bfloat16) for part in (front_other, front_own))
    grad_front = pin(grad_front, front_other, front_own)
    grad_query_low = grad_front[:, : HQ * HD]
    grad_key_low = grad_front[:, HQ * HD : (HQ + HK) * HD]
    grad_value_low = grad_front[:, (HQ + HK) * HD :]
    grad_normed = (
        matmul_cols(grad_query_low, full_query)
        + matmul_cols(grad_key_low, full_key)
        + matmul_cols(grad_value_low, full_value)
    )
    qk_part = jnp.pad(
        grad_qk_gain.reshape(links[0], -1),
        ((0, 0), (0, attn_gain.shape[0] - qk_gain.shape[0])),
    )
    small = jnp.pad(qk_part.reshape(-1, 1), ((0, 0), (0, 127)))
    small = small.astype(jnp.bfloat16).reshape(links[0], 2, -1, 128)
    own_front = jnp.concatenate([front_own, lax.dynamic_slice_in_dim(small, core, 1, 1)[:, 0]], axis=2)
    other_front = jnp.concatenate(
        [front_other, lax.dynamic_slice_in_dim(small, 1 - core, 1, 1)[:, 0]], axis=2
    )
    front_sent = rep_swap(other_front, 1)
    own_front, front_sent, mixed_act, grad_normed = pin(
        (own_front, front_sent, mixed_act, grad_normed)
    )
    front_back = Flow(scatter_steps(links, own_front, front_sent))
    grad_inputs = grad_hidden + norm_back(
        grad_normed, inputs, scale_one, full_attn_gain.astype(jnp.float32)
    )
    result = live_rows * (hidden + matmul_plain(mixed_act, full_down))
    grad_inputs, result = sync((grad_inputs, result), up_back, gate_back, front_back, out_back)
    sync((), front_back, out_back, gate_back)
    sync((), front_back, up_back, out_back)
    sync((), front_back, up_back)
    front_share = join_rows(front_back.finish())
    share_query = front_share[:, : HQ * HD]
    share_key = front_share[:, HQ * HD : (HQ + HK) * HD]
    share_value = front_share[:, (HQ + HK) * HD : (HQ + 2 * HK) * HD]
    extras = front_share[:, (HQ + 2 * HK) * HD :]
    share_qk = extras[: qk_gain.shape[0], 0]
    share_out = join_rows(out_back.finish())
    share_gate = join_rows(gate_back.finish())
    share_up = join_rows(up_back.finish())
    share_down = join_columns(down_back.finish())
    def gain_share(gain, *pairs):
        inner = sum(
            jnp.sum(weight.astype(jnp.float32) * share, axis=1) for weight, share in pairs
        )
        return inner / gain.astype(jnp.float32)

    share_again = gain_share(
        attn_gain, (w_query, share_query), (w_key, share_key), (w_value, share_value)
    )
    share_fgain = gain_share(ffn_gain, (w_gate, share_gate), (w_up, share_up))
    return (
        result.astype(jnp.bfloat16),
        grad_inputs.astype(jnp.bfloat16),
        share_again,
        share_query,
        share_key,
        share_value,
        share_qk,
        share_out,
        share_fgain,
        share_gate,
        share_up,
        share_down,
    )


def solution(mesh):
    return jax.shard_map(
        functools.partial(body, make_links(mesh)),
        mesh=mesh,
        in_specs=(
            P(("shard", "rep"), None),
            P(("shard", "rep"), None),
            P(("shard", "rep")),
            P("shard"),
            P("shard", None),
            P("shard", None),
            P("shard", None),
            P("shard"),
            P("shard", None),
            P("shard"),
            P("shard", None),
            P("shard", None),
            P("shard", None),
        ),
        out_specs=(
            P(("shard", "rep"), None),
            P(("shard", "rep"), None),
            P("shard"),
            P("shard", None),
            P("shard", None),
            P("shard", None),
            P("shard"),
            P("shard", None),
            P("shard"),
            P("shard", None),
            P("shard", None),
            P("shard", None),
        ),
        check_vma=False,
    )
```
